128 devices in a mesh: pw: 64 (over z, y, x), mm: 2 (over core).
Axes of the slice: x: 4, y: 4, z: 4, core: 2. Of those that a mesh axis runs over, the one named last changes fastest.
Arguments:
- coefficients: float32 [2, 2, 28672, 384], P(None, 'mm', 'pw'), may hold values from -0.0009765625 to 0.0009765625
- col_map: int32 [28672], replicated, may hold values from 0 to 147456, as said below
- charge_cell: int32 [3, 512], replicated, may hold values from 0 to 383
- charge_frac: float32 [3, 512], replicated, may hold values from 0.05 to 0.95
- charge: float32 [512], replicated, may hold values from -1.5 to 1.5
- tile_list: int32 [128, 16], P(('pw', 'mm')), may hold values from 0 to 511, as said below
Outputs:
- field_orbital: float32 [2, 2, 64, 384, 384], P(None, 'mm', 'pw')
- forces: float32 [3, 512], replicated
The draws below stay inside these ranges and needn't reach their ends.
Inputs may be any that keep to these rules, and one draw needn't show every extreme that they name: Block d of col_map, its 448 entries from d * 448, belongs to pw index d. In each block the live entries, grid columns gb * 384 + gc below 147456, come first and the rest equal 147456; live entries are distinct over all blocks, 14336 in all; blocks d and d plus half the number of blocks together hold exactly 448 live entries; some block is full in every draw. `tile_list`: each row holds 16 distinct charge numbers.
All inputs are finite; a program needn't handle non-finite values.
Results may differ from the reference program's by a relative error of at most 0.0003.
Values sent between devices are 32-bit elements; how exact they have to be, the bound alone decides.
No kernel may reach another device: no remote copies, remote signals or barrier semaphores. Data moves between devices by JAX's collectives and lax.ppermute only.
A program may use at most 192 MiB of HBM per device.

```python
import math
import jax
import jax.numpy as jnp
from jax import lax

NG = 384
ORBS = 2
COL_DEV = 224
NP = 1
NQ = 512
NBR = 16
SLOTS = 448
NCOL = 14336
SLOT_ALL = 28672
PLANES = 64
NGH = 192
N_PW = 64
N_MM = 2


def draw_col_map(key, part):
    cell_count = NG * NG
    radius = NG // 4
    grid_index = jnp.arange(cell_count, dtype=jnp.int32)
    row_freq = grid_index // NG
    line_freq = grid_index % NG
    fold_row = jnp.minimum(row_freq, NG - row_freq)
    fold_line = jnp.minimum(line_freq, NG - line_freq)
    inside = (fold_row * fold_row + fold_line * fold_line <= radius * radius).astype(jnp.int32)
    ranking = jax.random.permutation(jax.random.fold_in(key, 11), cell_count).astype(jnp.int32)
    score = (1 - inside) * cell_count + ranking
    order = jnp.argsort(score, stable=True).astype(jnp.int32)
    chosen = order[:NCOL]
    pair_count = N_PW // 2
    delta = jax.random.randint(jax.random.fold_in(key, 12), (pair_count,), 0, COL_DEV + 1).astype(jnp.int32)
    delta = delta.at[0].set(COL_DEV)
    delta = delta[jax.random.permutation(jax.random.fold_in(key, 13), pair_count)]
    flip_sign = jax.random.randint(jax.random.fold_in(key, 14), (pair_count,), 0, 2).astype(jnp.int32) * 2 - 1
    lower_counts = COL_DEV + flip_sign * delta
    counts = jnp.concatenate([lower_counts, 2 * COL_DEV - lower_counts])
    offsets = jnp.cumsum(counts) - counts
    slot_index = jnp.arange(SLOTS, dtype=jnp.int32)
    picked = jnp.clip(offsets[:, None] + slot_index[None, :], 0, NCOL - 1)
    live = slot_index[None, :] < counts[:, None]
    values = jnp.where(live, chosen[picked], cell_count)
    return values.reshape(-1).astype(jnp.int32)


def draw_tile_list(key, part):
    tile_keys = jax.random.split(jax.random.fold_in(key, 21), N_PW * N_MM)

    def one_row(row_key):
        return jax.random.permutation(row_key, NQ)[:NBR]
    return jax.vmap(one_row)(tile_keys).astype(jnp.int32)


def with_ends(result, stream_key, smallest, largest):
    place = [jax.random.randint(jax.random.fold_in(stream_key, axis), (), 0, length) for axis, length in enumerate(result.shape)]
    main_axis = result.shape.index(max(result.shape))
    next_to = place[:main_axis] + [(place[main_axis] + 1) % result.shape[main_axis]] + place[main_axis + 1:]
    return result.at[tuple(place)].set(smallest).at[tuple(next_to)].set(largest)


def level_of(own_key, extent, cuts, least, top_value):
    level = 1.0
    for position, shards_of in cuts:
        draws = jax.random.uniform(jax.random.fold_in(jax.random.fold_in(own_key, 6), position), (shards_of,), jnp.float32, least / len(cuts), top_value / len(cuts))
        level = level * jnp.repeat(jnp.exp(draws), extent[position] // shards_of).reshape((-1,) + (1,) * (len(extent) - 1 - position))
    return level


def noise(key, dims, deviation, bound, shards=(), held_as=jnp.bfloat16):
    level = level_of(key, dims, shards, -0.22, 0.18) if shards else 1.0
    array = jax.random.normal(key, dims, jnp.float32) * deviation * level
    return jnp.minimum(jnp.maximum(array, -bound), bound).astype(held_as)


def setup_inputs(seed: int = 0) -> dict:
    seeds = jax.random.split(jax.random.key(seed), 7)
    return {
        "coefficients": noise(seeds[0], (2, ORBS, SLOT_ALL, NG), (8 * NCOL * NG) ** -0.5, 0.0009765625, ((1, 2), (2, 64)), jnp.float32),
        "col_map": draw_col_map(jax.random.fold_in(seeds[6], 71), 0),
        "charge_cell": with_ends(jax.random.randint(seeds[2], (3, NQ), 0, NG), jax.random.fold_in(seeds[2], 1), 0, NG - 1).astype(jnp.int32),
        "charge_frac": jnp.clip(jax.random.uniform(seeds[3], (3, NQ), jnp.float32, 0.05, 0.95), 0.05, 0.95),
        "charge": jnp.clip(jax.random.uniform(seeds[4], (NQ,), jnp.float32, -1.5, 1.5), -1.5, 1.5),
        "tile_list": draw_tile_list(jax.random.fold_in(seeds[6], 71), 0),
    }


spacing = 0.25
soften_sq = 0.09
damping = 1.0
volume = spacing * spacing * spacing
peak_slope = 2.0 / (math.sqrt(math.pi) * damping)

def tile_field(density, start_a, start_b, grid_len, neighbor_row, charge_cell, charge_frac, charge):
    plane_count, row_count, line_count = density.shape
    coord_a = (start_a + jnp.arange(plane_count)).astype(density.dtype)
    coord_b = (start_b + jnp.arange(row_count)).astype(density.dtype)
    coord_c = jnp.arange(line_count).astype(density.dtype)
    half_len = grid_len / 2.0

    def wrap_offset(coord, center):
        return spacing * (jnp.mod(coord - center + half_len, grid_len) - half_len)

    def visit(total, index):
        center = charge_cell[:, index].astype(density.dtype) + charge_frac[:, index]
        off_a = wrap_offset(coord_a, center[0])
        off_b = wrap_offset(coord_b, center[1])
        off_c = wrap_offset(coord_c, center[2])
        dist_sq = off_a[:, None, None] ** 2 + off_b[None, :, None] ** 2 + off_c[None, None, :] ** 2 + soften_sq
        radius = jnp.sqrt(dist_sq)
        ratio = lax.erf(radius / damping)
        kernel = ratio / radius
        slope = (peak_slope * jnp.exp(-dist_sq / (damping * damping)) * radius - ratio) / dist_sq
        weight = density * slope / radius
        push_a = jnp.sum(lax.optimization_barrier(jnp.sum(weight, axis=(1, 2))) * off_a)
        push_b = jnp.sum(lax.optimization_barrier(jnp.sum(weight, axis=(0, 2))) * off_b)
        push_c = jnp.sum(lax.optimization_barrier(jnp.sum(weight, axis=(0, 1))) * off_c)
        strength = charge[index]
        return (total + strength * kernel, strength * volume * jnp.stack([push_a, push_b, push_c]))
    potential, pushes = lax.scan(visit, jnp.zeros(density.shape, density.dtype), neighbor_row)
    return (potential, jnp.transpose(pushes))

def reference(coefficients, col_map, charge_cell, charge_frac, charge, tile_list):
    real_parts = []
    imag_parts = []
    for orbital in range(ORBS):
        columns = lax.complex(coefficients[0, orbital], coefficients[1, orbital])
        spectrum = jnp.zeros((NG * NG, NG), columns.dtype).at[col_map].set(columns, mode='drop')
        field = jnp.fft.ifftn(spectrum.reshape(NG, NG, NG)) * (NG * NG * NG)
        field = jnp.transpose(field, (2, 0, 1))[:PLANES]
        real_parts.append(jnp.real(field))
        imag_parts.append(jnp.imag(field))
    density = real_parts[0] * real_parts[0] + imag_parts[0] * imag_parts[0]
    for orbital in range(1, ORBS):
        density = density + real_parts[orbital] * real_parts[orbital] + imag_parts[orbital] * imag_parts[orbital]
    blocks = density.reshape(N_PW, NP, N_MM, NGH, NG).transpose(0, 2, 1, 3, 4).reshape(N_PW * N_MM, NP, NGH, NG)

    def one_tile(inputs):
        index, block, neighbor_row = inputs
        start_a = index // N_MM * NP
        start_b = index % N_MM * NGH
        return tile_field(block, start_a, start_b, NG, neighbor_row, charge_cell, charge_frac, charge)
    tile_pots, pushes = lax.map(one_tile, (jnp.arange(N_PW * N_MM, dtype=jnp.int32), blocks, tile_list))
    potential = tile_pots.reshape(N_PW, N_MM, NP, NGH, NG).transpose(0, 2, 1, 3, 4).reshape(PLANES, NG, NG)
    spread = jnp.transpose(pushes, (1, 0, 2)).reshape(3, -1)
    forces = jnp.zeros((3, NQ), jnp.float32).at[:, tile_list.reshape(-1)].add(spread)
    field_orbital = jnp.stack([jnp.stack([potential * part for part in real_parts]), jnp.stack([potential * part for part in imag_parts])])
    return (field_orbital, forces)
```

```python
import functools
import math

import jax
import jax.numpy as jnp
import ml_dtypes
import numpy as np
from jax import lax
from jax.experimental import pallas as pl
from jax.experimental.pallas import tpu as pltpu
from jax.sharding import PartitionSpec as P

f32, bf16, i32 = jnp.float32, jnp.bfloat16, jnp.int32
N = 384
HALF = 192
LANE = 128
SPACING = 0.25
SOFTEN = 0.09
VOLUME = SPACING**3
PEAK = 2.0 / math.sqrt(math.pi)
EMPTY = N * N
TILE_CHUNKS = 8
NT = (((1,), (1,)), ((), ()))
VMEM_LIMIT = 60 * 1024 * 1024


def split_table(table):
    high = table.astype(np.float32).astype(ml_dtypes.bfloat16)
    low = (table - high.astype(np.float64)).astype(np.float32).astype(ml_dtypes.bfloat16)
    return high, low


def tables(planes):
    index = np.arange(N, dtype=np.int64)
    angle = 2.0 * np.pi / N * ((index[:, None] * index[None, :]) % N).astype(np.float64)
    cos, sin = np.cos(angle), np.sin(angle)
    cz, sz = cos[:planes], sin[:planes]
    first = np.block([[cz, -sz], [sz, cz]])
    first_high, first_low = split_table(first)
    cos_high, cos_low = split_table(cos)
    sin_high, sin_low = split_table(sin)
    return (
        np.concatenate([first_high, first_low], axis=0),
        np.concatenate([cos_high, sin_high, cos_low, sin_low], axis=0),
    )


def mm(a, b, dims=(((1,), (0,)), ((), ()))):
    return lax.dot_general(a, b, dims, preferred_element_type=f32)


def halves(value):
    high = value.astype(bf16)
    low = (value - high.astype(f32)).astype(bf16)
    return high, low


def columns_kernel(coef_ref, table_ref, out_ref, high_ref, low_ref):
    slots = coef_ref.shape[1]
    pad = high_ref.shape[0] - slots
    planes = out_ref.shape[0]
    for part in range(2):
        high, low = halves(coef_ref[part])
        high_ref[:slots, part * N : (part + 1) * N] = high
        low_ref[:slots, part * N : (part + 1) * N] = low
    high_ref[slots:, :] = jnp.zeros((pad, 2 * N), bf16)
    low_ref[slots:, :] = jnp.zeros((pad, 2 * N), bf16)
    rows = 2 * planes
    both = mm(table_ref[...], high_ref[...], NT)
    result = both[:rows] + both[rows:] + mm(table_ref[:rows], low_ref[...], NT)
    for part in range(2):
        for piece in range(4):
            out_ref[:, 4 * part + piece, :] = result[
                part * planes : (part + 1) * planes, piece * LANE : (piece + 1) * LANE
            ]


def wrap(offset):
    shifted = offset + HALF
    shifted = jnp.where(shifted < 0, shifted + N, shifted)
    shifted = jnp.where(shifted >= N, shifted - N, shifted)
    return SPACING * (shifted - HALF)


ERF_NUM = (
    -2.72614225801306e-10,
    2.77068142495902e-08,
    -2.10102402082508e-06,
    -5.69250639462346e-05,
    -7.34990630326855e-04,
    -2.95459980854025e-03,
    -1.60960333262415e-02,
)
ERF_DEN = (
    -1.45660718464996e-05,
    -2.13374055278905e-04,
    -1.68282697438203e-03,
    -7.37332916720468e-03,
    -1.42647390514189e-02,
)


def erf(s):
    s = jnp.minimum(s, 4.0)
    sq = s * s
    num = jnp.full_like(s, ERF_NUM[0])
    for c in ERF_NUM[1:]:
        num = num * sq + c
    den = jnp.full_like(s, ERF_DEN[0])
    for c in ERF_DEN[1:]:
        den = den * sq + c
    return s * num / den


def charges_kernel(
    list_s,
    cell_s,
    frac_s,
    plane_s,
    live_s,
    list_ref,
    cell_ref,
    frac_ref,
    charge_ref,
    gc_ref,
    pot_ref,
    slope_ref,
    offb_ref,
    offc_ref,
    col_ref,
    order_s,
    count_s,
    uab_ref,
    eab_ref,
    uc_ref,
    ec_ref,
):
    chunks = live_s.shape[0]

    def note(i, c):
        order_s[c] = i
        return c + live_s[i]

    count = lax.fori_loop(0, chunks, note, jnp.int32(0))
    for j in range(TILE_CHUNKS):
        order_s[count + j] = jnp.int32(chunks)
    count_s[0] = count
    gc = gc_ref[...]
    for pair in range(3):
        inside = (gc >= pair * LANE) & (gc < (pair + 1) * LANE)
        count_s[1 + pair] = jnp.max(jnp.where(inside, 1.0, 0.0)).astype(i32)

    listed = list_ref[...]
    mask = lax.broadcasted_iota(i32, (LANE, cell_ref.shape[1]), 1) == listed
    center = cell_ref[...].astype(f32) + frac_ref[...]

    def pick(row):
        return jnp.sum(jnp.where(mask, row, 0.0), axis=1, keepdims=True)

    ca, cb, cc = (pick(center[i : i + 1]) for i in range(3))
    strength = pick(charge_ref[...])
    plane = plane_s[0].astype(f32)
    off_a = wrap(plane - ca)
    col_ref[...] = jnp.concatenate(
        [off_a, strength, listed.astype(f32)] + [jnp.zeros((LANE, 5), f32)], axis=1
    )
    off_c = wrap(lax.broadcasted_iota(i32, (32, N), 1).astype(f32) - cc[:32])
    offc_ref[...] = off_c
    sq_c = off_c * off_c
    uc_ref[...] = sq_c
    ec_ref[...] = jnp.exp(-sq_c)

    def across(column):
        return jnp.transpose(jnp.broadcast_to(column, (LANE, LANE)))[:1]

    off_b = wrap(lax.broadcasted_iota(i32, (N, LANE), 0).astype(f32) - across(cb))
    offb_ref[...] = off_b
    row_a = across(off_a)
    uab = off_b * off_b + (row_a * row_a + SOFTEN)
    uab_ref[...] = uab
    eab_ref[...] = PEAK * jnp.exp(-uab)
    pot_ref[...] = jnp.zeros((N, N), f32)

    for q in range(32):
        base = (q // 16) * HALF
        ucq = jnp.broadcast_to(uc_ref[q : q + 1, :], (8, N))
        ecq = jnp.broadcast_to(ec_ref[q : q + 1, :], (8, N))
        own = list_s[q]
        power = jnp.broadcast_to(strength[q : q + 1, :], (8, N))

        def far(i, _, q=q, base=base, ucq=ucq, ecq=ecq, power=power):
            r = pl.multiple_of(base + 8 * i, 8)
            u = uab_ref[pl.ds(r, 8), q : q + 1] + ucq
            k = lax.rsqrt(u)
            e = eab_ref[pl.ds(r, 8), q : q + 1] * ecq
            slope_ref[q, pl.ds(pl.multiple_of(8 * i, 8), 8), :] = k * k * (e - k)
            pot_ref[pl.ds(r, 8), :] += power * k
            return 0

        lax.fori_loop(0, HALF // 8, far, 0, unroll=4)
        da = wrap(plane - (cell_s[0, own].astype(f32) + frac_s[0, own]))
        sb = cell_s[1, own].astype(f32) + frac_s[1, own]

        @pl.when(da * da < 16.0)
        def _(q=q, base=base, ucq=ucq, ecq=ecq, power=power, da=da, sb=sb):
            def near(i, _):
                r = pl.multiple_of(base + 8 * i, 8)
                db = jnp.abs(wrap(r.astype(f32) + 3.5 - sb))
                db = jnp.maximum(db - 3.5 * SPACING, 0.0)

                @pl.when(da * da + db * db < 16.0)
                def _():
                    u = uab_ref[pl.ds(r, 8), q : q + 1] + ucq
                    k = lax.rsqrt(u)
                    e = eab_ref[pl.ds(r, 8), q : q + 1] * ecq
                    full = erf(u * k) * k
                    slope_ref[q, pl.ds(pl.multiple_of(8 * i, 8), 8), :] = k * k * (e - full)
                    pot_ref[pl.ds(r, 8), :] += power * (full - k)

                return 0

            lax.fori_loop(0, HALF // 8, near, 0)


def grid_kernel(
    order_s,
    count_s,
    recv_ref,
    gb_ref,
    gc_ref,
    table_ref,
    pot_ref,
    slope_ref,
    offb_ref,
    offc_ref,
    col_ref,
    field_ref,
    push_ref,
    acc_ref,
    hot_ref,
    val_ref,
    tab_ref,
    flow_ref,
    mid_ref,
    dens_ref,
    sum_ref,
):
    sources = recv_ref.shape[0]
    width = TILE_CHUNKS * LANE
    acc_ref[...] = jnp.zeros(acc_ref.shape, f32)
    iota_b = lax.broadcasted_iota(i32, (N, LANE), 0)
    iota_c = lax.broadcasted_iota(i32, (LANE, LANE), 0)

    def tile(t, _):
        where = []
        for j in range(TILE_CHUNKS):
            index = order_s[t * TILE_CHUNKS + j]
            where.append(index)
            hot = iota_b == gb_ref[pl.ds(index, 1), :]
            hot_ref[:, j * LANE : (j + 1) * LANE] = jnp.where(hot, 1.0, 0.0).astype(bf16)
        for pair in range(3):

            @pl.when(count_s[1 + pair] > 0)
            def _(pair=pair):
                for j, index in enumerate(where):
                    source = jnp.minimum(index >> 2, sources - 1)
                    piece = index & 3
                    hot = (iota_c + pair * LANE) == gc_ref[pl.ds(index, 1), :]
                    cut = slice(j * LANE, (j + 1) * LANE)
                    for part in range(2):
                        value = recv_ref[source, pl.ds(4 * part + piece, 1), :]
                        high = value.astype(bf16).astype(f32)
                        low = value - high
                        for k, v in ((part, high), (2 + part, low)):
                            val_ref[k * LANE : (k + 1) * LANE, cut] = jnp.where(
                                hot, v, 0.0
                            ).astype(bf16)
                acc_ref[pair] += mm(hot_ref[...], val_ref[...], NT)

        return 0

    tiles = (count_s[0] + TILE_CHUNKS - 1) // TILE_CHUNKS
    lax.fori_loop(0, tiles, tile, 0)

    for level in range(2):
        cos = table_ref[2 * level * N : (2 * level + 1) * N, :]
        sin = table_ref[(2 * level + 1) * N : (2 * level + 2) * N, :]
        for pair in range(3):
            cut = slice(pair * LANE, (pair + 1) * LANE)
            top = slice(2 * pair * LANE, (2 * pair + 1) * LANE)
            bottom = slice((2 * pair + 1) * LANE, (2 * pair + 2) * LANE)
            tab_ref[level, top, :N] = cos[cut]
            tab_ref[level, top, N:] = sin[cut]
            tab_ref[level, bottom, :N] = -sin[cut]
            tab_ref[level, bottom, N:] = cos[cut]
    for pair in range(3):
        cut = slice(2 * pair * LANE, 2 * (pair + 1) * LANE)
        flow_ref[:N, cut] = acc_ref[pair, :, : 2 * LANE].astype(bf16)
        flow_ref[N:, cut] = acc_ref[pair, :, 2 * LANE :].astype(bf16)
    both = mm(flow_ref[...], tab_ref[0])
    passed = both[:N] + both[N:] + mm(flow_ref[:N], tab_ref[1])
    high, low = halves(passed)
    mid_ref[...] = mm(table_ref[: 2 * N], high) + (
        mm(table_ref[2 * N :], high) + mm(table_ref[: 2 * N], low)
    )

    def finish(i, _):
        r = pl.ds(pl.multiple_of(8 * i, 8), 8)
        s = pl.ds(pl.multiple_of(N + 8 * i, 8), 8)
        real = mid_ref[r, :N] - mid_ref[s, N:]
        imag = mid_ref[s, :N] + mid_ref[r, N:]
        dens_ref[r, :] = real * real + imag * imag
        pot = pot_ref[r, :]
        field_ref[0, r, :] = pot * real
        field_ref[1, r, :] = pot * imag
        return 0

    lax.fori_loop(0, N // 8, finish, 0, unroll=4)

    for q in range(32):
        base = (q // 16) * HALF

        def gather(i, carry, q=q, base=base):
            plain, scaled = carry
            r = pl.ds(pl.multiple_of(base + 8 * i, 8), 8)
            w = dens_ref[r, :] * slope_ref[q, pl.ds(pl.multiple_of(8 * i, 8), 8), :]
            return plain + w, scaled + w * offb_ref[r, q : q + 1]

        zero = jnp.zeros((8, N), f32)
        plain, scaled = lax.fori_loop(0, HALF // 8, gather, (zero, zero), unroll=4)
        sum_ref[q : q + 1, :] = jnp.sum(plain, axis=0, keepdims=True)
        sum_ref[32 + q : 33 + q, :] = jnp.sum(scaled, axis=0, keepdims=True)
    plain = sum_ref[:32, :]
    off_a = col_ref[:32, 0:1]
    scale = col_ref[:32, 1:2] * VOLUME
    push_a = off_a * jnp.sum(plain, axis=1, keepdims=True) * scale
    push_b = jnp.sum(sum_ref[32:, :], axis=1, keepdims=True) * scale
    push_c = jnp.sum(plain * offc_ref[...], axis=1, keepdims=True) * scale
    packed = jnp.concatenate([push_a, push_b, push_c, 0.5 * col_ref[:32, 2:3]], axis=0)
    turned = jnp.transpose(jnp.broadcast_to(packed, (LANE, LANE)))
    push_ref[...] = turned[:8]


def spread_kernel(terms_ref, out_ref):
    terms = terms_ref[...]
    charges = out_ref.shape[1]
    lane = lax.broadcasted_iota(i32, (terms.shape[0], charges), 1).astype(f32)
    totals = [jnp.zeros((terms.shape[0], charges), f32)] * 3
    for q in range(32):
        hot = terms[:, 96 + q : 97 + q] == lane
        for axis in range(3):
            value = terms[:, 32 * axis + q : 32 * axis + q + 1]
            totals[axis] = totals[axis] + jnp.where(hot, value, 0.0)
    for axis in range(3):
        out_ref[axis : axis + 1, :] = jnp.sum(totals[axis], axis=0, keepdims=True)


def vmem(count):
    return [pl.BlockSpec(memory_space=pltpu.VMEM)] * count


def smem(count):
    return [pl.BlockSpec(memory_space=pltpu.SMEM)] * count


def params():
    return pltpu.CompilerParams(vmem_limit_bytes=VMEM_LIMIT)


def local(coefficients, col_map, charge_cell, charge_frac, charge, tile_list):
    slots = coefficients.shape[2]
    sources = lax.axis_size("pw")
    planes = sources
    plane = lax.axis_index("pw").astype(i32)
    first_table, second_table = tables(planes)
    chunks = 4 * sources

    own = tile_list[0]
    other = lax.ppermute(own, "mm", [(0, 1), (1, 0)])
    first = lax.axis_index("mm") == 0
    listed = jnp.concatenate([jnp.where(first, own, other), jnp.where(first, other, own)])
    listed_col = jnp.pad(listed, (0, LANE - 32), constant_values=-1)[:, None]

    sent = pl.pallas_call(
        columns_kernel,
        out_shape=jax.ShapeDtypeStruct((planes, 8, LANE), f32),
        in_specs=vmem(2),
        out_specs=vmem(1)[0],
        scratch_shapes=[pltpu.VMEM((4 * LANE, 2 * N), bf16)] * 2,
        compiler_params=params(),
        name="columns",
    )(coefficients.reshape(2, slots, N), jnp.asarray(first_table))
    recv = lax.all_to_all(sent, "pw", 0, 0, tiled=True)

    grid = jnp.pad(
        col_map.reshape(sources, slots), ((0, 2), (0, 4 * LANE - slots)), constant_values=EMPTY
    ).reshape(chunks + 8, LANE)
    live = grid < EMPTY
    gb = jnp.where(live, grid // N, -1000)
    gc = jnp.where(live, grid % N, -1000)
    live_chunk = live[:chunks, 0].astype(i32)

    pot, slope, offb, offc, col, order, count = pl.pallas_call(
        charges_kernel,
        out_shape=(
            jax.ShapeDtypeStruct((N, N), f32),
            jax.ShapeDtypeStruct((32, HALF, N), f32),
            jax.ShapeDtypeStruct((N, LANE), f32),
            jax.ShapeDtypeStruct((32, N), f32),
            jax.ShapeDtypeStruct((LANE, 8), f32),
            jax.ShapeDtypeStruct((chunks + TILE_CHUNKS,), i32),
            jax.ShapeDtypeStruct((4,), i32),
        ),
        in_specs=smem(5) + vmem(5),
        out_specs=tuple(vmem(5) + smem(2)),
        scratch_shapes=[
            pltpu.VMEM((N, LANE), f32),
            pltpu.VMEM((N, LANE), f32),
            pltpu.VMEM((32, N), f32),
            pltpu.VMEM((32, N), f32),
        ],
        compiler_params=params(),
        name="charges",
    )(
        listed,
        charge_cell,
        charge_frac,
        plane[None],
        live_chunk,
        listed_col,
        charge_cell,
        charge_frac,
        charge[None],
        gc,
    )

    field, push = pl.pallas_call(
        grid_kernel,
        out_shape=(
            jax.ShapeDtypeStruct((2, N, N), f32),
            jax.ShapeDtypeStruct((8, LANE), f32),
        ),
        in_specs=smem(2) + vmem(9),
        out_specs=tuple(vmem(2)),
        scratch_shapes=[
            pltpu.VMEM((3, N, 4 * LANE), f32),
            pltpu.VMEM((N, TILE_CHUNKS * LANE), bf16),
            pltpu.VMEM((4 * LANE, TILE_CHUNKS * LANE), bf16),
            pltpu.VMEM((2, 2 * N, 2 * N), bf16),
            pltpu.VMEM((2 * N, 2 * N), bf16),
            pltpu.VMEM((2 * N, 2 * N), f32),
            pltpu.VMEM((N, N), f32),
            pltpu.VMEM((64, N), f32),
        ],
        compiler_params=params(),
        name="grid",
    )(order, count, recv, gb, gc, jnp.asarray(second_table), pot, slope, offb, offc, col)

    push = push[:1]
    push = push + lax.ppermute(push, "mm", [(0, 1), (1, 0)])
    terms = lax.all_to_all(
        jnp.broadcast_to(push[None], (sources, 1, LANE)), "pw", 0, 0, tiled=True
    ).reshape(sources, LANE)
    forces = pl.pallas_call(
        spread_kernel,
        out_shape=jax.ShapeDtypeStruct((3, charge.shape[0]), f32),
        in_specs=vmem(1),
        out_specs=vmem(1)[0],
        compiler_params=params(),
        name="spread",
    )(terms)
    return (field[:, None, None], forces)


def solution(mesh):
    placed = (P(None, "mm", "pw", None), P(), P(), P(), P(), P(("pw", "mm"), None))
    return jax.shard_map(
        local,
        mesh=mesh,
        in_specs=placed,
        out_specs=(P(None, "mm", "pw", None, None), P()),
        check_vma=False,
    )
```

```python
import functools
import math

import jax
import jax.numpy as jnp
import ml_dtypes
import numpy as np
from jax import lax
from jax.experimental import pallas as pl
from jax.experimental.pallas import tpu as pltpu
from jax.sharding import PartitionSpec as P

f32, bf16, i32 = jnp.float32, jnp.bfloat16, jnp.int32
N = 384
HALF = 192
LANE = 128
SPACING = 0.25
SOFTEN = 0.09
VOLUME = SPACING**3
PEAK = 2.0 / math.sqrt(math.pi)
EMPTY = N * N
TILE_CHUNKS = 4
NT = (((1,), (1,)), ((), ()))
VMEM_LIMIT = 60 * 1024 * 1024


def split_table(table):
    high = table.astype(np.float32).astype(ml_dtypes.bfloat16)
    low = (table - high.astype(np.float64)).astype(np.float32).astype(ml_dtypes.bfloat16)
    return high, low


def tables(planes):
    index = np.arange(N, dtype=np.int64)
    angle = 2.0 * np.pi / N * ((index[:, None] * index[None, :]) % N).astype(np.float64)
    cos, sin = np.cos(angle), np.sin(angle)
    cz, sz = cos[:planes], sin[:planes]
    first = np.block([[cz, -sz], [sz, cz]])
    first_high, first_low = split_table(first)
    cos_high, cos_low = split_table(cos)
    sin_high, sin_low = split_table(sin)
    return (
        np.concatenate([first_high, first_low], axis=0),
        np.concatenate([cos_high, sin_high, cos_low, sin_low], axis=0),
    )


def mm(a, b, dims=(((1,), (0,)), ((), ()))):
    return lax.dot_general(a, b, dims, preferred_element_type=f32)


def halves(value):
    high = value.astype(bf16)
    low = (value - high.astype(f32)).astype(bf16)
    return high, low


def columns_kernel(coef_ref, table_ref, out_ref, high_ref, low_ref):
    slots = coef_ref.shape[1]
    pad = high_ref.shape[0] - slots
    planes = out_ref.shape[0]
    for part in range(2):
        high, low = halves(coef_ref[part])
        high_ref[:slots, part * N : (part + 1) * N] = high
        low_ref[:slots, part * N : (part + 1) * N] = low
    high_ref[slots:, :] = jnp.zeros((pad, 2 * N), bf16)
    low_ref[slots:, :] = jnp.zeros((pad, 2 * N), bf16)
    rows = 2 * planes
    both = mm(table_ref[...], high_ref[...], NT)
    result = both[:rows] + both[rows:] + mm(table_ref[:rows], low_ref[...], NT)
    for part in range(2):
        for piece in range(4):
            out_ref[:, 4 * part + piece, :] = result[
                part * planes : (part + 1) * planes, piece * LANE : (piece + 1) * LANE
            ]


def wrap(offset):
    shifted = offset + HALF
    shifted = jnp.where(shifted < 0, shifted + N, shifted)
    shifted = jnp.where(shifted >= N, shifted - N, shifted)
    return SPACING * (shifted - HALF)


ERF_NUM = (
    -2.72614225801306e-10,
    2.77068142495902e-08,
    -2.10102402082508e-06,
    -5.69250639462346e-05,
    -7.34990630326855e-04,
    -2.95459980854025e-03,
    -1.60960333262415e-02,
)
ERF_DEN = (
    -1.45660718464996e-05,
    -2.13374055278905e-04,
    -1.68282697438203e-03,
    -7.37332916720468e-03,
    -1.42647390514189e-02,
)


def erf(s):
    s = jnp.minimum(s, 4.0)
    sq = s * s
    num = jnp.full_like(s, ERF_NUM[0])
    for c in ERF_NUM[1:]:
        num = num * sq + c
    den = jnp.full_like(s, ERF_DEN[0])
    for c in ERF_DEN[1:]:
        den = den * sq + c
    return s * num / den


def charges_kernel(
    list_s,
    cell_s,
    frac_s,
    plane_s,
    live_s,
    list_ref,
    cell_ref,
    frac_ref,
    charge_ref,
    grid_ref,
    pot_ref,
    slope_out,
    offb_ref,
    offc_ref,
    col_ref,
    gb_ref,
    gc_ref,
    order_s,
    plan_s,
    uab_ref,
    eab_ref,
    uc_ref,
    ec_ref,
    slope_ref,
    sems,
):
    chunks = live_s.shape[0]

    def note(i, c):
        order_s[c] = i
        return c + live_s[i]

    count = lax.fori_loop(0, chunks, note, jnp.int32(0), unroll=8)
    for j in range(4 * TILE_CHUNKS):
        order_s[count + j] = jnp.int32(chunks)
    plan_s[0] = count
    cells = grid_ref[...]
    live = cells < EMPTY
    row = jnp.floor((cells.astype(f32) + 0.5) * (1.0 / N)).astype(i32)
    gb = jnp.where(live, row, -1000)
    gc = jnp.where(live, cells - N * row, -1000)
    blocks = cells.shape[0]
    for values, out, start in ((gb, gb_ref, 4), (gc, gc_ref, 8)):
        for piece in range(4):
            out[piece, :blocks, :] = values[:, piece * LANE : (piece + 1) * LANE]
        out[:, blocks:, :] = jnp.full((4, 8, LANE), -1000, i32)
        found = jnp.int32(0)
        for band in range(3):
            inside = (values >= band * LANE) & (values < (band + 1) * LANE)
            plan_s[start + found] = jnp.int32(band)
            found = found + jnp.max(jnp.where(inside, 1.0, 0.0)).astype(i32)
        for slot in range(4):
            plan_s[start + slot] = jnp.where(slot < found, plan_s[start + slot], 3)
        plan_s[start // 4] = (found + 1) // 2

    listed = list_ref[...]
    mask = lax.broadcasted_iota(i32, (LANE, cell_ref.shape[1]), 1) == listed
    center = cell_ref[...].astype(f32) + frac_ref[...]

    def pick(row):
        return jnp.sum(jnp.where(mask, row, 0.0), axis=1, keepdims=True)

    ca, cb, cc = (pick(center[i : i + 1]) for i in range(3))
    strength = pick(charge_ref[...])
    plane = plane_s[0].astype(f32)
    off_a = wrap(plane - ca)
    col_ref[...] = jnp.concatenate(
        [off_a, strength, listed.astype(f32)] + [jnp.zeros((LANE, 5), f32)], axis=1
    )
    off_c = wrap(lax.broadcasted_iota(i32, (32, N), 1).astype(f32) - cc[:32])
    offc_ref[...] = off_c
    sq_c = off_c * off_c
    uc_ref[...] = sq_c
    ec_ref[...] = jnp.exp(-sq_c)

    def across(column):
        return jnp.transpose(jnp.broadcast_to(column, (LANE, LANE)))[:1]

    off_b = wrap(lax.broadcasted_iota(i32, (N, LANE), 0).astype(f32) - across(cb))
    offb_ref[...] = off_b
    row_a = across(off_a)
    uab = off_b * off_b + (row_a * row_a + SOFTEN)
    uab_ref[...] = uab
    eab_ref[...] = PEAK * jnp.exp(-uab)
    pot_ref[...] = jnp.zeros((N, N), f32)

    copies = []
    for q in range(32):
        base = (q // 16) * HALF
        ucq = jnp.broadcast_to(uc_ref[q : q + 1, :], (8, N))
        ecq = jnp.broadcast_to(ec_ref[q : q + 1, :], (8, N))
        own = list_s[q]
        power = jnp.broadcast_to(strength[q : q + 1, :], (8, N))
        for i in range(HALF // 8):
            r = slice(base + 8 * i, base + 8 * i + 8)
            k = lax.rsqrt(uab_ref[r, q : q + 1] + ucq)
            e = eab_ref[r, q : q + 1] * ecq
            slope_ref[q, 8 * i : 8 * i + 8, :] = k * k * (e - k)
            pot_ref[r, :] += power * k
        da = wrap(plane - (cell_s[0, own].astype(f32) + frac_s[0, own]))
        sb = cell_s[1, own].astype(f32) + frac_s[1, own]

        @pl.when(da * da < 16.0)
        def _(q=q, base=base, ucq=ucq, ecq=ecq, power=power, da=da, sb=sb):
            def near(i, _):
                r = pl.multiple_of(base + 8 * i, 8)
                db = jnp.abs(wrap(r.astype(f32) + 3.5 - sb))
                db = jnp.maximum(db - 3.5 * SPACING, 0.0)

                @pl.when(da * da + db * db < 16.0)
                def _():
                    u = uab_ref[pl.ds(r, 8), q : q + 1] + ucq
                    k = lax.rsqrt(u)
                    e = eab_ref[pl.ds(r, 8), q : q + 1] * ecq
                    full = erf(u * k) * k
                    slope_ref[q, pl.ds(pl.multiple_of(8 * i, 8), 8), :] = k * k * (e - full)
                    pot_ref[pl.ds(r, 8), :] += power * (full - k)

                return 0

            lax.fori_loop(0, HALF // 8, near, 0)

        copy = pltpu.make_async_copy(slope_ref.at[q], slope_out.at[q], sems.at[q])
        copy.start()
        copies.append(copy)
    for copy in copies:
        copy.wait()


def grid_kernel(
    order_s,
    plan_s,
    recv_ref,
    gb_ref,
    gc_ref,
    table_in,
    pot_in,
    slope_in,
    offb_ref,
    offc_ref,
    col_ref,
    field_out,
    push_ref,
    acc_ref,
    val_a,
    val_b,
    hot_a,
    hot_b,
    tab_ref,
    flow_ref,
    edge_ref,
    pass_ref,
    mid_ref,
    dens_ref,
    sum_ref,
    field_ref,
    table_ref,
    pot_ref,
    slope_ref,
    sems,
):
    table_copy = pltpu.make_async_copy(table_in, table_ref, sems.at[0])
    pot_copy = pltpu.make_async_copy(pot_in, pot_ref, sems.at[1])
    slope_copy = pltpu.make_async_copy(slope_in, slope_ref, sems.at[2])
    table_copy.start()
    pot_copy.start()
    slope_copy.start()
    sources = recv_ref.shape[0]
    width = TILE_CHUNKS * LANE
    iota = lax.broadcasted_iota(i32, (LANE, LANE), 0)

    def build(tile, group_b, group_c, val_ref, hot_ref):
        for j in range(TILE_CHUNKS):
            index = order_s[tile * TILE_CHUNKS + j]
            block, piece = index >> 2, index & 3
            cut = slice(j * LANE, (j + 1) * LANE)
            gb = gb_ref[piece, pl.ds(block, 1), :]
            gc = gc_ref[piece, pl.ds(block, 1), :]
            source = jnp.minimum(block, sources - 1)
            parts = []
            for part in range(2):
                value = recv_ref[source, pl.ds(4 * part + piece, 1), :]
                high = value.astype(bf16).astype(f32)
                parts.append((part, high))
                parts.append((2 + part, value - high))
            for h in range(2):
                hot = iota == gc - LANE * plan_s[8 + 2 * group_c + h]
                hot_ref[h * LANE : (h + 1) * LANE, cut] = jnp.where(hot, 1.0, 0.0).astype(bf16)
                hit = iota == gb - LANE * plan_s[4 + 2 * group_b + h]
                for k, v in parts:
                    top = (4 * h + k) * LANE
                    val_ref[top : top + LANE, cut] = jnp.where(hit, v, 0.0).astype(bf16)

    acc_ref[0] = jnp.zeros(acc_ref.shape[1:], f32)
    build(0, 0, 0, val_a, hot_a)

    def step(t, _):
        build(2 * t + 1, 0, 0, val_b, hot_b)
        acc_ref[0] += mm(val_a[...], hot_a[...], NT)
        build(2 * t + 2, 0, 0, val_a, hot_a)
        acc_ref[0] += mm(val_b[...], hot_b[...], NT)
        return 0

    steps = (plan_s[0] + 2 * TILE_CHUNKS - 1) // (2 * TILE_CHUNKS)
    lax.fori_loop(0, steps, step, 0)

    def rest(combo, _):
        group_b, group_c = combo >> 1, combo & 1

        @pl.when((group_b < plan_s[1]) & (group_c < plan_s[2]))
        def _():
            acc_ref[combo] = jnp.zeros(acc_ref.shape[1:], f32)

            def extra(t, _):
                build(t, group_b, group_c, val_a, hot_a)
                acc_ref[combo] += mm(val_a[...], hot_a[...], NT)
                return 0

            lax.fori_loop(0, 2 * steps, extra, 0)

        return 0

    lax.fori_loop(1, 4, rest, 0)

    table_copy.wait()

    def transform(group_b):
        def along(group_c, first):
            for level in range(2):
                for h in range(2):
                    band = jnp.minimum(plan_s[8 + 2 * group_c + h], 2) * LANE
                    base = 2 * level * N
                    cos = table_ref[pl.ds(pl.multiple_of(base + band, LANE), LANE), :]
                    sin = table_ref[pl.ds(pl.multiple_of(base + N + band, LANE), LANE), :]
                    top = slice(h * LANE, (h + 1) * LANE)
                    bottom = slice((2 + h) * LANE, (3 + h) * LANE)
                    tab_ref[level, top, :N] = cos
                    tab_ref[level, top, N:] = sin
                    tab_ref[level, bottom, :N] = -sin
                    tab_ref[level, bottom, N:] = cos
            combo = 2 * group_b + group_c
            for h in range(2):
                for k in range(4):
                    top = ((k // 2) * 2 + h) * LANE
                    flow_ref[top : top + LANE, (k % 2) * 2 * LANE : (k % 2 + 1) * 2 * LANE] = acc_ref[
                        combo, (4 * h + k) * LANE : (4 * h + k + 1) * LANE, :
                    ].astype(bf16)
            half = 2 * LANE
            both = mm(flow_ref[...], tab_ref[0])
            result = both[:half] + both[half:] + mm(flow_ref[:half], tab_ref[1])
            pass_ref[...] = result if first else pass_ref[...] + result

        along(0, True)

        @pl.when(plan_s[2] > 1)
        def _():
            along(1, False)

        for h in range(2):
            band = jnp.minimum(plan_s[4 + 2 * group_b + h], 2) * LANE
            edge_ref[:, h * LANE : (h + 1) * LANE] = table_ref[
                :, pl.ds(pl.multiple_of(band, LANE), LANE)
            ]
        high, low = halves(pass_ref[...])
        result = mm(edge_ref[: 2 * N], high) + (
            mm(edge_ref[2 * N :], high) + mm(edge_ref[: 2 * N], low)
        )
        mid_ref[...] = result if group_b == 0 else mid_ref[...] + result

    transform(0)

    @pl.when(plan_s[1] > 1)
    def _():
        transform(1)

    pot_copy.wait()

    def finish(i, _):
        r = pl.ds(pl.multiple_of(8 * i, 8), 8)
        s = pl.ds(pl.multiple_of(N + 8 * i, 8), 8)
        real = mid_ref[r, :N] - mid_ref[s, N:]
        imag = mid_ref[s, :N] + mid_ref[r, N:]
        dens_ref[r, :] = real * real + imag * imag
        pot = pot_ref[r, :]
        field_ref[0, r, :] = pot * real
        field_ref[1, r, :] = pot * imag
        return 0

    lax.fori_loop(0, N // 8, finish, 0, unroll=8)
    field_copy = pltpu.make_async_copy(field_ref, field_out, sems.at[3])
    field_copy.start()
    slope_copy.wait()

    for q in range(32):
        base = (q // 16) * HALF
        plain = [jnp.zeros((8, LANE), f32)] * 3
        scaled = jnp.zeros((8, LANE), f32)
        for i in range(HALF // 8):
            r = slice(base + 8 * i, base + 8 * i + 8)
            w = dens_ref[r, :] * slope_ref[q, 8 * i : 8 * i + 8, :]
            w = [w[:, k * LANE : (k + 1) * LANE] for k in range(3)]
            plain = [p + v for p, v in zip(plain, w)]
            scaled = scaled + (w[0] + w[1] + w[2]) * offb_ref[r, q : q + 1]
        for k in range(3):
            sum_ref[q : q + 1, k * LANE : (k + 1) * LANE] = jnp.sum(plain[k], axis=0, keepdims=True)
        sum_ref[32 + q : 33 + q, :LANE] = jnp.sum(scaled, axis=0, keepdims=True)
    plain = sum_ref[:32, :]
    off_a = col_ref[:32, 0:1]
    scale = col_ref[:32, 1:2] * VOLUME
    push_a = off_a * jnp.sum(plain, axis=1, keepdims=True) * scale
    push_b = jnp.sum(sum_ref[32:, :LANE], axis=1, keepdims=True) * scale
    push_c = jnp.sum(plain * offc_ref[...], axis=1, keepdims=True) * scale
    packed = jnp.concatenate([push_a, push_b, push_c, 0.5 * col_ref[:32, 2:3]], axis=0)
    push_ref[...] = jnp.transpose(jnp.broadcast_to(packed, (LANE, LANE)))[:1]
    field_copy.wait()


def spread_kernel(terms_ref, out_ref):
    terms = terms_ref[...]
    charges = out_ref.shape[1]
    lane = lax.broadcasted_iota(i32, (terms.shape[0], charges), 1).astype(f32)
    totals = [jnp.zeros((terms.shape[0], charges), f32)] * 3
    for q in range(32):
        hot = terms[:, 96 + q : 97 + q] == lane
        for axis in range(3):
            value = terms[:, 32 * axis + q : 32 * axis + q + 1]
            totals[axis] = totals[axis] + jnp.where(hot, value, 0.0)
    for axis in range(3):
        out_ref[axis : axis + 1, :] = jnp.sum(totals[axis], axis=0, keepdims=True)


def vmem(count):
    return [pl.BlockSpec(memory_space=pltpu.VMEM)] * count


def smem(count):
    return [pl.BlockSpec(memory_space=pltpu.SMEM)] * count


def anywhere(count):
    return [pl.BlockSpec(memory_space=pl.ANY)] * count


def params():
    return pltpu.CompilerParams(vmem_limit_bytes=VMEM_LIMIT)


def local(coefficients, col_map, charge_cell, charge_frac, charge, tile_list):
    slots = coefficients.shape[2]
    sources = lax.axis_size("pw")
    planes = sources
    plane = lax.axis_index("pw").astype(i32)
    first_table, second_table = tables(planes)
    chunks = 4 * sources

    own = tile_list[0]
    other = lax.ppermute(own, "mm", [(0, 1), (1, 0)])
    first = lax.axis_index("mm") == 0
    listed = jnp.concatenate([jnp.where(first, own, other), jnp.where(first, other, own)])
    listed_col = jnp.pad(listed, (0, LANE - 32), constant_values=-1)[:, None]

    sent = pl.pallas_call(
        columns_kernel,
        out_shape=jax.ShapeDtypeStruct((planes, 8, LANE), f32),
        in_specs=vmem(2),
        out_specs=vmem(1)[0],
        scratch_shapes=[pltpu.VMEM((4 * LANE, 2 * N), bf16)] * 2,
        compiler_params=params(),
        name="columns",
    )(coefficients.reshape(2, slots, N), jnp.asarray(first_table))
    recv = lax.all_to_all(sent, "pw", 0, 0, tiled=True)

    blocks = col_map.reshape(sources, slots)
    grid = jnp.pad(blocks, ((0, 0), (0, 4 * LANE - slots)), constant_values=EMPTY)
    live_chunk = (blocks[:, ::LANE] < EMPTY).astype(i32).reshape(chunks)

    pot, slope, offb, offc, col, gb, gc, order, plan = pl.pallas_call(
        charges_kernel,
        out_shape=(
            jax.ShapeDtypeStruct((N, N), f32),
            jax.ShapeDtypeStruct((32, HALF, N), f32),
            jax.ShapeDtypeStruct((N, LANE), f32),
            jax.ShapeDtypeStruct((32, N), f32),
            jax.ShapeDtypeStruct((LANE, 8), f32),
            jax.ShapeDtypeStruct((4, sources + 8, LANE), i32),
            jax.ShapeDtypeStruct((4, sources + 8, LANE), i32),
            jax.ShapeDtypeStruct((chunks + 4 * TILE_CHUNKS,), i32),
            jax.ShapeDtypeStruct((16,), i32),
        ),
        in_specs=smem(5) + vmem(5),
        out_specs=tuple(vmem(1) + anywhere(1) + vmem(5) + smem(2)),
        scratch_shapes=[
            pltpu.VMEM((N, LANE), f32),
            pltpu.VMEM((N, LANE), f32),
            pltpu.VMEM((32, N), f32),
            pltpu.VMEM((32, N), f32),
            pltpu.VMEM((32, HALF, N), f32),
            pltpu.SemaphoreType.DMA((32,)),
        ],
        compiler_params=params(),
        name="charges",
    )(
        listed,
        charge_cell,
        charge_frac,
        plane[None],
        live_chunk,
        listed_col,
        charge_cell,
        charge_frac,
        charge[None],
        grid,
    )

    field, push = pl.pallas_call(
        grid_kernel,
        out_shape=(
            jax.ShapeDtypeStruct((2, N, N), f32),
            jax.ShapeDtypeStruct((1, LANE), f32),
        ),
        in_specs=smem(2) + vmem(3) + anywhere(3) + vmem(3),
        out_specs=tuple(anywhere(1) + vmem(1)),
        scratch_shapes=[
            pltpu.VMEM((4, 8 * LANE, 2 * LANE), f32),
            pltpu.VMEM((8 * LANE, TILE_CHUNKS * LANE), bf16),
            pltpu.VMEM((8 * LANE, TILE_CHUNKS * LANE), bf16),
            pltpu.VMEM((2 * LANE, TILE_CHUNKS * LANE), bf16),
            pltpu.VMEM((2 * LANE, TILE_CHUNKS * LANE), bf16),
            pltpu.VMEM((2, 4 * LANE, 2 * N), bf16),
            pltpu.VMEM((4 * LANE, 4 * LANE), bf16),
            pltpu.VMEM((4 * N, 2 * LANE), bf16),
            pltpu.VMEM((2 * LANE, 2 * N), f32),
            pltpu.VMEM((2 * N, 2 * N), f32),
            pltpu.VMEM((N, N), f32),
            pltpu.VMEM((64, N), f32),
            pltpu.VMEM((2, N, N), f32),
            pltpu.VMEM((4 * N, N), bf16),
            pltpu.VMEM((N, N), f32),
            pltpu.VMEM((32, HALF, N), f32),
            pltpu.SemaphoreType.DMA((4,)),
        ],
        compiler_params=params(),
        name="grid",
    )(order, plan, recv, gb, gc, jnp.asarray(second_table), pot, slope, offb, offc, col)

    push = push + lax.ppermute(push, "mm", [(0, 1), (1, 0)])
    terms = lax.all_to_all(
        jnp.broadcast_to(push[None], (sources, 1, LANE)), "pw", 0, 0, tiled=True
    ).reshape(sources, LANE)
    forces = pl.pallas_call(
        spread_kernel,
        out_shape=jax.ShapeDtypeStruct((3, charge.shape[0]), f32),
        in_specs=vmem(1),
        out_specs=vmem(1)[0],
        compiler_params=params(),
        name="spread",
    )(terms)
    return (field[:, None, None], forces)


def solution(mesh):
    placed = (P(None, "mm", "pw", None), P(), P(), P(), P(), P(("pw", "mm"), None))
    return jax.shard_map(
        local,
        mesh=mesh,
        in_specs=placed,
        out_specs=(P(None, "mm", "pw", None, None), P()),
        check_vma=False,
    )
```

```python
import functools
import math

import jax
import jax.numpy as jnp
import ml_dtypes
import numpy as np
from jax import lax
from jax.experimental import pallas as pl
from jax.experimental.pallas import tpu as pltpu
from jax.sharding import PartitionSpec as P

f32, bf16, i32 = jnp.float32, jnp.bfloat16, jnp.int32
N = 384
HALF = 192
LANE = 128
SPACING = 0.25
SOFTEN = 0.09
VOLUME = SPACING**3
PEAK = 2.0 / math.sqrt(math.pi)
EMPTY = N * N
TILE_CHUNKS = 8
NT = (((1,), (1,)), ((), ()))


def split_table(table):
    high = table.astype(np.float32).astype(ml_dtypes.bfloat16)
    low = (table - high.astype(np.float64)).astype(np.float32).astype(ml_dtypes.bfloat16)
    return high, low


def tables(planes):
    index = np.arange(N, dtype=np.int64)
    angle = 2.0 * np.pi / N * ((index[:, None] * index[None, :]) % N).astype(np.float64)
    cos, sin = np.cos(angle), np.sin(angle)
    cz, sz = cos[:planes], sin[:planes]
    first = np.block([[cz, -sz], [sz, cz]])
    first_high, first_low = split_table(first)
    cos_high, cos_low = split_table(cos)
    sin_high, sin_low = split_table(sin)
    return (
        np.concatenate([first_high, first_low], axis=0),
        np.concatenate([cos_high, sin_high, cos_low, sin_low], axis=0),
    )


def mm(a, b, dims=(((1,), (0,)), ((), ()))):
    return lax.dot_general(a, b, dims, preferred_element_type=f32)


def halves(value):
    high = value.astype(bf16)
    low = (value - high.astype(f32)).astype(bf16)
    return high, low


def columns_kernel(coef_ref, table_ref, out_ref, high_ref, low_ref):
    slots = coef_ref.shape[1]
    pad = high_ref.shape[0] - slots
    planes = out_ref.shape[0]
    for part in range(2):
        high, low = halves(coef_ref[part])
        high_ref[:slots, part * N : (part + 1) * N] = high
        low_ref[:slots, part * N : (part + 1) * N] = low
    high_ref[slots:, :] = jnp.zeros((pad, 2 * N), bf16)
    low_ref[slots:, :] = jnp.zeros((pad, 2 * N), bf16)
    rows = 2 * planes
    both = mm(table_ref[...], high_ref[...], NT)
    result = both[:rows] + both[rows:] + mm(table_ref[:rows], low_ref[...], NT)
    for part in range(2):
        for piece in range(4):
            out_ref[:, 4 * part + piece, :] = result[
                part * planes : (part + 1) * planes, piece * LANE : (piece + 1) * LANE
            ]


def wrap(offset):
    shifted = offset + HALF
    shifted = jnp.where(shifted < 0, shifted + N, shifted)
    shifted = jnp.where(shifted >= N, shifted - N, shifted)
    return SPACING * (shifted - HALF)


ERF_NUM = (
    -2.72614225801306e-10,
    2.77068142495902e-08,
    -2.10102402082508e-06,
    -5.69250639462346e-05,
    -7.34990630326855e-04,
    -2.95459980854025e-03,
    -1.60960333262415e-02,
)
ERF_DEN = (
    -1.45660718464996e-05,
    -2.13374055278905e-04,
    -1.68282697438203e-03,
    -7.37332916720468e-03,
    -1.42647390514189e-02,
)


def erf(s):
    s = jnp.minimum(s, 4.0)
    sq = s * s
    num = jnp.full_like(s, ERF_NUM[0])
    for c in ERF_NUM[1:]:
        num = num * sq + c
    den = jnp.full_like(s, ERF_DEN[0])
    for c in ERF_DEN[1:]:
        den = den * sq + c
    return s * num / den


def charges_kernel(
    list_s,
    cell_s,
    frac_s,
    plane_s,
    live_s,
    list_ref,
    cell_ref,
    frac_ref,
    charge_ref,
    grid_ref,
    pot_ref,
    slope_out,
    offb_ref,
    offc_ref,
    col_ref,
    gb_ref,
    gc_ref,
    order_s,
    plan_s,
    uab_ref,
    eab_ref,
    uc_ref,
    ec_ref,
    slope_ref,
    sems,
):
    chunks = live_s.shape[0]

    def note(i, c):
        order_s[c] = i
        return c + live_s[i]

    count = lax.fori_loop(0, chunks, note, jnp.int32(0), unroll=8)
    for j in range(4 * TILE_CHUNKS):
        order_s[count + j] = jnp.int32(chunks)
    plan_s[0] = count
    cells = grid_ref[...]
    live = cells < EMPTY
    row = jnp.floor((cells.astype(f32) + 0.5) * (1.0 / N)).astype(i32)
    gb = jnp.where(live, row, -1000)
    gc = jnp.where(live, cells - N * row, -1000)
    blocks = cells.shape[0]
    for values, out, start in ((gb, gb_ref, 4), (gc, gc_ref, 8)):
        for piece in range(4):
            out[piece, :blocks, :] = values[:, piece * LANE : (piece + 1) * LANE]
        out[:, blocks:, :] = jnp.full((4, 8, LANE), -1000, i32)
        found = jnp.int32(0)
        for band in range(3):
            inside = (values >= band * LANE) & (values < (band + 1) * LANE)
            plan_s[start + found] = jnp.int32(band)
            found = found + jnp.max(jnp.where(inside, 1.0, 0.0)).astype(i32)
        for slot in range(4):
            plan_s[start + slot] = jnp.where(slot < found, plan_s[start + slot], 3)
        plan_s[start // 4] = (found + 1) // 2

    listed = list_ref[...]
    mask = lax.broadcasted_iota(i32, (LANE, cell_ref.shape[1]), 1) == listed
    center = cell_ref[...].astype(f32) + frac_ref[...]

    def pick(row):
        return jnp.sum(jnp.where(mask, row, 0.0), axis=1, keepdims=True)

    ca, cb, cc = (pick(center[i : i + 1]) for i in range(3))
    strength = pick(charge_ref[...])
    plane = plane_s[0].astype(f32)
    off_a = wrap(plane - ca)
    col_ref[...] = jnp.concatenate(
        [off_a, strength, listed.astype(f32)] + [jnp.zeros((LANE, 5), f32)], axis=1
    )
    off_c = wrap(lax.broadcasted_iota(i32, (32, N), 1).astype(f32) - cc[:32])
    offc_ref[...] = off_c
    sq_c = off_c * off_c
    uc_ref[...] = sq_c
    ec_ref[...] = jnp.exp(-sq_c)

    def across(column):
        return jnp.transpose(jnp.broadcast_to(column, (LANE, LANE)))[:1]

    off_b = wrap(lax.broadcasted_iota(i32, (N, LANE), 0).astype(f32) - across(cb))
    offb_ref[...] = off_b
    row_a = across(off_a)
    uab = off_b * off_b + (row_a * row_a + SOFTEN)
    uab_ref[...] = uab
    eab_ref[...] = PEAK * jnp.exp(-uab)
    pot_ref[...] = jnp.zeros((N, N), f32)

    copies = []
    for q in range(32):
        base = (q // 16) * HALF
        ucq = jnp.broadcast_to(uc_ref[q : q + 1, :], (8, N))
        ecq = jnp.broadcast_to(ec_ref[q : q + 1, :], (8, N))
        own = list_s[q]
        power = jnp.broadcast_to(strength[q : q + 1, :], (8, N))
        for i in range(HALF // 8):
            r = slice(base + 8 * i, base + 8 * i + 8)
            k = lax.rsqrt(uab_ref[r, q : q + 1] + ucq)
            e = eab_ref[r, q : q + 1] * ecq
            slope_ref[q, 8 * i : 8 * i + 8, :] = k * k * (e - k)
            pot_ref[r, :] += power * k
        da = wrap(plane - (cell_s[0, own].astype(f32) + frac_s[0, own]))
        sb = cell_s[1, own].astype(f32) + frac_s[1, own]

        @pl.when(da * da < 16.0)
        def _(q=q, base=base, ucq=ucq, ecq=ecq, power=power, da=da, sb=sb):
            first = jnp.floor((sb - 16.0) * 0.125).astype(i32)

            def near(k, _):
                group = first + k
                group = jnp.where(group < 0, group + N // 8, group)
                group = jnp.where(group >= N // 8, group - N // 8, group)
                i = group - base // 8

                @pl.when((i >= 0) & (i < HALF // 8))
                def _():
                    r = pl.multiple_of(8 * group, 8)
                    u = uab_ref[pl.ds(r, 8), q : q + 1] + ucq
                    k = lax.rsqrt(u)
                    e = eab_ref[pl.ds(r, 8), q : q + 1] * ecq
                    full = erf(u * k) * k
                    slope_ref[q, pl.ds(pl.multiple_of(8 * i, 8), 8), :] = k * k * (e - full)
                    pot_ref[pl.ds(r, 8), :] += power * (full - k)

                return 0

            lax.fori_loop(0, 6, near, 0)

        copy = pltpu.make_async_copy(slope_ref.at[q], slope_out.at[q], sems.at[q])
        copy.start()
        copies.append(copy)
    for copy in copies:
        copy.wait()

def grid_kernel(
    order_s,
    plan_s,
    recv_ref,
    gb_ref,
    gc_ref,
    table_ref,
    pot_ref,
    slope_in,
    offb_ref,
    offc_ref,
    col_ref,
    field_out,
    push_ref,
    acc_ref,
    val_a,
    val_b,
    hot_a,
    hot_b,
    tab_ref,
    flow_ref,
    edge_ref,
    pass_ref,
    mid_ref,
    dens_ref,
    sum_ref,
    field_ref,
    slope_ref,
    sems,
):
    slope_copy = pltpu.make_async_copy(slope_in, slope_ref, sems.at[1])
    slope_copy.start()
    sources = recv_ref.shape[0]
    iota = lax.broadcasted_iota(i32, (LANE, LANE), 0).astype(f32).astype(bf16)
    one, zero = jnp.ones((LANE, LANE), bf16), jnp.zeros((LANE, LANE), bf16)

    def within(cells, band):
        return iota == (cells - LANE * band).astype(f32).astype(bf16)

    def build(tile, group_b, group_c, val_ref, hot_ref):
        for j in range(TILE_CHUNKS):
            index = order_s[tile * TILE_CHUNKS + j]
            block, piece = index >> 2, index & 3
            cut = slice(j * LANE, (j + 1) * LANE)
            gb = gb_ref[piece, pl.ds(block, 1), :]
            gc = gc_ref[piece, pl.ds(block, 1), :]
            source = jnp.minimum(block, sources - 1)
            parts = []
            for part in range(2):
                value = recv_ref[source, pl.ds(4 * part + piece, 1), :]
                high, low = halves(value)
                parts.append((part, high))
                parts.append((2 + part, low))
            for h in range(2):
                hot = within(gc, plan_s[8 + 2 * group_c + h])
                hot_ref[h * LANE : (h + 1) * LANE, cut] = jnp.where(hot, one, zero)
                hit = within(gb, plan_s[4 + 2 * group_b + h])
                for k, v in parts:
                    top = (4 * h + k) * LANE
                    val_ref[top : top + LANE, cut] = jnp.where(hit, v, zero)

    acc_ref[0] = jnp.zeros(acc_ref.shape[1:], f32)
    build(0, 0, 0, val_a, hot_a)

    def step(t, _):
        acc_ref[0] += mm(val_a[...], hot_a[...], NT)
        build(2 * t + 1, 0, 0, val_b, hot_b)
        acc_ref[0] += mm(val_b[...], hot_b[...], NT)
        build(2 * t + 2, 0, 0, val_a, hot_a)
        return 0

    steps = (plan_s[0] + 2 * TILE_CHUNKS - 1) // (2 * TILE_CHUNKS)
    lax.fori_loop(0, steps, step, 0)

    def rest(combo, _):
        group_b, group_c = combo >> 1, combo & 1

        @pl.when((group_b < plan_s[1]) & (group_c < plan_s[2]))
        def _():
            acc_ref[combo] = jnp.zeros(acc_ref.shape[1:], f32)

            def extra(t, _):
                build(t, group_b, group_c, val_a, hot_a)
                acc_ref[combo] += mm(val_a[...], hot_a[...], NT)
                return 0

            lax.fori_loop(0, 2 * steps, extra, 0)

        return 0

    lax.fori_loop(1, 4, rest, 0)

    def transform(group_b):
        def along(group_c, first):
            for level in range(2):
                for h in range(2):
                    band = jnp.minimum(plan_s[8 + 2 * group_c + h], 2) * LANE
                    base = 2 * level * N
                    cos = table_ref[pl.ds(pl.multiple_of(base + band, LANE), LANE), :]
                    sin = table_ref[pl.ds(pl.multiple_of(base + N + band, LANE), LANE), :]
                    top = slice(h * LANE, (h + 1) * LANE)
                    bottom = slice((2 + h) * LANE, (3 + h) * LANE)
                    tab_ref[level, top, :N] = cos
                    tab_ref[level, top, N:] = sin
                    tab_ref[level, bottom, :N] = -sin
                    tab_ref[level, bottom, N:] = cos
            combo = 2 * group_b + group_c
            for h in range(2):
                for k in range(4):
                    top = ((k // 2) * 2 + h) * LANE
                    flow_ref[top : top + LANE, (k % 2) * 2 * LANE : (k % 2 + 1) * 2 * LANE] = acc_ref[
                        combo, (4 * h + k) * LANE : (4 * h + k + 1) * LANE, :
                    ].astype(bf16)
            half = 2 * LANE
            both = mm(flow_ref[...], tab_ref[0])
            result = both[:half] + both[half:] + mm(flow_ref[:half], tab_ref[1])
            pass_ref[...] = result if first else pass_ref[...] + result

        along(0, True)

        @pl.when(plan_s[2] > 1)
        def _():
            along(1, False)

        for h in range(2):
            band = jnp.minimum(plan_s[4 + 2 * group_b + h], 2) * LANE
            edge_ref[:, h * LANE : (h + 1) * LANE] = table_ref[
                :, pl.ds(pl.multiple_of(band, LANE), LANE)
            ]
        high, low = halves(pass_ref[...])
        result = mm(edge_ref[: 2 * N], high) + (
            mm(edge_ref[2 * N :], high) + mm(edge_ref[: 2 * N], low)
        )
        mid_ref[...] = result if group_b == 0 else mid_ref[...] + result

    transform(0)

    @pl.when(plan_s[1] > 1)
    def _():
        transform(1)

    def finish(i, _):
        r = pl.ds(pl.multiple_of(8 * i, 8), 8)
        s = pl.ds(pl.multiple_of(N + 8 * i, 8), 8)
        real = mid_ref[r, :N] - mid_ref[s, N:]
        imag = mid_ref[s, :N] + mid_ref[r, N:]
        dens_ref[r, :] = real * real + imag * imag
        pot = pot_ref[r, :]
        field_ref[0, r, :] = pot * real
        field_ref[1, r, :] = pot * imag
        return 0

    lax.fori_loop(0, N // 8, finish, 0, unroll=8)
    field_copy = pltpu.make_async_copy(field_ref, field_out, sems.at[0])
    field_copy.start()
    slope_copy.wait()
    for q in range(32):
        base = (q // 16) * HALF
        plain = [jnp.zeros((8, LANE), f32)] * 3
        scaled = jnp.zeros((8, LANE), f32)
        for i in range(HALF // 8):
            r = slice(base + 8 * i, base + 8 * i + 8)
            w = dens_ref[r, :] * slope_ref[q, 8 * i : 8 * i + 8, :]
            w = [w[:, k * LANE : (k + 1) * LANE] for k in range(3)]
            plain = [p + v for p, v in zip(plain, w)]
            scaled = scaled + (w[0] + w[1] + w[2]) * offb_ref[r, q : q + 1]
        for k in range(3):
            sum_ref[q : q + 1, k * LANE : (k + 1) * LANE] = jnp.sum(plain[k], axis=0, keepdims=True)
        sum_ref[32 + q : 33 + q, :LANE] = jnp.sum(scaled, axis=0, keepdims=True)
    plain = sum_ref[:32, :]
    off_a = col_ref[:32, 0:1]
    scale = col_ref[:32, 1:2] * VOLUME
    push_a = off_a * jnp.sum(plain, axis=1, keepdims=True) * scale
    push_b = jnp.sum(sum_ref[32:, :LANE], axis=1, keepdims=True) * scale
    push_c = jnp.sum(plain * offc_ref[...], axis=1, keepdims=True) * scale
    packed = jnp.concatenate([push_a, push_b, push_c, 0.5 * col_ref[:32, 2:3]], axis=0)
    push_ref[...] = jnp.transpose(jnp.broadcast_to(packed, (LANE, LANE)))[:1]
    field_copy.wait()


def spread_kernel(terms_ref, out_ref):
    terms = terms_ref[...]
    charges = out_ref.shape[1]
    lane = lax.broadcasted_iota(i32, (terms.shape[0], charges), 1).astype(f32)
    totals = [jnp.zeros((terms.shape[0], charges), f32)] * 3
    for q in range(32):
        hot = terms[:, 96 + q : 97 + q] == lane
        for axis in range(3):
            value = terms[:, 32 * axis + q : 32 * axis + q + 1]
            totals[axis] = totals[axis] + jnp.where(hot, value, 0.0)
    for axis in range(3):
        out_ref[axis : axis + 1, :] = jnp.sum(totals[axis], axis=0, keepdims=True)


def vmem(count):
    return [pl.BlockSpec(memory_space=pltpu.VMEM)] * count


def smem(count):
    return [pl.BlockSpec(memory_space=pltpu.SMEM)] * count


def anywhere(count):
    return [pl.BlockSpec(memory_space=pltpu.HBM)] * count


def params(mebibytes):
    return pltpu.CompilerParams(vmem_limit_bytes=mebibytes * 1024 * 1024)


def local(coefficients, col_map, charge_cell, charge_frac, charge, tile_list):
    slots = coefficients.shape[2]
    sources = lax.axis_size("pw")
    planes = sources
    plane = lax.axis_index("pw").astype(i32)
    first_table, second_table = tables(planes)
    chunks = 4 * sources

    own = tile_list[0]
    other = lax.ppermute(own, "mm", [(0, 1), (1, 0)])
    first = lax.axis_index("mm") == 0
    listed = jnp.concatenate([jnp.where(first, own, other), jnp.where(first, other, own)])
    listed_col = jnp.pad(listed, (0, LANE - 32), constant_values=-1)[:, None]

    sent = pl.pallas_call(
        columns_kernel,
        out_shape=jax.ShapeDtypeStruct((planes, 8, LANE), f32),
        in_specs=vmem(2),
        out_specs=vmem(1)[0],
        scratch_shapes=[pltpu.VMEM((4 * LANE, 2 * N), bf16)] * 2,
        compiler_params=params(12),
        name="columns",
    )(coefficients.reshape(2, slots, N), jnp.asarray(first_table))
    recv = lax.all_to_all(sent, "pw", 0, 0, tiled=True)

    blocks = col_map.reshape(sources, slots)
    grid = jnp.pad(blocks, ((0, 0), (0, 4 * LANE - slots)), constant_values=EMPTY)
    live_chunk = (blocks[:, ::LANE] < EMPTY).astype(i32).reshape(chunks)

    pot, slope, offb, offc, col, gb, gc, order, plan = pl.pallas_call(
        charges_kernel,
        out_shape=(
            jax.ShapeDtypeStruct((N, N), f32),
            pltpu.HBM((32, HALF, N), f32),
            jax.ShapeDtypeStruct((N, LANE), f32),
            jax.ShapeDtypeStruct((32, N), f32),
            jax.ShapeDtypeStruct((LANE, 8), f32),
            jax.ShapeDtypeStruct((4, sources + 8, LANE), i32),
            jax.ShapeDtypeStruct((4, sources + 8, LANE), i32),
            jax.ShapeDtypeStruct((chunks + 4 * TILE_CHUNKS,), i32),
            jax.ShapeDtypeStruct((16,), i32),
        ),
        in_specs=smem(5) + vmem(5),
        out_specs=tuple(vmem(1) + anywhere(1) + vmem(5) + smem(2)),
        scratch_shapes=[
            pltpu.VMEM((N, LANE), f32),
            pltpu.VMEM((N, LANE), f32),
            pltpu.VMEM((32, N), f32),
            pltpu.VMEM((32, N), f32),
            pltpu.VMEM((32, HALF, N), f32),
            pltpu.SemaphoreType.DMA((32,)),
        ],
        compiler_params=params(50),
        name="charges",
    )(
        listed,
        charge_cell,
        charge_frac,
        plane[None],
        live_chunk,
        listed_col,
        charge_cell,
        charge_frac,
        charge[None],
        grid,
    )

    field, push = pl.pallas_call(
        grid_kernel,
        out_shape=(
            jax.ShapeDtypeStruct((2, N, N), f32),
            jax.ShapeDtypeStruct((1, LANE), f32),
        ),
        in_specs=smem(2) + vmem(5) + anywhere(1) + vmem(3),
        out_specs=tuple(anywhere(1) + vmem(1)),
        scratch_shapes=[
            pltpu.VMEM((4, 8 * LANE, 2 * LANE), f32),
            pltpu.VMEM((8 * LANE, TILE_CHUNKS * LANE), bf16),
            pltpu.VMEM((8 * LANE, TILE_CHUNKS * LANE), bf16),
            pltpu.VMEM((2 * LANE, TILE_CHUNKS * LANE), bf16),
            pltpu.VMEM((2 * LANE, TILE_CHUNKS * LANE), bf16),
            pltpu.VMEM((2, 4 * LANE, 2 * N), bf16),
            pltpu.VMEM((4 * LANE, 4 * LANE), bf16),
            pltpu.VMEM((4 * N, 2 * LANE), bf16),
            pltpu.VMEM((2 * LANE, 2 * N), f32),
            pltpu.VMEM((2 * N, 2 * N), f32),
            pltpu.VMEM((N, N), f32),
            pltpu.VMEM((64, N), f32),
            pltpu.VMEM((2, N, N), f32),
            pltpu.VMEM((32, HALF, N), f32),
            pltpu.SemaphoreType.DMA((2,)),
        ],
        compiler_params=params(50),
        name="grid",
    )(order, plan, recv, gb, gc, jnp.asarray(second_table), pot, slope, offb, offc, col)

    push = push + lax.ppermute(push, "mm", [(0, 1), (1, 0)])
    terms = lax.all_to_all(
        jnp.broadcast_to(push[None], (sources, 1, LANE)), "pw", 0, 0, tiled=True
    ).reshape(sources, LANE)
    forces = pl.pallas_call(
        spread_kernel,
        out_shape=jax.ShapeDtypeStruct((3, charge.shape[0]), f32),
        in_specs=vmem(1),
        out_specs=vmem(1)[0],
        compiler_params=params(12),
        name="spread",
    )(terms)
    return (field[:, None, None], forces)


def solution(mesh):
    placed = (P(None, "mm", "pw", None), P(), P(), P(), P(), P(("pw", "mm"), None))
    return jax.shard_map(
        local,
        mesh=mesh,
        in_specs=placed,
        out_specs=(P(None, "mm", "pw", None, None), P()),
        check_vma=False,
    )
```

```python
import functools
import math

import jax
import jax.numpy as jnp
import ml_dtypes
import numpy as np
from jax import lax
from jax.experimental import pallas as pl
from jax.experimental.pallas import tpu as pltpu
from jax.sharding import PartitionSpec as P

f32, bf16, i32 = jnp.float32, jnp.bfloat16, jnp.int32
N = 384
HALF = 192
LANE = 128
SPACING = 0.25
SOFTEN = 0.09
VOLUME = SPACING**3
PEAK = 2.0 / math.sqrt(math.pi)
EMPTY = N * N
TILE_CHUNKS = 8
NT = (((1,), (1,)), ((), ()))


def split_table(table):
    high = table.astype(np.float32).astype(ml_dtypes.bfloat16)
    low = (table - high.astype(np.float64)).astype(np.float32).astype(ml_dtypes.bfloat16)
    return high, low


def tables(planes):
    index = np.arange(N, dtype=np.int64)
    angle = 2.0 * np.pi / N * ((index[:, None] * index[None, :]) % N).astype(np.float64)
    cos, sin = np.cos(angle), np.sin(angle)
    cz, sz = cos[:planes], sin[:planes]
    first = np.block([[cz, -sz], [sz, cz]])
    first_high, first_low = split_table(first)
    cos_high, cos_low = split_table(cos)
    sin_high, sin_low = split_table(sin)
    return (
        np.concatenate([first_high, first_low], axis=0),
        np.concatenate([cos_high, sin_high, cos_low, sin_low], axis=0),
    )


def mm(a, b, dims=(((1,), (0,)), ((), ()))):
    return lax.dot_general(a, b, dims, preferred_element_type=f32)


def halves(value):
    high = value.astype(bf16)
    low = (value - high.astype(f32)).astype(bf16)
    return high, low


def flip_table(length):
    row = lax.broadcasted_iota(i32, (length, length), 0)
    column = lax.broadcasted_iota(i32, (length, length), 1)
    return jnp.where(row + column == length - 1, 1.0, 0.0).astype(bf16)


def columns_kernel(
    plane_s, coef_in, table_in, out_ref, coef_ref, table_ref, high_ref, low_ref, sems
):
    slots = coef_ref.shape[1]
    half = slots // 2
    copies = []
    for part in range(2):
        for piece in range(2):
            cut = pl.ds(piece * half, half)
            copies.append(
                pltpu.make_async_copy(
                    coef_in.at[part, cut], coef_ref.at[part, cut], sems.at[2 * part + piece]
                )
            )
    copies.append(pltpu.make_async_copy(table_in, table_ref, sems.at[4]))
    for copy in copies:
        copy.start()
    width = high_ref.shape[0]
    planes = out_ref.shape[0]
    high_ref[slots:, :] = jnp.zeros((width - slots, 2 * N), bf16)
    low_ref[slots:, :] = jnp.zeros((width - slots, 2 * N), bf16)
    for part in range(2):
        for piece in range(2):
            copies[2 * part + piece].wait()
            rows = slice(piece * half, (piece + 1) * half)
            high, low = halves(coef_ref[part, rows])
            high_ref[rows, part * N : (part + 1) * N] = high
            low_ref[rows, part * N : (part + 1) * N] = low
    copies[4].wait()
    rows = 2 * planes
    both = mm(table_ref[...], high_ref[...], NT)
    result = both[:rows] + both[rows:] + mm(table_ref[:rows], low_ref[...], NT)

    def put(values):
        for part in range(2):
            for piece in range(4):
                out_ref[:, 4 * part + piece, :] = values[
                    part * planes : (part + 1) * planes, piece * LANE : (piece + 1) * LANE
                ]

    reverse = plane_s[0] >= planes // 2

    @pl.when(jnp.logical_not(reverse))
    def _():
        put(result)

    @pl.when(reverse)
    def _():
        high, low = halves(result)
        flip = flip_table(width)
        put(mm(high, flip) + mm(low, flip))


def wrap(offset):
    shifted = offset + HALF
    shifted = jnp.where(shifted < 0, shifted + N, shifted)
    shifted = jnp.where(shifted >= N, shifted - N, shifted)
    return SPACING * (shifted - HALF)


ERF_NUM = (
    -2.72614225801306e-10,
    2.77068142495902e-08,
    -2.10102402082508e-06,
    -5.69250639462346e-05,
    -7.34990630326855e-04,
    -2.95459980854025e-03,
    -1.60960333262415e-02,
)
ERF_DEN = (
    -1.45660718464996e-05,
    -2.13374055278905e-04,
    -1.68282697438203e-03,
    -7.37332916720468e-03,
    -1.42647390514189e-02,
)


def erf(s):
    s = jnp.minimum(s, 4.0)
    sq = s * s
    num = jnp.full_like(s, ERF_NUM[0])
    for c in ERF_NUM[1:]:
        num = num * sq + c
    den = jnp.full_like(s, ERF_DEN[0])
    for c in ERF_DEN[1:]:
        den = den * sq + c
    return s * num / den


def charges_kernel(
    list_s,
    cell_s,
    frac_s,
    plane_s,
    list_ref,
    cell_ref,
    frac_ref,
    charge_ref,
    grid_ref,
    pot_ref,
    slope_out,
    offb_ref,
    offc_ref,
    col_ref,
    gb_ref,
    gc_ref,
    owner_ref,
    plan_s,
    uab_ref,
    eab_ref,
    uc_ref,
    ec_ref,
    slope_ref,
    sems,
):
    cells = grid_ref[...]
    pairs = cells.shape[0] // 2
    row = jnp.floor((cells.astype(f32) + 0.5) * (1.0 / N))
    gb = jnp.where(cells < EMPTY, row, -1000.0)
    gc = jnp.where(cells < EMPTY, cells.astype(f32) - N * row, -1000.0)
    high, low = halves(jnp.concatenate([gb[pairs:], gc[pairs:]], axis=0))
    flip = flip_table(cells.shape[1])
    turned = mm(high, flip) + mm(low, flip)
    owned = jnp.where(gb[:pairs] >= 0.0, 1.0, 0.0)
    for piece in range(4):
        cut = slice(piece * LANE, (piece + 1) * LANE)
        owner_ref[:, piece, :] = owned[:, cut]
        owner_ref[:, 4 + piece, :] = owned[:, cut]
    for values, other, out, start in (
        (gb[:pairs], turned[:pairs], gb_ref, 4),
        (gc[:pairs], turned[pairs:], gc_ref, 8),
    ):
        merged = jnp.maximum(values, other)
        for piece in range(4):
            out[piece] = merged[:, piece * LANE : (piece + 1) * LANE]
        found = jnp.int32(0)
        for band in range(3):
            inside = (merged >= band * LANE) & (merged < (band + 1) * LANE)
            plan_s[start + found] = jnp.int32(band)
            found = found + jnp.max(jnp.where(inside, 1.0, 0.0)).astype(i32)
        for slot in range(4):
            plan_s[start + slot] = jnp.where(slot < found, plan_s[start + slot], 3)
        plan_s[start // 4] = (found + 1) // 2

    listed = list_ref[...]
    mask = lax.broadcasted_iota(i32, (LANE, cell_ref.shape[1]), 1) == listed
    center = cell_ref[...].astype(f32) + frac_ref[...]

    def pick(row):
        return jnp.sum(jnp.where(mask, row, 0.0), axis=1, keepdims=True)

    ca, cb, cc = (pick(center[i : i + 1]) for i in range(3))
    strength = pick(charge_ref[...])
    plane = plane_s[0].astype(f32)
    off_a = wrap(plane - ca)
    col_ref[...] = jnp.concatenate(
        [off_a, strength, listed.astype(f32)] + [jnp.zeros((LANE, 5), f32)], axis=1
    )
    off_c = wrap(lax.broadcasted_iota(i32, (32, N), 1).astype(f32) - cc[:32])
    offc_ref[...] = off_c
    sq_c = off_c * off_c
    uc_ref[...] = sq_c
    ec_ref[...] = jnp.exp(-sq_c)

    def across(column):
        return jnp.transpose(jnp.broadcast_to(column, (LANE, LANE)))[:1]

    off_b = wrap(lax.broadcasted_iota(i32, (N, LANE), 0).astype(f32) - across(cb))
    offb_ref[...] = off_b
    row_a = across(off_a)
    uab = off_b * off_b + (row_a * row_a + SOFTEN)
    uab_ref[...] = uab
    eab_ref[...] = PEAK * jnp.exp(-uab)

    def wide(ref, q):
        return jnp.broadcast_to(ref[q : q + 1, :], (8, N))

    def power(q):
        return jnp.broadcast_to(strength[q : q + 1, :], (8, N))

    def near(q):
        base = (q // 16) * HALF
        own = list_s[q]
        da = wrap(plane - (cell_s[0, own].astype(f32) + frac_s[0, own]))

        @pl.when(da * da < 16.0)
        def _():
            sb = cell_s[1, own].astype(f32) + frac_s[1, own]
            first = jnp.floor((sb - 16.0) * 0.125).astype(i32)

            def fix(k, _):
                group = first + k
                group = jnp.where(group < 0, group + N // 8, group)
                group = jnp.where(group >= N // 8, group - N // 8, group)
                i = group - base // 8

                @pl.when((i >= 0) & (i < HALF // 8))
                def _():
                    r = pl.multiple_of(8 * group, 8)
                    u = uab_ref[pl.ds(r, 8), q : q + 1] + wide(uc_ref, q)
                    k = lax.rsqrt(u)
                    e = eab_ref[pl.ds(r, 8), q : q + 1] * wide(ec_ref, q)
                    full = erf(u * k) * k
                    slope_ref[q, pl.ds(pl.multiple_of(8 * i, 8), 8), :] = k * k * (e - full)
                    pot_ref[pl.ds(r, 8), :] += power(q) * (full - k)

                return 0

            lax.fori_loop(0, 6, fix, 0)

    copies = []
    for a in range(0, 16, 2):
        for half in range(2):
            pair = (16 * half + a, 16 * half + a + 1)
            lanes = [(q, wide(uc_ref, q), wide(ec_ref, q), power(q)) for q in pair]
            for i in range(HALF // 8):
                r = slice(half * HALF + 8 * i, half * HALF + 8 * i + 8)
                total = None
                for q, ucq, ecq, strong in lanes:
                    k = lax.rsqrt(uab_ref[r, q : q + 1] + ucq)
                    e = eab_ref[r, q : q + 1] * ecq
                    slope_ref[q, 8 * i : 8 * i + 8, :] = k * k * (e - k)
                    total = strong * k if total is None else total + strong * k
                pot_ref[r, :] = total if a == 0 else pot_ref[r, :] + total
        for q in (a, a + 1, 16 + a, 17 + a):
            near(q)
            copy = pltpu.make_async_copy(slope_ref.at[q], slope_out.at[q], sems.at[q])
            copy.start()
            copies.append(copy)
    for copy in copies:
        copy.wait()


def grid_kernel(
    plan_s,
    recv_ref,
    owner_ref,
    gb_ref,
    gc_ref,
    table_ref,
    pot_ref,
    slope_in,
    offb_ref,
    offc_ref,
    col_ref,
    field_out,
    push_ref,
    acc_ref,
    val_a,
    val_b,
    hot_a,
    hot_b,
    tab_ref,
    flow_ref,
    edge_ref,
    pass_ref,
    mid_ref,
    dens_ref,
    sum_ref,
    field_ref,
    slope_ref,
    merged_ref,
    sems,
):
    slope_copy = pltpu.make_async_copy(slope_in, slope_ref, sems.at[1])
    slope_copy.start()
    pairs = merged_ref.shape[0]
    merged_ref[...] = jnp.where(owner_ref[...] > 0.0, recv_ref[:pairs], recv_ref[pairs:])
    iota = lax.broadcasted_iota(i32, (LANE, LANE), 0).astype(f32).astype(bf16)
    one, zero = jnp.ones((LANE, LANE), bf16), jnp.zeros((LANE, LANE), bf16)

    def within(cells, band):
        return iota == (cells - (LANE * band).astype(f32)).astype(bf16)

    def build(tile, group_b, group_c, val_ref, hot_ref):
        for j in range(TILE_CHUNKS):
            pair = jnp.minimum(tile * (TILE_CHUNKS // 4) + j // 4, pairs - 1)
            piece = j % 4
            cut = slice(j * LANE, (j + 1) * LANE)
            gb = gb_ref[piece, pl.ds(pair, 1), :]
            gc = gc_ref[piece, pl.ds(pair, 1), :]
            parts = []
            for part in range(2):
                value = merged_ref[pair, 4 * part + piece : 4 * part + piece + 1, :]
                high, low = halves(value)
                parts.append((part, high))
                parts.append((2 + part, low))
            for h in range(2):
                hot = within(gc, plan_s[8 + 2 * group_c + h])
                hot_ref[h * LANE : (h + 1) * LANE, cut] = jnp.where(hot, one, zero)
                hit = within(gb, plan_s[4 + 2 * group_b + h])
                for k, v in parts:
                    top = (4 * h + k) * LANE
                    val_ref[top : top + LANE, cut] = jnp.where(hit, v, zero)

    acc_ref[0] = jnp.zeros(acc_ref.shape[1:], f32)
    build(0, 0, 0, val_a, hot_a)

    def step(t, _):
        acc_ref[0] += mm(val_a[...], hot_a[...], NT)
        build(2 * t + 1, 0, 0, val_b, hot_b)
        acc_ref[0] += mm(val_b[...], hot_b[...], NT)
        build(2 * t + 2, 0, 0, val_a, hot_a)
        return 0

    steps = 2 * pairs // TILE_CHUNKS
    lax.fori_loop(0, steps, step, 0)

    def rest(combo, _):
        group_b, group_c = combo >> 1, combo & 1

        @pl.when((group_b < plan_s[1]) & (group_c < plan_s[2]))
        def _():
            acc_ref[combo] = jnp.zeros(acc_ref.shape[1:], f32)

            def extra(t, _):
                build(t, group_b, group_c, val_a, hot_a)
                acc_ref[combo] += mm(val_a[...], hot_a[...], NT)
                return 0

            lax.fori_loop(0, 2 * steps, extra, 0)

        return 0

    lax.fori_loop(1, 4, rest, 0)

    def transform(group_b):
        def along(group_c, first):
            for level in range(2):
                for h in range(2):
                    band = jnp.minimum(plan_s[8 + 2 * group_c + h], 2) * LANE
                    base = 2 * level * N
                    cos = table_ref[pl.ds(pl.multiple_of(base + band, LANE), LANE), :]
                    sin = table_ref[pl.ds(pl.multiple_of(base + N + band, LANE), LANE), :]
                    top = slice(h * LANE, (h + 1) * LANE)
                    bottom = slice((2 + h) * LANE, (3 + h) * LANE)
                    tab_ref[level, top, :N] = cos
                    tab_ref[level, top, N:] = sin
                    tab_ref[level, bottom, :N] = -sin
                    tab_ref[level, bottom, N:] = cos
            combo = 2 * group_b + group_c
            for h in range(2):
                for k in range(4):
                    top = ((k // 2) * 2 + h) * LANE
                    flow_ref[top : top + LANE, (k % 2) * 2 * LANE : (k % 2 + 1) * 2 * LANE] = acc_ref[
                        combo, (4 * h + k) * LANE : (4 * h + k + 1) * LANE, :
                    ].astype(bf16)
            half = 2 * LANE
            both = mm(flow_ref[...], tab_ref[0])
            result = both[:half] + both[half:] + mm(flow_ref[:half], tab_ref[1])
            pass_ref[...] = result if first else pass_ref[...] + result

        along(0, True)

        @pl.when(plan_s[2] > 1)
        def _():
            along(1, False)

        for h in range(2):
            band = jnp.minimum(plan_s[4 + 2 * group_b + h], 2) * LANE
            edge_ref[:, h * LANE : (h + 1) * LANE] = table_ref[
                :, pl.ds(pl.multiple_of(band, LANE), LANE)
            ]
        high, low = halves(pass_ref[...])
        result = mm(edge_ref[: 2 * N], high) + (
            mm(edge_ref[2 * N :], high) + mm(edge_ref[: 2 * N], low)
        )
        mid_ref[...] = result if group_b == 0 else mid_ref[...] + result

    transform(0)

    @pl.when(plan_s[1] > 1)
    def _():
        transform(1)

    def finish(i, _):
        r = pl.ds(pl.multiple_of(8 * i, 8), 8)
        s = pl.ds(pl.multiple_of(N + 8 * i, 8), 8)
        real = mid_ref[r, :N] - mid_ref[s, N:]
        imag = mid_ref[s, :N] + mid_ref[r, N:]
        dens_ref[r, :] = real * real + imag * imag
        pot = pot_ref[r, :]
        field_ref[0, r, :] = pot * real
        field_ref[1, r, :] = pot * imag
        return 0

    lax.fori_loop(0, N // 8, finish, 0, unroll=8)
    field_copy = pltpu.make_async_copy(field_ref, field_out, sems.at[0])
    field_copy.start()
    slope_copy.wait()
    for q in range(32):
        base = (q // 16) * HALF
        plain = [jnp.zeros((8, LANE), f32)] * 3
        scaled = jnp.zeros((8, LANE), f32)
        for i in range(HALF // 8):
            r = slice(base + 8 * i, base + 8 * i + 8)
            w = dens_ref[r, :] * slope_ref[q, 8 * i : 8 * i + 8, :]
            w = [w[:, k * LANE : (k + 1) * LANE] for k in range(3)]
            plain = [p + v for p, v in zip(plain, w)]
            scaled = scaled + (w[0] + w[1] + w[2]) * offb_ref[r, q : q + 1]
        for k in range(3):
            sum_ref[q : q + 1, k * LANE : (k + 1) * LANE] = jnp.sum(plain[k], axis=0, keepdims=True)
        sum_ref[32 + q : 33 + q, :LANE] = jnp.sum(scaled, axis=0, keepdims=True)
    plain = sum_ref[:32, :]
    off_a = col_ref[:32, 0:1]
    scale = col_ref[:32, 1:2] * VOLUME
    push_a = off_a * jnp.sum(plain, axis=1, keepdims=True) * scale
    push_b = jnp.sum(sum_ref[32:, :LANE], axis=1, keepdims=True) * scale
    push_c = jnp.sum(plain * offc_ref[...], axis=1, keepdims=True) * scale
    packed = jnp.concatenate([push_a, push_b, push_c, 0.5 * col_ref[:32, 2:3]], axis=0)
    push_ref[...] = jnp.transpose(jnp.broadcast_to(packed, (LANE, LANE)))[:1]
    field_copy.wait()


def spread_kernel(terms_ref, out_ref):
    terms = terms_ref[...]
    charges = out_ref.shape[1]
    lane = lax.broadcasted_iota(i32, (terms.shape[0], charges), 1).astype(f32)
    totals = [jnp.zeros((terms.shape[0], charges), f32)] * 3
    for q in range(32):
        hot = terms[:, 96 + q : 97 + q] == lane
        for axis in range(3):
            value = terms[:, 32 * axis + q : 32 * axis + q + 1]
            totals[axis] = totals[axis] + jnp.where(hot, value, 0.0)
    for axis in range(3):
        out_ref[axis : axis + 1, :] = jnp.sum(totals[axis], axis=0, keepdims=True)


def vmem(count):
    return [pl.BlockSpec(memory_space=pltpu.VMEM)] * count


def smem(count):
    return [pl.BlockSpec(memory_space=pltpu.SMEM)] * count


def anywhere(count):
    return [pl.BlockSpec(memory_space=pltpu.HBM)] * count


def params(mebibytes):
    return pltpu.CompilerParams(vmem_limit_bytes=mebibytes * 1024 * 1024)


def local(coefficients, col_map, charge_cell, charge_frac, charge, tile_list):
    slots = coefficients.shape[2]
    sources = lax.axis_size("pw")
    planes = sources
    plane = lax.axis_index("pw").astype(i32)
    first_table, second_table = tables(planes)

    own = tile_list[0]
    other = lax.ppermute(own, "mm", [(0, 1), (1, 0)])
    first = lax.axis_index("mm") == 0
    listed = jnp.concatenate([jnp.where(first, own, other), jnp.where(first, other, own)])
    listed_col = jnp.pad(listed, (0, LANE - 32), constant_values=-1)[:, None]

    sent = pl.pallas_call(
        columns_kernel,
        out_shape=jax.ShapeDtypeStruct((planes, 8, LANE), f32),
        in_specs=smem(1) + anywhere(2),
        out_specs=vmem(1)[0],
        scratch_shapes=[
            pltpu.VMEM((2, slots, N), f32),
            pltpu.VMEM(first_table.shape, bf16),
            pltpu.VMEM((4 * LANE, 2 * N), bf16),
            pltpu.VMEM((4 * LANE, 2 * N), bf16),
            pltpu.SemaphoreType.DMA((5,)),
        ],
        compiler_params=params(60),
        name="columns",
    )(plane[None], coefficients.reshape(2, slots, N), jnp.asarray(first_table))
    recv = lax.all_to_all(sent, "pw", 0, 0, tiled=True)

    blocks = col_map.reshape(sources, slots)
    grid = jnp.pad(blocks, ((0, 0), (0, 4 * LANE - slots)), constant_values=EMPTY)

    pot, slope, offb, offc, col, gb, gc, owner, plan = pl.pallas_call(
        charges_kernel,
        out_shape=(
            jax.ShapeDtypeStruct((N, N), f32),
            pltpu.HBM((32, HALF, N), f32),
            jax.ShapeDtypeStruct((N, LANE), f32),
            jax.ShapeDtypeStruct((32, N), f32),
            jax.ShapeDtypeStruct((LANE, 8), f32),
            jax.ShapeDtypeStruct((4, sources // 2, LANE), f32),
            jax.ShapeDtypeStruct((4, sources // 2, LANE), f32),
            jax.ShapeDtypeStruct((sources // 2, 8, LANE), f32),
            jax.ShapeDtypeStruct((16,), i32),
        ),
        in_specs=smem(4) + vmem(5),
        out_specs=tuple(vmem(1) + anywhere(1) + vmem(6) + smem(1)),
        scratch_shapes=[
            pltpu.VMEM((N, LANE), f32),
            pltpu.VMEM((N, LANE), f32),
            pltpu.VMEM((32, N), f32),
            pltpu.VMEM((32, N), f32),
            pltpu.VMEM((32, HALF, N), f32),
            pltpu.SemaphoreType.DMA((32,)),
        ],
        compiler_params=params(50),
        name="charges",
    )(
        listed,
        charge_cell,
        charge_frac,
        plane[None],
        listed_col,
        charge_cell,
        charge_frac,
        charge[None],
        grid,
    )

    field, push = pl.pallas_call(
        grid_kernel,
        out_shape=(
            jax.ShapeDtypeStruct((2, N, N), f32),
            jax.ShapeDtypeStruct((1, LANE), f32),
        ),
        in_specs=smem(1) + vmem(6) + anywhere(1) + vmem(3),
        out_specs=tuple(anywhere(1) + vmem(1)),
        scratch_shapes=[
            pltpu.VMEM((4, 8 * LANE, 2 * LANE), f32),
            pltpu.VMEM((8 * LANE, TILE_CHUNKS * LANE), bf16),
            pltpu.VMEM((8 * LANE, TILE_CHUNKS * LANE), bf16),
            pltpu.VMEM((2 * LANE, TILE_CHUNKS * LANE), bf16),
            pltpu.VMEM((2 * LANE, TILE_CHUNKS * LANE), bf16),
            pltpu.VMEM((2, 4 * LANE, 2 * N), bf16),
            pltpu.VMEM((4 * LANE, 4 * LANE), bf16),
            pltpu.VMEM((4 * N, 2 * LANE), bf16),
            pltpu.VMEM((2 * LANE, 2 * N), f32),
            pltpu.VMEM((2 * N, 2 * N), f32),
            pltpu.VMEM((N, N), f32),
            pltpu.VMEM((64, N), f32),
            pltpu.VMEM((2, N, N), f32),
            pltpu.VMEM((32, HALF, N), f32),
            pltpu.VMEM((sources // 2, 8, LANE), f32),
            pltpu.SemaphoreType.DMA((2,)),
        ],
        compiler_params=params(50),
        name="grid",
    )(plan, recv, owner, gb, gc, jnp.asarray(second_table), pot, slope, offb, offc, col)

    push = push + lax.ppermute(push, "mm", [(0, 1), (1, 0)])
    terms = lax.all_to_all(
        jnp.broadcast_to(push[None], (sources, 1, LANE)), "pw", 0, 0, tiled=True
    ).reshape(sources, LANE)
    forces = pl.pallas_call(
        spread_kernel,
        out_shape=jax.ShapeDtypeStruct((3, charge.shape[0]), f32),
        in_specs=vmem(1),
        out_specs=vmem(1)[0],
        compiler_params=params(12),
        name="spread",
    )(terms)
    return (field[:, None, None], forces)


def solution(mesh):
    placed = (P(None, "mm", "pw", None), P(), P(), P(), P(), P(("pw", "mm"), None))
    return jax.shard_map(
        local,
        mesh=mesh,
        in_specs=placed,
        out_specs=(P(None, "mm", "pw", None, None), P()),
        check_vma=False,
    )
```

```python
import functools
import math

import jax
import jax.numpy as jnp
import ml_dtypes
import numpy as np
from jax import lax
from jax.experimental import pallas as pl
from jax.experimental.pallas import tpu as pltpu
from jax.sharding import PartitionSpec as P

f32, bf16, i32 = jnp.float32, jnp.bfloat16, jnp.int32
N = 384
HALF = 192
LANE = 128
SPACING = 0.25
SOFTEN = 0.09
VOLUME = SPACING**3
PEAK = 2.0 / math.sqrt(math.pi)
EMPTY = N * N
TILE_CHUNKS = 8
WINDOW = 208
BLOCKS = N // 16
NT = (((1,), (1,)), ((), ()))
TN = (((0,), (0,)), ((), ()))


def split_table(table):
    high = table.astype(np.float32).astype(ml_dtypes.bfloat16)
    low = (table - high.astype(np.float64)).astype(np.float32).astype(ml_dtypes.bfloat16)
    return high, low


def tables(planes):
    index = np.arange(N, dtype=np.int64)
    angle = 2.0 * np.pi / N * ((index[:, None] * index[None, :]) % N).astype(np.float64)
    cos, sin = np.cos(angle), np.sin(angle)
    cz, sz = cos[:planes], sin[:planes]
    first = np.block([[cz, -sz], [sz, cz]])
    first_high, first_low = split_table(first)
    cos_high, cos_low = split_table(cos)
    sin_high, sin_low = split_table(sin)
    return (
        np.concatenate([first_high, first_low], axis=0),
        np.concatenate([cos_high, sin_high, cos_low, sin_low], axis=0),
    )


def mm(a, b, dims=(((1,), (0,)), ((), ()))):
    return lax.dot_general(a, b, dims, preferred_element_type=f32)


def halves(value):
    high = value.astype(bf16)
    low = (value - high.astype(f32)).astype(bf16)
    return high, low


def flip_table(length):
    row = lax.broadcasted_iota(i32, (length, length), 0)
    column = lax.broadcasted_iota(i32, (length, length), 1)
    return jnp.where(row + column == length - 1, 1.0, 0.0).astype(bf16)


def columns_kernel(
    plane_s, coef_in, table_in, out_ref, coef_ref, table_ref, high_ref, low_ref, sems
):
    slots = coef_ref.shape[1]
    half = slots // 2
    copies = []
    for part in range(2):
        for piece in range(2):
            cut = pl.ds(piece * half, half)
            copies.append(
                pltpu.make_async_copy(
                    coef_in.at[part, cut], coef_ref.at[part, cut], sems.at[2 * part + piece]
                )
            )
    copies.append(pltpu.make_async_copy(table_in, table_ref, sems.at[4]))
    for copy in copies:
        copy.start()
    width = high_ref.shape[0]
    planes = out_ref.shape[0]
    high_ref[slots:, :] = jnp.zeros((width - slots, 2 * N), bf16)
    low_ref[slots:, :] = jnp.zeros((width - slots, 2 * N), bf16)
    for part in range(2):
        for piece in range(2):
            copies[2 * part + piece].wait()
            rows = slice(piece * half, (piece + 1) * half)
            high, low = halves(coef_ref[part, rows])
            high_ref[rows, part * N : (part + 1) * N] = high
            low_ref[rows, part * N : (part + 1) * N] = low
    copies[4].wait()
    rows = 2 * planes
    both = mm(table_ref[...], high_ref[...], NT)
    result = both[:rows] + both[rows:] + mm(table_ref[:rows], low_ref[...], NT)

    def put(values):
        for part in range(2):
            for piece in range(4):
                out_ref[:, 4 * part + piece, :] = values[
                    part * planes : (part + 1) * planes, piece * LANE : (piece + 1) * LANE
                ]

    reverse = plane_s[0] >= planes // 2

    @pl.when(jnp.logical_not(reverse))
    def _():
        put(result)

    @pl.when(reverse)
    def _():
        high, low = halves(result)
        flip = flip_table(width)
        put(mm(high, flip) + mm(low, flip))


def wrap(offset):
    shifted = offset + HALF
    shifted = jnp.where(shifted < 0, shifted + N, shifted)
    shifted = jnp.where(shifted >= N, shifted - N, shifted)
    return SPACING * (shifted - HALF)


ERF_NUM = (
    -2.72614225801306e-10,
    2.77068142495902e-08,
    -2.10102402082508e-06,
    -5.69250639462346e-05,
    -7.34990630326855e-04,
    -2.95459980854025e-03,
    -1.60960333262415e-02,
)
ERF_DEN = (
    -1.45660718464996e-05,
    -2.13374055278905e-04,
    -1.68282697438203e-03,
    -7.37332916720468e-03,
    -1.42647390514189e-02,
)


def erf(s):
    s = jnp.minimum(s, 4.0)
    sq = s * s
    num = jnp.full_like(s, ERF_NUM[0])
    for c in ERF_NUM[1:]:
        num = num * sq + c
    den = jnp.full_like(s, ERF_DEN[0])
    for c in ERF_DEN[1:]:
        den = den * sq + c
    return s * num / den


def charges_kernel(
    list_s,
    cell_s,
    frac_s,
    charge_s,
    plane_s,
    list_ref,
    cell_ref,
    frac_ref,
    charge_ref,
    grid_ref,
    pot_ref,
    slope_out,
    offb_ref,
    offc_ref,
    col_ref,
    gb_ref,
    gc_ref,
    owner_ref,
    plan_s,
    uab_ref,
    eab_ref,
    uc_ref,
    ec_ref,
    slope_ref,
    sems,
):
    cells = grid_ref[...]
    pairs = cells.shape[0] // 2
    row = jnp.floor((cells.astype(f32) + 0.5) * (1.0 / N))
    gb = jnp.where(cells < EMPTY, row, -1000.0)
    gc = jnp.where(cells < EMPTY, cells.astype(f32) - N * row, -1000.0)
    high, low = halves(jnp.concatenate([gb[pairs:], gc[pairs:]], axis=0))
    flip = flip_table(cells.shape[1])
    turned = mm(high, flip) + mm(low, flip)
    owned = jnp.where(gb[:pairs] >= 0.0, 1.0, 0.0)
    for piece in range(4):
        cut = slice(piece * LANE, (piece + 1) * LANE)
        owner_ref[:, piece, :] = owned[:, cut]
        owner_ref[:, 4 + piece, :] = owned[:, cut]
    merged_b = jnp.maximum(gb[:pairs], turned[:pairs])
    merged_c = jnp.maximum(gc[:pairs], turned[pairs:])
    found = jnp.int32(0)
    for band in range(3):
        inside = (merged_c >= band * LANE) & (merged_c < (band + 1) * LANE)
        plan_s[8 + found] = jnp.int32(band)
        found = found + jnp.max(jnp.where(inside, 1.0, 0.0)).astype(i32)
    for slot in range(4):
        plan_s[8 + slot] = jnp.where(slot < found, plan_s[8 + slot], 3)
    plan_s[2] = (found + 1) // 2
    alive = merged_b >= 0.0
    block = jnp.where(alive, merged_b * (1.0 / 16.0), 0.0).astype(i32)
    used = jnp.left_shift(jnp.where(alive, 1, 0), block)
    while used.shape[0] > 8:
        used = used[: used.shape[0] // 2] | used[used.shape[0] // 2 :]
    while used.shape[1] > LANE:
        used = used[:, : used.shape[1] // 2] | used[:, used.shape[1] // 2 :]
    for axis, width in ((0, 8), (1, LANE)):
        shift = width // 2
        while shift:
            used = used | pltpu.roll(used, shift, axis)
            shift //= 2
    occupied = jnp.max(used.astype(f32)).astype(i32)
    start = jnp.int32(-1)
    for k in range(BLOCKS):
        outside = sum(1 << ((k + j) % BLOCKS) for j in range(WINDOW // 16, BLOCKS))
        start = jnp.where((occupied & outside) == 0, k, start)
    plan_s[1] = jnp.where(start < 0, 2, 1)
    start = jnp.maximum(start, 0)
    plan_s[3] = start
    shifted = merged_b - (16 * start).astype(f32)
    shifted = jnp.where(shifted < 0.0, shifted + N, shifted)
    shifted = jnp.where(alive, shifted, -1000.0)
    for values, out in ((shifted, gb_ref), (merged_c, gc_ref)):
        for piece in range(4):
            out[piece] = values[:, piece * LANE : (piece + 1) * LANE]

    listed = list_ref[...]
    mask = lax.broadcasted_iota(i32, (LANE, cell_ref.shape[1]), 1) == listed
    center = cell_ref[...].astype(f32) + frac_ref[...]

    def pick(row):
        return jnp.sum(jnp.where(mask, row, 0.0), axis=1, keepdims=True)

    ca, cb, cc = (pick(center[i : i + 1]) for i in range(3))
    strength = pick(charge_ref[...])
    plane = plane_s[0].astype(f32)
    off_a = wrap(plane - ca)
    col_ref[...] = jnp.concatenate(
        [off_a, strength, listed.astype(f32)] + [jnp.zeros((LANE, 5), f32)], axis=1
    )
    off_c = wrap(lax.broadcasted_iota(i32, (32, N), 1).astype(f32) - cc[:32])
    offc_ref[...] = off_c
    sq_c = off_c * off_c
    uc_ref[...] = sq_c
    ec_ref[...] = jnp.exp(-sq_c)

    def across(column):
        return jnp.transpose(jnp.broadcast_to(column, (LANE, LANE)))[:1]

    off_b = wrap(lax.broadcasted_iota(i32, (N, LANE), 0).astype(f32) - across(cb))
    offb_ref[...] = off_b
    row_a = across(off_a)
    uab = off_b * off_b + (row_a * row_a + SOFTEN)
    uab_ref[...] = uab
    eab_ref[...] = PEAK * jnp.exp(-uab)

    def wide(ref, q):
        return jnp.broadcast_to(ref[q : q + 1, :], (8, N))

    def power(q):
        return jnp.broadcast_to(strength[q : q + 1, :], (8, N))

    close = (row_a * row_a < 16.0).astype(f32)
    lane = lax.broadcasted_iota(i32, (1, LANE), 1)
    bits = []
    for half in range(2):
        weight = jnp.where((lane >= 16 * half) & (lane < 16 * half + 16), 1, 0)
        weight = jnp.left_shift(weight, lane & 15).astype(f32)
        bits.append(jnp.sum(close * weight).astype(i32))

    def fix_charge(q):
        base = (q >> 4) * (HALF // 8)
        own = list_s[q]
        center = [cell_s[axis, own].astype(f32) + frac_s[axis, own] for axis in range(3)]
        strong = charge_s[0, own]
        da = wrap(plane - center[0])
        rest = da * da + SOFTEN
        dc = wrap(lax.broadcasted_iota(i32, (8, N), 1).astype(f32) - center[2])
        rest = rest + dc * dc
        row = lax.broadcasted_iota(i32, (8, N), 0).astype(f32)
        first = jnp.floor((center[1] - 16.0) * 0.125).astype(i32)

        def fix(step, _):
            group = first + step
            group = jnp.where(group < 0, group + N // 8, group)
            group = jnp.where(group >= N // 8, group - N // 8, group)
            i = group - base

            @pl.when((i >= 0) & (i < HALF // 8))
            def _():
                r = pl.ds(pl.multiple_of(8 * group, 8), 8)
                db = wrap(row + ((8 * group).astype(f32) - center[1]))
                u = db * db + rest
                k = lax.rsqrt(u)
                full = erf(u * k) * k
                slope = k * k * (PEAK * jnp.exp(-u) - full)
                slope_ref[q, pl.ds(pl.multiple_of(8 * i, 8), 8), :] = slope
                pot_ref[r, :] += strong * (full - k)

            return 0

        lax.fori_loop(0, 6, fix, 0)

    copies = []
    for a in range(0, 16, 2):
        for half in range(2):
            pair = (16 * half + a, 16 * half + a + 1)
            lanes = [(q, wide(uc_ref, q), wide(ec_ref, q), power(q)) for q in pair]
            for i in range(HALF // 8):
                r = slice(half * HALF + 8 * i, half * HALF + 8 * i + 8)
                total = None
                for q, ucq, ecq, strong in lanes:
                    k = lax.rsqrt(uab_ref[r, q : q + 1] + ucq)
                    e = eab_ref[r, q : q + 1] * ecq
                    slope_ref[q, 8 * i : 8 * i + 8, :] = k * k * (e - k)
                    total = strong * k if total is None else total + strong * k
                pot_ref[r, :] = total if a == 0 else pot_ref[r, :] + total
        found = [jnp.right_shift(value, a) & 3 for value in bits]
        found = found[0] + 4 * found[1]

        @pl.when(found > 0)
        def _(a=a, found=found):
            def visit(j, _):
                @pl.when((jnp.right_shift(found, j) & 1) > 0)
                def _():
                    fix_charge(16 * (j >> 1) + a + (j & 1))

                return 0

            lax.fori_loop(0, 4, visit, 0)

        for q in (a, a + 1, 16 + a, 17 + a):
            copy = pltpu.make_async_copy(slope_ref.at[q], slope_out.at[q], sems.at[q])
            copy.start()
            copies.append(copy)
    for copy in copies:
        copy.wait()


def grid_kernel(
    plan_s,
    recv_ref,
    owner_ref,
    gb_ref,
    gc_ref,
    table_ref,
    pot_ref,
    slope_in,
    offb_ref,
    offc_ref,
    col_ref,
    field_out,
    push_ref,
    acc_ref,
    val_a,
    val_b,
    hot_a,
    hot_b,
    tab_ref,
    flow_ref,
    edge_ref,
    pass_ref,
    mid_ref,
    dens_ref,
    sum_ref,
    field_ref,
    slope_ref,
    merged_ref,
    sems,
):
    slope_copy = pltpu.make_async_copy(slope_in, slope_ref, sems.at[1])
    slope_copy.start()
    pairs = merged_ref.shape[0]
    merged_ref[...] = jnp.where(owner_ref[...] > 0.0, recv_ref[:pairs], recv_ref[pairs:])
    def counter(rows):
        return lax.broadcasted_iota(i32, (rows, LANE), 0).astype(f32).astype(bf16)

    iota_b, iota_c = counter(WINDOW), counter(LANE)
    zero = jnp.zeros((WINDOW, LANE), bf16)
    one_c, zero_c = jnp.ones((LANE, LANE), bf16), jnp.zeros((LANE, LANE), bf16)

    def build(tile, group_b, group_c, val_ref, hot_ref):
        for j in range(TILE_CHUNKS):
            pair = jnp.minimum(tile * (TILE_CHUNKS // 4) + j // 4, pairs - 1)
            piece = j % 4
            cut = slice(j * LANE, (j + 1) * LANE)
            gb = gb_ref[piece, pl.ds(pair, 1), :]
            gc = gc_ref[piece, pl.ds(pair, 1), :]
            parts = []
            for part in range(2):
                value = merged_ref[pair, 4 * part + piece : 4 * part + piece + 1, :]
                high, low = halves(value)
                parts.append((part, high))
                parts.append((2 + part, low))
            for h in range(2):
                band = (LANE * plan_s[8 + 2 * group_c + h]).astype(f32)
                hot = iota_c == (gc - band).astype(bf16)
                hot_ref[h * LANE : (h + 1) * LANE, cut] = jnp.where(hot, one_c, zero_c)
            hit = iota_b == (gb - WINDOW * jnp.float32(group_b)).astype(bf16)
            for k, v in parts:
                val_ref[k * WINDOW : (k + 1) * WINDOW, cut] = jnp.where(hit, v, zero)

    acc_ref[0] = jnp.zeros(acc_ref.shape[1:], f32)
    build(0, 0, 0, val_a, hot_a)

    def step(t, _):
        acc_ref[0] += mm(val_a[...], hot_a[...], NT)
        build(2 * t + 1, 0, 0, val_b, hot_b)
        acc_ref[0] += mm(val_b[...], hot_b[...], NT)
        build(2 * t + 2, 0, 0, val_a, hot_a)
        return 0

    steps = 2 * pairs // TILE_CHUNKS
    lax.fori_loop(0, steps, step, 0)

    def rest(combo, _):
        group_b, group_c = combo >> 1, combo & 1

        @pl.when((group_b < plan_s[1]) & (group_c < plan_s[2]))
        def _():
            acc_ref[combo] = jnp.zeros(acc_ref.shape[1:], f32)

            def extra(t, _):
                build(t, group_b, group_c, val_a, hot_a)
                acc_ref[combo] += mm(val_a[...], hot_a[...], NT)
                return 0

            lax.fori_loop(0, 2 * steps, extra, 0)

        return 0

    lax.fori_loop(1, 4, rest, 0)

    def transform(group_b):
        def along(group_c, first):
            for level in range(2):
                for h in range(2):
                    band = jnp.minimum(plan_s[8 + 2 * group_c + h], 2) * LANE
                    base = 2 * level * N
                    cos = table_ref[pl.ds(pl.multiple_of(base + band, LANE), LANE), :]
                    sin = table_ref[pl.ds(pl.multiple_of(base + N + band, LANE), LANE), :]
                    top = slice(h * LANE, (h + 1) * LANE)
                    bottom = slice((2 + h) * LANE, (3 + h) * LANE)
                    tab_ref[level, top, :N] = cos
                    tab_ref[level, top, N:] = sin
                    tab_ref[level, bottom, :N] = -sin
                    tab_ref[level, bottom, N:] = cos
            combo = 2 * group_b + group_c
            for k in range(4):
                top = (k // 2) * WINDOW
                flow_ref[top : top + WINDOW, (k % 2) * 2 * LANE : (k % 2 + 1) * 2 * LANE] = acc_ref[
                    combo, k * WINDOW : (k + 1) * WINDOW, :
                ].astype(bf16)
            half = WINDOW
            both = mm(flow_ref[...], tab_ref[0])
            result = both[:half] + both[half:] + mm(flow_ref[:half], tab_ref[1])
            pass_ref[...] = result if first else pass_ref[...] + result

        along(0, True)

        @pl.when(plan_s[2] > 1)
        def _():
            along(1, False)

        for j in range(WINDOW // 16):
            block = plan_s[3] + (group_b * WINDOW) // 16 + j
            block = jnp.where(block >= BLOCKS, block - BLOCKS, block)
            for k in range(4):
                row = pl.multiple_of(k * N + 16 * block, 16)
                edge_ref[16 * j : 16 * j + 16, k * N : (k + 1) * N] = table_ref[pl.ds(row, 16), :]
        high, low = halves(pass_ref[...])
        result = mm(edge_ref[:, : 2 * N], high, TN) + (
            mm(edge_ref[:, 2 * N :], high, TN) + mm(edge_ref[:, : 2 * N], low, TN)
        )
        mid_ref[...] = result if group_b == 0 else mid_ref[...] + result

    transform(0)

    @pl.when(plan_s[1] > 1)
    def _():
        transform(1)

    def finish(i, _):
        r = pl.ds(pl.multiple_of(8 * i, 8), 8)
        s = pl.ds(pl.multiple_of(N + 8 * i, 8), 8)
        real = mid_ref[r, :N] - mid_ref[s, N:]
        imag = mid_ref[s, :N] + mid_ref[r, N:]
        dens_ref[r, :] = real * real + imag * imag
        pot = pot_ref[r, :]
        field_ref[0, r, :] = pot * real
        field_ref[1, r, :] = pot * imag
        return 0

    lax.fori_loop(0, N // 8, finish, 0, unroll=8)
    field_copy = pltpu.make_async_copy(field_ref, field_out, sems.at[0])
    field_copy.start()
    slope_copy.wait()
    for q in range(32):
        base = (q // 16) * HALF
        plain = [jnp.zeros((8, LANE), f32)] * 3
        scaled = jnp.zeros((8, LANE), f32)
        for i in range(HALF // 8):
            r = slice(base + 8 * i, base + 8 * i + 8)
            w = dens_ref[r, :] * slope_ref[q, 8 * i : 8 * i + 8, :]
            w = [w[:, k * LANE : (k + 1) * LANE] for k in range(3)]
            plain = [p + v for p, v in zip(plain, w)]
            scaled = scaled + (w[0] + w[1] + w[2]) * offb_ref[r, q : q + 1]
        for k in range(3):
            sum_ref[q : q + 1, k * LANE : (k + 1) * LANE] = jnp.sum(plain[k], axis=0, keepdims=True)
        sum_ref[32 + q : 33 + q, :LANE] = jnp.sum(scaled, axis=0, keepdims=True)
    plain = sum_ref[:32, :]
    off_a = col_ref[:32, 0:1]
    scale = col_ref[:32, 1:2] * VOLUME
    push_a = off_a * jnp.sum(plain, axis=1, keepdims=True) * scale
    push_b = jnp.sum(sum_ref[32:, :LANE], axis=1, keepdims=True) * scale
    push_c = jnp.sum(plain * offc_ref[...], axis=1, keepdims=True) * scale
    packed = jnp.concatenate([push_a, push_b, push_c, 0.5 * col_ref[:32, 2:3]], axis=0)
    push_ref[...] = jnp.transpose(jnp.broadcast_to(packed, (LANE, LANE)))[:1]
    field_copy.wait()


def spread_kernel(terms_ref, out_ref):
    terms = terms_ref[...]
    charges = out_ref.shape[1]
    lane = lax.broadcasted_iota(i32, (terms.shape[0], charges), 1).astype(f32)
    totals = [jnp.zeros((terms.shape[0], charges), f32)] * 3
    for q in range(32):
        hot = terms[:, 96 + q : 97 + q] == lane
        for axis in range(3):
            value = terms[:, 32 * axis + q : 32 * axis + q + 1]
            totals[axis] = totals[axis] + jnp.where(hot, value, 0.0)
    for axis in range(3):
        out_ref[axis : axis + 1, :] = jnp.sum(totals[axis], axis=0, keepdims=True)


def vmem(count):
    return [pl.BlockSpec(memory_space=pltpu.VMEM)] * count


def smem(count):
    return [pl.BlockSpec(memory_space=pltpu.SMEM)] * count


def anywhere(count):
    return [pl.BlockSpec(memory_space=pltpu.HBM)] * count


def params(mebibytes):
    return pltpu.CompilerParams(vmem_limit_bytes=mebibytes * 1024 * 1024)


def local(coefficients, col_map, charge_cell, charge_frac, charge, tile_list):
    slots = coefficients.shape[2]
    sources = lax.axis_size("pw")
    planes = sources
    plane = lax.axis_index("pw").astype(i32)
    first_table, second_table = tables(planes)

    sent = pl.pallas_call(
        columns_kernel,
        out_shape=jax.ShapeDtypeStruct((planes, 8, LANE), f32),
        in_specs=smem(1) + anywhere(2),
        out_specs=vmem(1)[0],
        scratch_shapes=[
            pltpu.VMEM((2, slots, N), f32),
            pltpu.VMEM(first_table.shape, bf16),
            pltpu.VMEM((4 * LANE, 2 * N), bf16),
            pltpu.VMEM((4 * LANE, 2 * N), bf16),
            pltpu.SemaphoreType.DMA((5,)),
        ],
        compiler_params=params(54),
        name="columns",
    )(plane[None], coefficients.reshape(2, slots, N), jnp.asarray(first_table))
    own, sent = lax.optimization_barrier((tile_list[0], sent))
    other = lax.ppermute(own, "mm", [(0, 1), (1, 0)])
    first = lax.axis_index("mm") == 0
    listed = jnp.concatenate([jnp.where(first, own, other), jnp.where(first, other, own)])
    listed_col = jnp.pad(listed, (0, LANE - 32), constant_values=-1)[:, None]

    recv = lax.all_to_all(sent, "pw", 0, 0, tiled=True)

    blocks = col_map.reshape(sources, slots)
    grid = jnp.pad(blocks, ((0, 0), (0, 4 * LANE - slots)), constant_values=EMPTY)

    pot, slope, offb, offc, col, gb, gc, owner, plan = pl.pallas_call(
        charges_kernel,
        out_shape=(
            jax.ShapeDtypeStruct((N, N), f32),
            pltpu.HBM((32, HALF, N), f32),
            jax.ShapeDtypeStruct((N, LANE), f32),
            jax.ShapeDtypeStruct((32, N), f32),
            jax.ShapeDtypeStruct((LANE, 8), f32),
            jax.ShapeDtypeStruct((4, sources // 2, LANE), f32),
            jax.ShapeDtypeStruct((4, sources // 2, LANE), f32),
            jax.ShapeDtypeStruct((sources // 2, 8, LANE), f32),
            jax.ShapeDtypeStruct((16,), i32),
        ),
        in_specs=smem(5) + vmem(5),
        out_specs=tuple(vmem(1) + anywhere(1) + vmem(6) + smem(1)),
        scratch_shapes=[
            pltpu.VMEM((N, LANE), f32),
            pltpu.VMEM((N, LANE), f32),
            pltpu.VMEM((32, N), f32),
            pltpu.VMEM((32, N), f32),
            pltpu.VMEM((32, HALF, N), f32),
            pltpu.SemaphoreType.DMA((32,)),
        ],
        compiler_params=params(50),
        name="charges",
    )(
        listed,
        charge_cell,
        charge_frac,
        charge[None],
        plane[None],
        listed_col,
        charge_cell,
        charge_frac,
        charge[None],
        grid,
    )

    field, push = pl.pallas_call(
        grid_kernel,
        out_shape=(
            jax.ShapeDtypeStruct((2, N, N), f32),
            jax.ShapeDtypeStruct((1, LANE), f32),
        ),
        in_specs=smem(1) + vmem(6) + anywhere(1) + vmem(3),
        out_specs=tuple(anywhere(1) + vmem(1)),
        scratch_shapes=[
            pltpu.VMEM((4, 4 * WINDOW, 2 * LANE), f32),
            pltpu.VMEM((4 * WINDOW, TILE_CHUNKS * LANE), bf16),
            pltpu.VMEM((4 * WINDOW, TILE_CHUNKS * LANE), bf16),
            pltpu.VMEM((2 * LANE, TILE_CHUNKS * LANE), bf16),
            pltpu.VMEM((2 * LANE, TILE_CHUNKS * LANE), bf16),
            pltpu.VMEM((2, 4 * LANE, 2 * N), bf16),
            pltpu.VMEM((2 * WINDOW, 4 * LANE), bf16),
            pltpu.VMEM((WINDOW, 4 * N), bf16),
            pltpu.VMEM((WINDOW, 2 * N), f32),
            pltpu.VMEM((2 * N, 2 * N), f32),
            pltpu.VMEM((N, N), f32),
            pltpu.VMEM((64, N), f32),
            pltpu.VMEM((2, N, N), f32),
            pltpu.VMEM((32, HALF, N), f32),
            pltpu.VMEM((sources // 2, 8, LANE), f32),
            pltpu.SemaphoreType.DMA((2,)),
        ],
        compiler_params=params(50),
        name="grid",
    )(plan, recv, owner, gb, gc, jnp.asarray(second_table), pot, slope, offb, offc, col)

    push = push + lax.ppermute(push, "mm", [(0, 1), (1, 0)])
    terms = lax.all_to_all(
        jnp.broadcast_to(push[None], (sources, 1, LANE)), "pw", 0, 0, tiled=True
    ).reshape(sources, LANE)
    forces = pl.pallas_call(
        spread_kernel,
        out_shape=jax.ShapeDtypeStruct((3, charge.shape[0]), f32),
        in_specs=vmem(1),
        out_specs=vmem(1)[0],
        compiler_params=params(12),
        name="spread",
    )(terms)
    return (field[:, None, None], forces)


def solution(mesh):
    placed = (P(None, "mm", "pw", None), P(), P(), P(), P(), P(("pw", "mm"), None))
    return jax.shard_map(
        local,
        mesh=mesh,
        in_specs=placed,
        out_specs=(P(None, "mm", "pw", None, None), P()),
        check_vma=False,
    )
```

```python
import functools
import math

import jax
import jax.numpy as jnp
import ml_dtypes
import numpy as np
from jax import lax
from jax.experimental import pallas as pl
from jax.experimental.pallas import tpu as pltpu
from jax.sharding import PartitionSpec as P

f32, bf16, i32 = jnp.float32, jnp.bfloat16, jnp.int32
N = 384
HALF = 192
LANE = 128
SPACING = 0.25
SOFTEN = 0.09
VOLUME = SPACING**3
PEAK = 2.0 / math.sqrt(math.pi)
EMPTY = N * N
TILE_CHUNKS = 8
WINDOW = 208
BLOCKS = N // 16
NT = (((1,), (1,)), ((), ()))
TN = (((0,), (0,)), ((), ()))


def split_table(table):
    high = table.astype(np.float32).astype(ml_dtypes.bfloat16)
    low = (table - high.astype(np.float64)).astype(np.float32).astype(ml_dtypes.bfloat16)
    return high, low


def tables(planes):
    index = np.arange(N, dtype=np.int64)
    angle = 2.0 * np.pi / N * ((index[:, None] * index[None, :]) % N).astype(np.float64)
    cos, sin = np.cos(angle), np.sin(angle)
    cz, sz = cos[:planes], sin[:planes]
    first = np.block([[cz, -sz], [sz, cz]])
    first_high, first_low = split_table(first)
    cos_high, cos_low = split_table(cos)
    sin_high, sin_low = split_table(sin)
    return (
        np.concatenate([first_high, first_low], axis=0),
        np.concatenate([cos_high, sin_high, cos_low, sin_low], axis=0),
    )


def mm(a, b, dims=(((1,), (0,)), ((), ()))):
    return lax.dot_general(a, b, dims, preferred_element_type=f32)


def halves(value):
    high = value.astype(bf16)
    low = (value - high.astype(f32)).astype(bf16)
    return high, low


def flip_table(length):
    row = lax.broadcasted_iota(i32, (length, length), 0)
    column = lax.broadcasted_iota(i32, (length, length), 1)
    return jnp.where(row + column == length - 1, 1.0, 0.0).astype(bf16)


def columns_kernel(
    plane_s, coef_in, table_in, out_ref, coef_ref, table_ref, high_ref, low_ref, sems
):
    slots = coef_ref.shape[1]
    half = slots // 2
    copies = []
    for part in range(2):
        for piece in range(2):
            cut = pl.ds(piece * half, half)
            copies.append(
                pltpu.make_async_copy(
                    coef_in.at[part, cut], coef_ref.at[part, cut], sems.at[2 * part + piece]
                )
            )
    copies.append(pltpu.make_async_copy(table_in, table_ref, sems.at[4]))
    for copy in copies:
        copy.start()
    width = high_ref.shape[0]
    planes = out_ref.shape[0]
    high_ref[slots:, :] = jnp.zeros((width - slots, 2 * N), bf16)
    low_ref[slots:, :] = jnp.zeros((width - slots, 2 * N), bf16)
    for part in range(2):
        for piece in range(2):
            copies[2 * part + piece].wait()
            rows = slice(piece * half, (piece + 1) * half)
            high, low = halves(coef_ref[part, rows])
            high_ref[rows, part * N : (part + 1) * N] = high
            low_ref[rows, part * N : (part + 1) * N] = low
    copies[4].wait()
    rows = 2 * planes
    both = mm(table_ref[...], high_ref[...], NT)
    result = both[:rows] + both[rows:] + mm(table_ref[:rows], low_ref[...], NT)

    def put(values):
        for part in range(2):
            for piece in range(4):
                out_ref[:, 4 * part + piece, :] = values[
                    part * planes : (part + 1) * planes, piece * LANE : (piece + 1) * LANE
                ]

    reverse = plane_s[0] >= planes // 2

    @pl.when(jnp.logical_not(reverse))
    def _():
        put(result)

    @pl.when(reverse)
    def _():
        high, low = halves(result)
        flip = flip_table(width)
        put(mm(high, flip) + mm(low, flip))


def wrap(offset):
    shifted = offset + HALF
    shifted = jnp.where(shifted < 0, shifted + N, shifted)
    shifted = jnp.where(shifted >= N, shifted - N, shifted)
    return SPACING * (shifted - HALF)


ERF_NUM = (
    -2.72614225801306e-10,
    2.77068142495902e-08,
    -2.10102402082508e-06,
    -5.69250639462346e-05,
    -7.34990630326855e-04,
    -2.95459980854025e-03,
    -1.60960333262415e-02,
)
ERF_DEN = (
    -1.45660718464996e-05,
    -2.13374055278905e-04,
    -1.68282697438203e-03,
    -7.37332916720468e-03,
    -1.42647390514189e-02,
)


def erf(s):
    s = jnp.minimum(s, 4.0)
    sq = s * s
    num = jnp.full_like(s, ERF_NUM[0])
    for c in ERF_NUM[1:]:
        num = num * sq + c
    den = jnp.full_like(s, ERF_DEN[0])
    for c in ERF_DEN[1:]:
        den = den * sq + c
    return s * num / den


def charges_kernel(
    list_s,
    cell_s,
    frac_s,
    charge_s,
    plane_s,
    list_ref,
    cell_ref,
    frac_ref,
    charge_ref,
    grid_ref,
    pot_ref,
    slope_out,
    offb_ref,
    offc_ref,
    col_ref,
    gb_ref,
    gc_ref,
    owner_ref,
    plan_s,
    uab_ref,
    eab_ref,
    uc_ref,
    ec_ref,
    slope_ref,
    sems,
):
    cells = grid_ref[...]
    pairs = cells.shape[0] // 2
    row = jnp.floor((cells.astype(f32) + 0.5) * (1.0 / N))
    gb = jnp.where(cells < EMPTY, row, -1000.0)
    gc = jnp.where(cells < EMPTY, cells.astype(f32) - N * row, -1000.0)
    high, low = halves(jnp.concatenate([gb[pairs:], gc[pairs:]], axis=0))
    flip = flip_table(cells.shape[1])
    turned = mm(high, flip) + mm(low, flip)
    owned = jnp.where(gb[:pairs] >= 0.0, 1.0, 0.0)
    for piece in range(4):
        cut = slice(piece * LANE, (piece + 1) * LANE)
        owner_ref[:, piece, :] = owned[:, cut]
        owner_ref[:, 4 + piece, :] = owned[:, cut]
    merged_b = jnp.maximum(gb[:pairs], turned[:pairs])
    merged_c = jnp.maximum(gc[:pairs], turned[pairs:])
    found = jnp.int32(0)
    for band in range(3):
        inside = (merged_c >= band * LANE) & (merged_c < (band + 1) * LANE)
        plan_s[8 + found] = jnp.int32(band)
        found = found + jnp.max(jnp.where(inside, 1.0, 0.0)).astype(i32)
    for slot in range(4):
        plan_s[8 + slot] = jnp.where(slot < found, plan_s[8 + slot], 3)
    plan_s[2] = (found + 1) // 2
    alive = merged_b >= 0.0
    block = jnp.where(alive, merged_b * (1.0 / 16.0), 0.0).astype(i32)
    used = jnp.left_shift(jnp.where(alive, 1, 0), block)
    while used.shape[0] > 8:
        used = used[: used.shape[0] // 2] | used[used.shape[0] // 2 :]
    while used.shape[1] > LANE:
        used = used[:, : used.shape[1] // 2] | used[:, used.shape[1] // 2 :]
    for axis, width in ((0, 8), (1, LANE)):
        shift = width // 2
        while shift:
            used = used | pltpu.roll(used, shift, axis)
            shift //= 2
    occupied = jnp.max(used.astype(f32)).astype(i32)
    start = jnp.int32(-1)
    for k in range(BLOCKS):
        outside = sum(1 << ((k + j) % BLOCKS) for j in range(WINDOW // 16, BLOCKS))
        start = jnp.where((occupied & outside) == 0, k, start)
    plan_s[1] = jnp.where(start < 0, 2, 1)
    start = jnp.maximum(start, 0)
    plan_s[3] = start
    shifted = merged_b - (16 * start).astype(f32)
    shifted = jnp.where(shifted < 0.0, shifted + N, shifted)
    shifted = jnp.where(alive, shifted, -1000.0)
    for values, out in ((shifted, gb_ref), (merged_c, gc_ref)):
        for piece in range(4):
            out[piece] = values[:, piece * LANE : (piece + 1) * LANE]

    listed = list_ref[...]
    mask = lax.broadcasted_iota(i32, (LANE, cell_ref.shape[1]), 1) == listed
    center = cell_ref[...].astype(f32) + frac_ref[...]

    def pick(row):
        return jnp.sum(jnp.where(mask, row, 0.0), axis=1, keepdims=True)

    ca, cb, cc = (pick(center[i : i + 1]) for i in range(3))
    strength = pick(charge_ref[...])
    plane = plane_s[0].astype(f32)
    off_a = wrap(plane - ca)
    col_ref[...] = jnp.concatenate(
        [off_a, strength, listed.astype(f32)] + [jnp.zeros((LANE, 5), f32)], axis=1
    )
    off_c = wrap(lax.broadcasted_iota(i32, (32, N), 1).astype(f32) - cc[:32])
    offc_ref[...] = off_c
    sq_c = off_c * off_c
    uc_ref[...] = sq_c
    ec_ref[...] = jnp.exp(-sq_c)

    def across(column):
        return jnp.transpose(jnp.broadcast_to(column, (LANE, LANE)))[:1]

    off_b = wrap(lax.broadcasted_iota(i32, (N, LANE), 0).astype(f32) - across(cb))
    offb_ref[...] = off_b
    row_a = across(off_a)
    uab = off_b * off_b + (row_a * row_a + SOFTEN)
    uab_ref[...] = uab
    eab_ref[...] = PEAK * jnp.exp(-uab)

    def wide(ref, q):
        return jnp.broadcast_to(ref[q : q + 1, :], (8, N))

    def power(q):
        return jnp.broadcast_to(strength[q : q + 1, :], (8, N))

    close = (row_a * row_a < 16.0).astype(f32)
    lane = lax.broadcasted_iota(i32, (1, LANE), 1)
    bits = []
    for half in range(2):
        weight = jnp.where((lane >= 16 * half) & (lane < 16 * half + 16), 1, 0)
        weight = jnp.left_shift(weight, lane & 15).astype(f32)
        bits.append(jnp.sum(close * weight).astype(i32))

    def fix_charge(q):
        base = (q >> 4) * (HALF // 8)
        own = list_s[q]
        center = [cell_s[axis, own].astype(f32) + frac_s[axis, own] for axis in range(3)]
        strong = charge_s[0, own]
        da = wrap(plane - center[0])
        rest = da * da + SOFTEN
        dc = wrap(lax.broadcasted_iota(i32, (8, N), 1).astype(f32) - center[2])
        rest = rest + dc * dc
        row = lax.broadcasted_iota(i32, (8, N), 0).astype(f32)
        first = jnp.floor((center[1] - 16.0) * 0.125).astype(i32)

        def fix(step, _):
            group = first + step
            group = jnp.where(group < 0, group + N // 8, group)
            group = jnp.where(group >= N // 8, group - N // 8, group)
            i = group - base

            @pl.when((i >= 0) & (i < HALF // 8))
            def _():
                r = pl.ds(pl.multiple_of(8 * group, 8), 8)
                db = wrap(row + ((8 * group).astype(f32) - center[1]))
                u = db * db + rest
                k = lax.rsqrt(u)
                full = erf(u * k) * k
                slope = k * k * (PEAK * jnp.exp(-u) - full)
                slope_ref[q, pl.ds(pl.multiple_of(8 * i, 8), 8), :] = slope
                pot_ref[r, :] += strong * (full - k)

            return 0

        lax.fori_loop(0, 6, fix, 0)

    copies = []
    for a in range(0, 16, 2):
        for half in range(2):
            pair = (16 * half + a, 16 * half + a + 1)
            lanes = [(q, wide(uc_ref, q), wide(ec_ref, q), power(q)) for q in pair]
            for i in range(HALF // 8):
                r = slice(half * HALF + 8 * i, half * HALF + 8 * i + 8)
                total = None
                for q, ucq, ecq, strong in lanes:
                    k = lax.rsqrt(uab_ref[r, q : q + 1] + ucq)
                    e = eab_ref[r, q : q + 1] * ecq
                    slope_ref[q, 8 * i : 8 * i + 8, :] = k * k * (e - k)
                    total = strong * k if total is None else total + strong * k
                pot_ref[r, :] = total if a == 0 else pot_ref[r, :] + total
        found = [jnp.right_shift(value, a) & 3 for value in bits]
        found = found[0] + 4 * found[1]

        @pl.when(found > 0)
        def _(a=a, found=found):
            def visit(j, _):
                @pl.when((jnp.right_shift(found, j) & 1) > 0)
                def _():
                    fix_charge(16 * (j >> 1) + a + (j & 1))

                return 0

            lax.fori_loop(0, 4, visit, 0)

        for q in (a, a + 1, 16 + a, 17 + a):
            copy = pltpu.make_async_copy(slope_ref.at[q], slope_out.at[q], sems.at[q])
            copy.start()
            copies.append(copy)
    for copy in copies:
        copy.wait()


def grid_kernel(
    plan_s,
    recv_ref,
    owner_ref,
    gb_ref,
    gc_ref,
    table_ref,
    pot_ref,
    slope_in,
    offb_ref,
    offc_ref,
    col_ref,
    field_out,
    push_ref,
    acc_ref,
    tab_ref,
    flow_ref,
    edge_ref,
    pass_ref,
    mid_ref,
    dens_ref,
    sum_ref,
    field_ref,
    slope_ref,
    merged_ref,
    sems,
):
    slope_copy = pltpu.make_async_copy(slope_in, slope_ref, sems.at[1])
    slope_copy.start()
    pairs = merged_ref.shape[0]
    merged_ref[...] = jnp.where(owner_ref[...] > 0.0, recv_ref[:pairs], recv_ref[pairs:])
    def counter(rows):
        return lax.broadcasted_iota(i32, (rows, LANE), 0).astype(f32).astype(bf16)

    iota_b, iota_c = counter(WINDOW), counter(LANE)
    zero = jnp.zeros((WINDOW, LANE), bf16)
    one_c, zero_c = jnp.ones((LANE, LANE), bf16), jnp.zeros((LANE, LANE), bf16)

    def product(tile, group_b, group_c):
        columns, weights = [], []
        for j in range(TILE_CHUNKS):
            pair = tile * (TILE_CHUNKS // 4) + j // 4
            piece = j % 4
            gb = gb_ref[piece, pl.ds(pair, 1), :]
            gc = gc_ref[piece, pl.ds(pair, 1), :]
            parts = [None] * 4
            for part in range(2):
                value = merged_ref[pair, 4 * part + piece : 4 * part + piece + 1, :]
                parts[part], parts[2 + part] = halves(value)
            hots = []
            for h in range(2):
                band = (LANE * plan_s[8 + 2 * group_c + h]).astype(f32)
                hots.append(jnp.where(iota_c == (gc - band).astype(bf16), one_c, zero_c))
            weights.append(jnp.concatenate(hots, axis=0))
            hit = iota_b == (gb - WINDOW * jnp.asarray(group_b).astype(f32)).astype(bf16)
            columns.append(jnp.concatenate([jnp.where(hit, v, zero) for v in parts], axis=0))
        return mm(jnp.concatenate(columns, axis=1), jnp.concatenate(weights, axis=1), NT)

    acc_ref[0] = jnp.zeros(acc_ref.shape[1:], f32)
    def step(t, _):
        acc_ref[0] += product(2 * t, 0, 0)
        acc_ref[0] += product(2 * t + 1, 0, 0)
        return 0

    steps = 2 * pairs // TILE_CHUNKS
    lax.fori_loop(0, steps, step, 0)

    def rest(combo, _):
        group_b, group_c = combo >> 1, combo & 1

        @pl.when((group_b < plan_s[1]) & (group_c < plan_s[2]))
        def _():
            acc_ref[combo] = jnp.zeros(acc_ref.shape[1:], f32)

            def extra(t, _):
                acc_ref[combo] += product(t, group_b, group_c)
                return 0

            lax.fori_loop(0, 2 * steps, extra, 0)

        return 0

    lax.fori_loop(1, 4, rest, 0)

    def transform(group_b):
        def along(group_c, first):
            for level in range(2):
                for h in range(2):
                    band = jnp.minimum(plan_s[8 + 2 * group_c + h], 2) * LANE
                    base = 2 * level * N
                    cos = table_ref[pl.ds(pl.multiple_of(base + band, LANE), LANE), :]
                    sin = table_ref[pl.ds(pl.multiple_of(base + N + band, LANE), LANE), :]
                    top = slice(h * LANE, (h + 1) * LANE)
                    bottom = slice((2 + h) * LANE, (3 + h) * LANE)
                    tab_ref[level, top, :N] = cos
                    tab_ref[level, top, N:] = sin
                    tab_ref[level, bottom, :N] = -sin
                    tab_ref[level, bottom, N:] = cos
            combo = 2 * group_b + group_c
            for k in range(4):
                top = (k // 2) * WINDOW
                flow_ref[top : top + WINDOW, (k % 2) * 2 * LANE : (k % 2 + 1) * 2 * LANE] = acc_ref[
                    combo, k * WINDOW : (k + 1) * WINDOW, :
                ].astype(bf16)
            half = WINDOW
            both = mm(flow_ref[...], tab_ref[0])
            result = both[:half] + both[half:] + mm(flow_ref[:half], tab_ref[1])
            pass_ref[...] = result if first else pass_ref[...] + result

        along(0, True)

        @pl.when(plan_s[2] > 1)
        def _():
            along(1, False)

        for j in range(WINDOW // 16):
            block = plan_s[3] + (group_b * WINDOW) // 16 + j
            block = jnp.where(block >= BLOCKS, block - BLOCKS, block)
            for k in range(4):
                row = pl.multiple_of(k * N + 16 * block, 16)
                edge_ref[16 * j : 16 * j + 16, k * N : (k + 1) * N] = table_ref[pl.ds(row, 16), :]
        high, low = halves(pass_ref[...])
        result = mm(edge_ref[:, : 2 * N], high, TN) + (
            mm(edge_ref[:, 2 * N :], high, TN) + mm(edge_ref[:, : 2 * N], low, TN)
        )
        mid_ref[...] = result if group_b == 0 else mid_ref[...] + result

    transform(0)

    @pl.when(plan_s[1] > 1)
    def _():
        transform(1)

    def finish(i, _):
        r = pl.ds(pl.multiple_of(8 * i, 8), 8)
        s = pl.ds(pl.multiple_of(N + 8 * i, 8), 8)
        real = mid_ref[r, :N] - mid_ref[s, N:]
        imag = mid_ref[s, :N] + mid_ref[r, N:]
        dens_ref[r, :] = real * real + imag * imag
        pot = pot_ref[r, :]
        field_ref[0, r, :] = pot * real
        field_ref[1, r, :] = pot * imag
        return 0

    lax.fori_loop(0, N // 8, finish, 0, unroll=8)
    field_copy = pltpu.make_async_copy(field_ref, field_out, sems.at[0])
    field_copy.start()
    slope_copy.wait()
    for q in range(32):
        base = (q // 16) * HALF
        plain = [jnp.zeros((8, LANE), f32)] * 3
        scaled = jnp.zeros((8, LANE), f32)
        for i in range(HALF // 8):
            r = slice(base + 8 * i, base + 8 * i + 8)
            w = dens_ref[r, :] * slope_ref[q, 8 * i : 8 * i + 8, :]
            w = [w[:, k * LANE : (k + 1) * LANE] for k in range(3)]
            plain = [p + v for p, v in zip(plain, w)]
            scaled = scaled + (w[0] + w[1] + w[2]) * offb_ref[r, q : q + 1]
        for k in range(3):
            sum_ref[q : q + 1, k * LANE : (k + 1) * LANE] = jnp.sum(plain[k], axis=0, keepdims=True)
        sum_ref[32 + q : 33 + q, :LANE] = jnp.sum(scaled, axis=0, keepdims=True)
    plain = sum_ref[:32, :]
    off_a = col_ref[:32, 0:1]
    scale = col_ref[:32, 1:2] * VOLUME
    push_a = off_a * jnp.sum(plain, axis=1, keepdims=True) * scale
    push_b = jnp.sum(sum_ref[32:, :LANE], axis=1, keepdims=True) * scale
    push_c = jnp.sum(plain * offc_ref[...], axis=1, keepdims=True) * scale
    packed = jnp.concatenate([push_a, push_b, push_c, 0.5 * col_ref[:32, 2:3]], axis=0)
    push_ref[...] = jnp.transpose(jnp.broadcast_to(packed, (LANE, LANE)))[:1]
    field_copy.wait()


def spread_kernel(terms_ref, out_ref):
    terms = terms_ref[...]
    charges = out_ref.shape[1]
    lane = lax.broadcasted_iota(i32, (terms.shape[0], charges), 1).astype(f32)
    totals = [jnp.zeros((terms.shape[0], charges), f32)] * 3
    for q in range(32):
        hot = terms[:, 96 + q : 97 + q] == lane
        for axis in range(3):
            value = terms[:, 32 * axis + q : 32 * axis + q + 1]
            totals[axis] = totals[axis] + jnp.where(hot, value, 0.0)
    for axis in range(3):
        out_ref[axis : axis + 1, :] = jnp.sum(totals[axis], axis=0, keepdims=True)


def vmem(count):
    return [pl.BlockSpec(memory_space=pltpu.VMEM)] * count


def smem(count):
    return [pl.BlockSpec(memory_space=pltpu.SMEM)] * count


def anywhere(count):
    return [pl.BlockSpec(memory_space=pltpu.HBM)] * count


def params(mebibytes):
    return pltpu.CompilerParams(vmem_limit_bytes=mebibytes * 1024 * 1024)


def local(coefficients, col_map, charge_cell, charge_frac, charge, tile_list):
    slots = coefficients.shape[2]
    sources = lax.axis_size("pw")
    planes = sources
    plane = lax.axis_index("pw").astype(i32)
    first_table, second_table = tables(planes)

    sent = pl.pallas_call(
        columns_kernel,
        out_shape=jax.ShapeDtypeStruct((planes, 8, LANE), f32),
        in_specs=smem(1) + anywhere(2),
        out_specs=vmem(1)[0],
        scratch_shapes=[
            pltpu.VMEM((2, slots, N), f32),
            pltpu.VMEM(first_table.shape, bf16),
            pltpu.VMEM((4 * LANE, 2 * N), bf16),
            pltpu.VMEM((4 * LANE, 2 * N), bf16),
            pltpu.SemaphoreType.DMA((5,)),
        ],
        compiler_params=params(54),
        name="columns",
    )(plane[None], coefficients.reshape(2, slots, N), jnp.asarray(first_table))
    own, sent = lax.optimization_barrier((tile_list[0], sent))
    other = lax.ppermute(own, "mm", [(0, 1), (1, 0)])
    first = lax.axis_index("mm") == 0
    listed = jnp.concatenate([jnp.where(first, own, other), jnp.where(first, other, own)])
    listed_col = jnp.pad(listed, (0, LANE - 32), constant_values=-1)[:, None]

    recv = lax.all_to_all(sent, "pw", 0, 0, tiled=True)

    blocks = col_map.reshape(sources, slots)
    grid = jnp.pad(blocks, ((0, 0), (0, 4 * LANE - slots)), constant_values=EMPTY)

    pot, slope, offb, offc, col, gb, gc, owner, plan = pl.pallas_call(
        charges_kernel,
        out_shape=(
            jax.ShapeDtypeStruct((N, N), f32),
            pltpu.HBM((32, HALF, N), f32),
            jax.ShapeDtypeStruct((N, LANE), f32),
            jax.ShapeDtypeStruct((32, N), f32),
            jax.ShapeDtypeStruct((LANE, 8), f32),
            jax.ShapeDtypeStruct((4, sources // 2, LANE), f32),
            jax.ShapeDtypeStruct((4, sources // 2, LANE), f32),
            jax.ShapeDtypeStruct((sources // 2, 8, LANE), f32),
            jax.ShapeDtypeStruct((16,), i32),
        ),
        in_specs=smem(5) + vmem(5),
        out_specs=tuple(vmem(1) + anywhere(1) + vmem(6) + smem(1)),
        scratch_shapes=[
            pltpu.VMEM((N, LANE), f32),
            pltpu.VMEM((N, LANE), f32),
            pltpu.VMEM((32, N), f32),
            pltpu.VMEM((32, N), f32),
            pltpu.VMEM((32, HALF, N), f32),
            pltpu.SemaphoreType.DMA((32,)),
        ],
        compiler_params=params(50),
        name="charges",
    )(
        listed,
        charge_cell,
        charge_frac,
        charge[None],
        plane[None],
        listed_col,
        charge_cell,
        charge_frac,
        charge[None],
        grid,
    )

    field, push = pl.pallas_call(
        grid_kernel,
        out_shape=(
            jax.ShapeDtypeStruct((2, N, N), f32),
            jax.ShapeDtypeStruct((1, LANE), f32),
        ),
        in_specs=smem(1) + vmem(6) + anywhere(1) + vmem(3),
        out_specs=tuple(anywhere(1) + vmem(1)),
        scratch_shapes=[
            pltpu.VMEM((4, 4 * WINDOW, 2 * LANE), f32),
            pltpu.VMEM((2, 4 * LANE, 2 * N), bf16),
            pltpu.VMEM((2 * WINDOW, 4 * LANE), bf16),
            pltpu.VMEM((WINDOW, 4 * N), bf16),
            pltpu.VMEM((WINDOW, 2 * N), f32),
            pltpu.VMEM((2 * N, 2 * N), f32),
            pltpu.VMEM((N, N), f32),
            pltpu.VMEM((64, N), f32),
            pltpu.VMEM((2, N, N), f32),
            pltpu.VMEM((32, HALF, N), f32),
            pltpu.VMEM((sources // 2, 8, LANE), f32),
            pltpu.SemaphoreType.DMA((2,)),
        ],
        compiler_params=params(50),
        name="grid",
    )(plan, recv, owner, gb, gc, jnp.asarray(second_table), pot, slope, offb, offc, col)

    push = push + lax.ppermute(push, "mm", [(0, 1), (1, 0)])
    terms = lax.all_to_all(
        jnp.broadcast_to(push[None], (sources, 1, LANE)), "pw", 0, 0, tiled=True
    ).reshape(sources, LANE)
    forces = pl.pallas_call(
        spread_kernel,
        out_shape=jax.ShapeDtypeStruct((3, charge.shape[0]), f32),
        in_specs=vmem(1),
        out_specs=vmem(1)[0],
        compiler_params=params(12),
        name="spread",
    )(terms)
    return (field[:, None, None], forces)


def solution(mesh):
    placed = (P(None, "mm", "pw", None), P(), P(), P(), P(), P(("pw", "mm"), None))
    return jax.shard_map(
        local,
        mesh=mesh,
        in_specs=placed,
        out_specs=(P(None, "mm", "pw", None, None), P()),
        check_vma=False,
    )
```

```python
import functools
import math

import jax
import jax.numpy as jnp
import ml_dtypes
import numpy as np
from jax import lax
from jax.experimental import pallas as pl
from jax.experimental.pallas import tpu as pltpu
from jax.sharding import PartitionSpec as P

f32, bf16, i32 = jnp.float32, jnp.bfloat16, jnp.int32
N = 384
HALF = 192
LANE = 128
SPACING = 0.25
SOFTEN = 0.09
VOLUME = SPACING**3
PEAK = 2.0 / math.sqrt(math.pi)
EMPTY = N * N
TILE_CHUNKS = 32
WINDOW = 208
BLOCKS = N // 16
NT = (((1,), (1,)), ((), ()))
TN = (((0,), (0,)), ((), ()))


def split_table(table):
    high = table.astype(np.float32).astype(ml_dtypes.bfloat16)
    low = (table - high.astype(np.float64)).astype(np.float32).astype(ml_dtypes.bfloat16)
    return high, low


def tables(planes):
    index = np.arange(N, dtype=np.int64)
    angle = 2.0 * np.pi / N * ((index[:, None] * index[None, :]) % N).astype(np.float64)
    cos, sin = np.cos(angle), np.sin(angle)
    cz, sz = cos[:planes], sin[:planes]
    first = np.block([[cz, -sz], [sz, cz]])
    first_high, first_low = split_table(first)
    cos_high, cos_low = split_table(cos)
    sin_high, sin_low = split_table(sin)
    return (
        np.concatenate([first_high, first_low], axis=0),
        np.concatenate([cos_high, sin_high, cos_low, sin_low], axis=0),
    )


def mm(a, b, dims=(((1,), (0,)), ((), ()))):
    return lax.dot_general(a, b, dims, preferred_element_type=f32)


def halves(value):
    high = value.astype(bf16)
    low = (value - high.astype(f32)).astype(bf16)
    return high, low


def flip_table(length):
    row = lax.broadcasted_iota(i32, (length, length), 0)
    column = lax.broadcasted_iota(i32, (length, length), 1)
    return jnp.where(row + column == length - 1, 1.0, 0.0).astype(bf16)


def columns_kernel(
    plane_s, coef_in, table_in, out_ref, coef_ref, table_ref, high_ref, low_ref, sems
):
    slots = coef_ref.shape[1]
    half = slots // 2
    copies = []
    for part in range(2):
        for piece in range(2):
            cut = pl.ds(piece * half, half)
            copies.append(
                pltpu.make_async_copy(
                    coef_in.at[part, cut], coef_ref.at[part, cut], sems.at[2 * part + piece]
                )
            )
    copies.append(pltpu.make_async_copy(table_in, table_ref, sems.at[4]))
    for copy in copies:
        copy.start()
    width = high_ref.shape[0]
    planes = out_ref.shape[0]
    high_ref[slots:, :] = jnp.zeros((width - slots, 2 * N), bf16)
    low_ref[slots:, :] = jnp.zeros((width - slots, 2 * N), bf16)
    for part in range(2):
        for piece in range(2):
            copies[2 * part + piece].wait()
            rows = slice(piece * half, (piece + 1) * half)
            high, low = halves(coef_ref[part, rows])
            high_ref[rows, part * N : (part + 1) * N] = high
            low_ref[rows, part * N : (part + 1) * N] = low
    copies[4].wait()
    rows = 2 * planes
    both = mm(table_ref[...], high_ref[...], NT)
    result = both[:rows] + both[rows:] + mm(table_ref[:rows], low_ref[...], NT)

    def put(values):
        for part in range(2):
            for piece in range(4):
                out_ref[:, 4 * part + piece, :] = values[
                    part * planes : (part + 1) * planes, piece * LANE : (piece + 1) * LANE
                ]

    reverse = plane_s[0] >= planes // 2

    @pl.when(jnp.logical_not(reverse))
    def _():
        put(result)

    @pl.when(reverse)
    def _():
        high, low = halves(result)
        flip = flip_table(width)
        put(mm(high, flip) + mm(low, flip))


def wrap(offset):
    shifted = offset + HALF
    shifted = jnp.where(shifted < 0, shifted + N, shifted)
    shifted = jnp.where(shifted >= N, shifted - N, shifted)
    return SPACING * (shifted - HALF)


ERF_NUM = (
    -2.72614225801306e-10,
    2.77068142495902e-08,
    -2.10102402082508e-06,
    -5.69250639462346e-05,
    -7.34990630326855e-04,
    -2.95459980854025e-03,
    -1.60960333262415e-02,
)
ERF_DEN = (
    -1.45660718464996e-05,
    -2.13374055278905e-04,
    -1.68282697438203e-03,
    -7.37332916720468e-03,
    -1.42647390514189e-02,
)


def erf(s):
    s = jnp.minimum(s, 4.0)
    sq = s * s
    num = jnp.full_like(s, ERF_NUM[0])
    for c in ERF_NUM[1:]:
        num = num * sq + c
    den = jnp.full_like(s, ERF_DEN[0])
    for c in ERF_DEN[1:]:
        den = den * sq + c
    return s * num / den


def sort_cells(grid_ref, gb_ref, gc_ref, owner_ref, plan_s):
    cells = grid_ref[...]
    pairs = cells.shape[0] // 2
    row = jnp.floor((cells.astype(f32) + 0.5) * (1.0 / N))
    gb = jnp.where(cells < EMPTY, row, -1000.0)
    gc = jnp.where(cells < EMPTY, cells.astype(f32) - N * row, -1000.0)
    high, low = halves(jnp.concatenate([gb[pairs:], gc[pairs:]], axis=0))
    flip = flip_table(cells.shape[1])
    turned = mm(high, flip) + mm(low, flip)
    owned = jnp.where(gb[:pairs] >= 0.0, 1.0, 0.0)
    for piece in range(4):
        cut = slice(piece * LANE, (piece + 1) * LANE)
        owner_ref[:, piece, :] = owned[:, cut]
        owner_ref[:, 4 + piece, :] = owned[:, cut]
    merged_b = jnp.maximum(gb[:pairs], turned[:pairs])
    merged_c = jnp.maximum(gc[:pairs], turned[pairs:])
    found = jnp.int32(0)
    for band in range(3):
        inside = (merged_c >= band * LANE) & (merged_c < (band + 1) * LANE)
        plan_s[8 + found] = jnp.int32(band)
        found = found + jnp.max(jnp.where(inside, 1.0, 0.0)).astype(i32)
    for slot in range(4):
        plan_s[8 + slot] = jnp.where(slot < found, plan_s[8 + slot], 3)
    plan_s[2] = (found + 1) // 2
    alive = merged_b >= 0.0
    block = jnp.where(alive, merged_b * (1.0 / 16.0), 0.0).astype(i32)
    used = jnp.left_shift(jnp.where(alive, 1, 0), block)
    while used.shape[0] > 8:
        used = used[: used.shape[0] // 2] | used[used.shape[0] // 2 :]
    while used.shape[1] > LANE:
        used = used[:, : used.shape[1] // 2] | used[:, used.shape[1] // 2 :]
    for axis, width in ((0, 8), (1, LANE)):
        shift = width // 2
        while shift:
            used = used | pltpu.roll(used, shift, axis)
            shift //= 2
    occupied = jnp.max(used.astype(f32)).astype(i32)
    start = jnp.int32(-1)
    for k in range(BLOCKS):
        outside = sum(1 << ((k + j) % BLOCKS) for j in range(WINDOW // 16, BLOCKS))
        start = jnp.where((occupied & outside) == 0, k, start)
    plan_s[1] = jnp.where(start < 0, 2, 1)
    start = jnp.maximum(start, 0)
    plan_s[3] = start
    shifted = merged_b - (16 * start).astype(f32)
    shifted = jnp.where(shifted < 0.0, shifted + N, shifted)
    shifted = jnp.where(alive, shifted, -1000.0)
    for values, out in ((shifted, gb_ref), (merged_c, gc_ref)):
        for piece in range(4):
            out[piece] = values[:, piece * LANE : (piece + 1) * LANE]


def charges_kernel(
    list_s,
    cell_s,
    frac_s,
    charge_s,
    place_s,
    list_ref,
    cell_ref,
    frac_ref,
    charge_ref,
    *refs,
):
    refs = list(refs)
    grid_ref = refs.pop(0) if len(refs) > 11 else None
    pot_ref, slope_out, offb_ref, offc_ref, col_ref = refs[:5]
    if grid_ref is not None:
        sort_cells(grid_ref, *refs[5:9])
    uab_ref, eab_ref, uc_ref, ec_ref, slope_ref, sems = refs[-6:]
    plane = place_s[0].astype(f32)
    tile = place_s[1]
    start_row = (tile * HALF).astype(f32)
    listed = list_ref[...]
    mask = lax.broadcasted_iota(i32, (LANE, cell_ref.shape[1]), 1) == listed
    center = cell_ref[...].astype(f32) + frac_ref[...]

    def pick(row):
        return jnp.sum(jnp.where(mask, row, 0.0), axis=1, keepdims=True)

    ca, cb, cc = (pick(center[i : i + 1]) for i in range(3))
    strength = pick(charge_ref[...])
    off_a = wrap(plane - ca)
    col_ref[...] = jnp.concatenate(
        [off_a, strength, listed.astype(f32)] + [jnp.zeros((LANE, 5), f32)], axis=1
    )
    off_c = wrap(lax.broadcasted_iota(i32, (16, N), 1).astype(f32) - cc[:16])
    offc_ref[...] = off_c
    sq_c = off_c * off_c
    uc_ref[...] = sq_c
    ec_ref[...] = jnp.exp(-sq_c)

    def across(column):
        return jnp.transpose(jnp.broadcast_to(column, (LANE, LANE)))[:1]

    row = lax.broadcasted_iota(i32, (HALF, LANE), 0).astype(f32) + start_row
    off_b = wrap(row - across(cb))
    offb_ref[...] = off_b
    row_a = across(off_a)
    uab = off_b * off_b + (row_a * row_a + SOFTEN)
    uab_ref[...] = uab
    eab_ref[...] = PEAK * jnp.exp(-uab)

    def wide(ref, q):
        return jnp.broadcast_to(ref[q : q + 1, :], (8, N))

    def power(q):
        return jnp.broadcast_to(strength[q : q + 1, :], (8, N))

    close = (row_a * row_a < 16.0).astype(f32)
    lane = lax.broadcasted_iota(i32, (1, LANE), 1)
    weight = jnp.left_shift(jnp.where(lane < 16, 1, 0), lane & 15).astype(f32)
    bits = jnp.sum(close * weight).astype(i32)

    def wide(ref, q):
        return jnp.broadcast_to(ref[q : q + 1, :], (8, N))

    def power(q):
        return jnp.broadcast_to(strength[q : q + 1, :], (8, N))

    def fix_charge(q):
        own = list_s[q]
        center = [cell_s[axis, own].astype(f32) + frac_s[axis, own] for axis in range(3)]
        strong = charge_s[0, own]
        da = wrap(plane - center[0])
        rest = da * da + SOFTEN
        dc = wrap(lax.broadcasted_iota(i32, (8, N), 1).astype(f32) - center[2])
        rest = rest + dc * dc
        row = lax.broadcasted_iota(i32, (8, N), 0).astype(f32)
        first = jnp.floor((center[1] - 16.0) * 0.125).astype(i32)

        def fix(step, _):
            group = first + step
            group = jnp.where(group < 0, group + N // 8, group)
            group = jnp.where(group >= N // 8, group - N // 8, group)
            i = group - tile * (HALF // 8)

            @pl.when((i >= 0) & (i < HALF // 8))
            def _():
                r = pl.ds(pl.multiple_of(8 * i, 8), 8)
                db = wrap(row + ((8 * group).astype(f32) - center[1]))
                u = db * db + rest
                k = lax.rsqrt(u)
                full = erf(u * k) * k
                slope = k * k * (PEAK * jnp.exp(-u) - full)
                slope_ref[q, r, :] = slope
                pot_ref[r, :] += strong * (full - k)

            return 0

        lax.fori_loop(0, 6, fix, 0)

    copies = []
    for a in range(0, 16, 4):
        lanes = [(q, wide(uc_ref, q), wide(ec_ref, q), power(q)) for q in range(a, a + 4)]
        for i in range(HALF // 8):
            r = slice(8 * i, 8 * i + 8)
            total = None if a == 0 else pot_ref[r, :]
            for q, ucq, ecq, strong in lanes:
                k = lax.rsqrt(uab_ref[r, q : q + 1] + ucq)
                e = eab_ref[r, q : q + 1] * ecq
                slope_ref[q, r, :] = k * k * (e - k)
                total = strong * k if total is None else total + strong * k
            pot_ref[r, :] = total
        found = jnp.right_shift(bits, a) & 15

        @pl.when(found > 0)
        def _(a=a, found=found):
            def visit(j, _):
                @pl.when((jnp.right_shift(found, j) & 1) > 0)
                def _():
                    fix_charge(a + j)

                return 0

            lax.fori_loop(0, 4, visit, 0)

        for q in range(a, a + 4):
            copy = pltpu.make_async_copy(slope_ref.at[q], slope_out.at[q], sems.at[q])
            copy.start()
            copies.append(copy)
    for copy in copies:
        copy.wait()


def grid_kernel(
    plan_s,
    place_s,
    recv_ref,
    owner_ref,
    gb_ref,
    gc_ref,
    table_ref,
    own_pot_ref,
    own_slope_in,
    own_offb_ref,
    own_offc_ref,
    own_col_ref,
    other_pot_ref,
    other_slope_in,
    other_offb_ref,
    other_offc_ref,
    other_col_ref,
    field_out,
    push_ref,
    acc_ref,
    tab_ref,
    flow_ref,
    edge_ref,
    pass_ref,
    mid_ref,
    dens_ref,
    sum_ref,
    field_ref,
    slope_ref,
    merged_ref,
    sems,
):
    slope_copies = [
        pltpu.make_async_copy(source, slope_ref.at[side], sems.at[1 + side])
        for side, source in enumerate((own_slope_in, other_slope_in))
    ]
    for copy in slope_copies:
        copy.start()
    tile = place_s[1]
    bases = [tile * HALF, (1 - tile) * HALF]
    pairs = merged_ref.shape[0]
    merged_ref[...] = jnp.where(owner_ref[...] > 0.0, recv_ref[:pairs], recv_ref[pairs:])
    def counter(rows):
        return lax.broadcasted_iota(i32, (rows, LANE), 0).astype(f32).astype(bf16)

    iota_b, iota_c = counter(WINDOW), counter(LANE)
    zero = jnp.zeros((WINDOW, LANE), bf16)
    one_c, zero_c = jnp.ones((LANE, LANE), bf16), jnp.zeros((LANE, LANE), bf16)

    def product(tile, group_b, group_c):
        columns, weights = [], []
        for j in range(TILE_CHUNKS):
            pair = tile * (TILE_CHUNKS // 4) + j // 4
            piece = j % 4
            gb = gb_ref[piece, pl.ds(pair, 1), :]
            gc = gc_ref[piece, pl.ds(pair, 1), :]
            parts = [None] * 4
            for part in range(2):
                value = merged_ref[pair, 4 * part + piece : 4 * part + piece + 1, :]
                parts[part], parts[2 + part] = halves(value)
            hots = []
            for h in range(2):
                band = (LANE * plan_s[8 + 2 * group_c + h]).astype(f32)
                hots.append(jnp.where(iota_c == (gc - band).astype(bf16), one_c, zero_c))
            weights.append(jnp.concatenate(hots, axis=0))
            hit = iota_b == (gb - WINDOW * jnp.asarray(group_b).astype(f32)).astype(bf16)
            columns.append(jnp.concatenate([jnp.where(hit, v, zero) for v in parts], axis=0))
        return mm(jnp.concatenate(columns, axis=1), jnp.concatenate(weights, axis=1), NT)

    acc_ref[0] = jnp.zeros(acc_ref.shape[1:], f32)
    def step(t, _):
        acc_ref[0] += product(t, 0, 0)
        return 0

    steps = 4 * pairs // TILE_CHUNKS
    lax.fori_loop(0, steps, step, 0)

    def rest(combo, _):
        group_b, group_c = combo >> 1, combo & 1

        @pl.when((group_b < plan_s[1]) & (group_c < plan_s[2]))
        def _():
            acc_ref[combo] = jnp.zeros(acc_ref.shape[1:], f32)

            def extra(t, _):
                acc_ref[combo] += product(t, group_b, group_c)
                return 0

            lax.fori_loop(0, steps, extra, 0)

        return 0

    lax.fori_loop(1, 4, rest, 0)

    def transform(group_b):
        def along(group_c, first):
            for level in range(2):
                for h in range(2):
                    band = jnp.minimum(plan_s[8 + 2 * group_c + h], 2) * LANE
                    base = 2 * level * N
                    cos = table_ref[pl.ds(pl.multiple_of(base + band, LANE), LANE), :]
                    sin = table_ref[pl.ds(pl.multiple_of(base + N + band, LANE), LANE), :]
                    top = slice(h * LANE, (h + 1) * LANE)
                    bottom = slice((2 + h) * LANE, (3 + h) * LANE)
                    tab_ref[level, top, :N] = cos
                    tab_ref[level, top, N:] = sin
                    tab_ref[level, bottom, :N] = -sin
                    tab_ref[level, bottom, N:] = cos
            combo = 2 * group_b + group_c
            for k in range(4):
                top = (k // 2) * WINDOW
                flow_ref[top : top + WINDOW, (k % 2) * 2 * LANE : (k % 2 + 1) * 2 * LANE] = acc_ref[
                    combo, k * WINDOW : (k + 1) * WINDOW, :
                ].astype(bf16)
            half = WINDOW
            both = mm(flow_ref[...], tab_ref[0])
            result = both[:half] + both[half:] + mm(flow_ref[:half], tab_ref[1])
            pass_ref[...] = result if first else pass_ref[...] + result

        along(0, True)

        @pl.when(plan_s[2] > 1)
        def _():
            along(1, False)

        for j in range(WINDOW // 16):
            block = plan_s[3] + (group_b * WINDOW) // 16 + j
            block = jnp.where(block >= BLOCKS, block - BLOCKS, block)
            for k in range(4):
                row = pl.multiple_of(k * N + 16 * block, 16)
                edge_ref[16 * j : 16 * j + 16, k * N : (k + 1) * N] = table_ref[pl.ds(row, 16), :]
        high, low = halves(pass_ref[...])
        result = mm(edge_ref[:, : 2 * N], high, TN) + (
            mm(edge_ref[:, 2 * N :], high, TN) + mm(edge_ref[:, : 2 * N], low, TN)
        )
        mid_ref[...] = result if group_b == 0 else mid_ref[...] + result

    transform(0)

    @pl.when(plan_s[1] > 1)
    def _():
        transform(1)

    for base, pot_ref in zip(bases, (own_pot_ref, other_pot_ref)):

        def finish(i, _, base=base, pot_ref=pot_ref):
            r = pl.ds(pl.multiple_of(base + 8 * i, 8), 8)
            s = pl.ds(pl.multiple_of(N + base + 8 * i, 8), 8)
            real = mid_ref[r, :N] - mid_ref[s, N:]
            imag = mid_ref[s, :N] + mid_ref[r, N:]
            dens_ref[r, :] = real * real + imag * imag
            pot = pot_ref[pl.ds(pl.multiple_of(8 * i, 8), 8), :]
            field_ref[0, r, :] = pot * real
            field_ref[1, r, :] = pot * imag
            return 0

        lax.fori_loop(0, HALF // 8, finish, 0, unroll=8)
    field_copy = pltpu.make_async_copy(field_ref, field_out, sems.at[0])
    field_copy.start()
    columns = []
    for side in range(2):
        slope_copies[side].wait()
        offb_ref = (own_offb_ref, other_offb_ref)[side]
        offc_ref = (own_offc_ref, other_offc_ref)[side]
        col_ref = (own_col_ref, other_col_ref)[side]
        for q in range(16):
            plain = [jnp.zeros((8, LANE), f32)] * 3
            scaled = jnp.zeros((8, LANE), f32)
            for i in range(HALF // 8):
                r = slice(8 * i, 8 * i + 8)
                rows = pl.ds(pl.multiple_of(bases[side] + 8 * i, 8), 8)
                w = dens_ref[rows, :] * slope_ref[side, q, r, :]
                w = [w[:, k * LANE : (k + 1) * LANE] for k in range(3)]
                plain = [p + v for p, v in zip(plain, w)]
                scaled = scaled + (w[0] + w[1] + w[2]) * offb_ref[r, q : q + 1]
            for k in range(3):
                cut = slice(k * LANE, (k + 1) * LANE)
                sum_ref[q : q + 1, cut] = jnp.sum(plain[k], axis=0, keepdims=True)
            sum_ref[16 + q : 17 + q, :LANE] = jnp.sum(scaled, axis=0, keepdims=True)
        plain = sum_ref[:16, :]
        scale = col_ref[:16, 1:2] * VOLUME
        push_a = col_ref[:16, 0:1] * jnp.sum(plain, axis=1, keepdims=True) * scale
        push_b = jnp.sum(sum_ref[16:, :LANE], axis=1, keepdims=True) * scale
        push_c = jnp.sum(plain * offc_ref[...], axis=1, keepdims=True) * scale
        columns.append((push_a, push_b, push_c, 0.5 * col_ref[:16, 2:3]))
    ordered = []
    for own, other in zip(*columns):
        ordered.append(jnp.where(tile == 0, own, other))
        ordered.append(jnp.where(tile == 0, other, own))
    packed = jnp.concatenate(ordered, axis=0)
    push_ref[...] = jnp.transpose(jnp.broadcast_to(packed, (LANE, LANE)))[:1]
    field_copy.wait()


def spread_kernel(terms_ref, out_ref):
    terms = terms_ref[...]
    charges = out_ref.shape[1]
    lane = lax.broadcasted_iota(i32, (terms.shape[0], charges), 1).astype(f32)
    totals = [jnp.zeros((terms.shape[0], charges), f32)] * 3
    for q in range(32):
        hot = terms[:, 96 + q : 97 + q] == lane
        for axis in range(3):
            value = terms[:, 32 * axis + q : 32 * axis + q + 1]
            totals[axis] = totals[axis] + jnp.where(hot, value, 0.0)
    for axis in range(3):
        out_ref[axis : axis + 1, :] = jnp.sum(totals[axis], axis=0, keepdims=True)


def vmem(count):
    return [pl.BlockSpec(memory_space=pltpu.VMEM)] * count


def smem(count):
    return [pl.BlockSpec(memory_space=pltpu.SMEM)] * count


def anywhere(count):
    return [pl.BlockSpec(memory_space=pltpu.HBM)] * count


def params(mebibytes):
    return pltpu.CompilerParams(vmem_limit_bytes=mebibytes * 1024 * 1024)


def local(coefficients, col_map, charge_cell, charge_frac, charge, tile_list):
    slots = coefficients.shape[2]
    sources = lax.axis_size("pw")
    planes = sources
    plane = lax.axis_index("pw").astype(i32)
    first_table, second_table = tables(planes)

    sent = pl.pallas_call(
        columns_kernel,
        out_shape=jax.ShapeDtypeStruct((planes, 8, LANE), f32),
        in_specs=smem(1) + anywhere(2),
        out_specs=vmem(1)[0],
        scratch_shapes=[
            pltpu.VMEM((2, slots, N), f32),
            pltpu.VMEM(first_table.shape, bf16),
            pltpu.VMEM((4 * LANE, 2 * N), bf16),
            pltpu.VMEM((4 * LANE, 2 * N), bf16),
            pltpu.SemaphoreType.DMA((5,)),
        ],
        compiler_params=params(54),
        name="columns",
    )(plane[None], coefficients.reshape(2, slots, N), jnp.asarray(first_table))
    own = tile_list[0]
    other = lax.ppermute(own, "mm", [(0, 1), (1, 0)])
    tile = lax.axis_index("mm").astype(i32)
    recv = lax.all_to_all(sent, "pw", 0, 0, tiled=True)

    blocks = col_map.reshape(sources, slots)
    grid = jnp.pad(blocks, ((0, 0), (0, 4 * LANE - slots)), constant_values=EMPTY)

    def charges(listed, side, extra):
        shapes = [
            jax.ShapeDtypeStruct((HALF, N), f32),
            pltpu.HBM((16, HALF, N), f32),
            jax.ShapeDtypeStruct((HALF, LANE), f32),
            jax.ShapeDtypeStruct((16, N), f32),
            jax.ShapeDtypeStruct((LANE, 8), f32),
        ]
        places = vmem(1) + anywhere(1) + vmem(3)
        if extra:
            shapes += [
                jax.ShapeDtypeStruct((4, sources // 2, LANE), f32),
                jax.ShapeDtypeStruct((4, sources // 2, LANE), f32),
                jax.ShapeDtypeStruct((sources // 2, 8, LANE), f32),
                jax.ShapeDtypeStruct((16,), i32),
            ]
            places += vmem(3) + smem(1)
        place = jnp.stack([plane, side])
        column = jnp.pad(listed, (0, LANE - 16), constant_values=-1)[:, None]
        return pl.pallas_call(
            charges_kernel,
            out_shape=tuple(shapes),
            in_specs=smem(5) + vmem(4 + len(extra)),
            out_specs=tuple(places),
            scratch_shapes=[
                pltpu.VMEM((HALF, LANE), f32),
                pltpu.VMEM((HALF, LANE), f32),
                pltpu.VMEM((16, N), f32),
                pltpu.VMEM((16, N), f32),
                pltpu.VMEM((16, HALF, N), f32),
                pltpu.SemaphoreType.DMA((16,)),
            ],
            compiler_params=params(50),
            name="charges_own" if extra else "charges_other",
        )(
            listed,
            charge_cell,
            charge_frac,
            charge[None],
            place,
            column,
            charge_cell,
            charge_frac,
            charge[None],
            *extra,
        )

    mine = charges(own, tile, [grid])
    gb, gc, owner, plan = mine[5:]
    theirs = charges(other, 1 - tile, [])

    field, push = pl.pallas_call(
        grid_kernel,
        out_shape=(
            jax.ShapeDtypeStruct((2, N, N), f32),
            jax.ShapeDtypeStruct((1, LANE), f32),
        ),
        in_specs=smem(2) + vmem(5) + 2 * (vmem(1) + anywhere(1) + vmem(3)),
        out_specs=tuple(anywhere(1) + vmem(1)),
        scratch_shapes=[
            pltpu.VMEM((4, 4 * WINDOW, 2 * LANE), f32),
            pltpu.VMEM((2, 4 * LANE, 2 * N), bf16),
            pltpu.VMEM((2 * WINDOW, 4 * LANE), bf16),
            pltpu.VMEM((WINDOW, 4 * N), bf16),
            pltpu.VMEM((WINDOW, 2 * N), f32),
            pltpu.VMEM((2 * N, 2 * N), f32),
            pltpu.VMEM((N, N), f32),
            pltpu.VMEM((32, N), f32),
            pltpu.VMEM((2, N, N), f32),
            pltpu.VMEM((2, 16, HALF, N), f32),
            pltpu.VMEM((sources // 2, 8, LANE), f32),
            pltpu.SemaphoreType.DMA((3,)),
        ],
        compiler_params=params(50),
        name="grid",
    )(
        plan,
        jnp.stack([plane, tile]),
        recv,
        owner,
        gb,
        gc,
        jnp.asarray(second_table),
        *mine[:5],
        *theirs,
    )

    push = push + lax.ppermute(push, "mm", [(0, 1), (1, 0)])
    terms = lax.all_to_all(
        jnp.broadcast_to(push[None], (sources, 1, LANE)), "pw", 0, 0, tiled=True
    ).reshape(sources, LANE)
    forces = pl.pallas_call(
        spread_kernel,
        out_shape=jax.ShapeDtypeStruct((3, charge.shape[0]), f32),
        in_specs=vmem(1),
        out_specs=vmem(1)[0],
        compiler_params=params(12),
        name="spread",
    )(terms)
    return (field[:, None, None], forces)


def solution(mesh):
    placed = (P(None, "mm", "pw", None), P(), P(), P(), P(), P(("pw", "mm"), None))
    return jax.shard_map(
        local,
        mesh=mesh,
        in_specs=placed,
        out_specs=(P(None, "mm", "pw", None, None), P()),
        check_vma=False,
    )
```

```python
import functools
import math

import jax
import jax.numpy as jnp
import ml_dtypes
import numpy as np
from jax import lax
from jax.experimental import pallas as pl
from jax.experimental.pallas import tpu as pltpu
from jax.sharding import PartitionSpec as P

f32, bf16, i32 = jnp.float32, jnp.bfloat16, jnp.int32
N = 384
HALF = 192
LANE = 128
SPACING = 0.25
SOFTEN = 0.09
VOLUME = SPACING**3
PEAK = 2.0 / math.sqrt(math.pi)
EMPTY = N * N
TILE_CHUNKS = 32
WINDOW = 208
BLOCKS = N // 16
NT = (((1,), (1,)), ((), ()))
TN = (((0,), (0,)), ((), ()))


def split_table(table):
    high = table.astype(np.float32).astype(ml_dtypes.bfloat16)
    low = (table - high.astype(np.float64)).astype(np.float32).astype(ml_dtypes.bfloat16)
    return high, low


def tables(planes):
    index = np.arange(N, dtype=np.int64)
    angle = 2.0 * np.pi / N * ((index[:, None] * index[None, :]) % N).astype(np.float64)
    cos, sin = np.cos(angle), np.sin(angle)
    cz, sz = cos[:planes], sin[:planes]
    first = np.block([[cz, -sz], [sz, cz]])
    first_high, first_low = split_table(first)
    cos_high, cos_low = split_table(cos)
    sin_high, sin_low = split_table(sin)
    return (
        np.concatenate([first_high, first_low], axis=0),
        np.concatenate([cos_high, sin_high, cos_low, sin_low], axis=0),
    )


def mm(a, b, dims=(((1,), (0,)), ((), ()))):
    return lax.dot_general(a, b, dims, preferred_element_type=f32)


def halves(value):
    high = value.astype(bf16)
    low = (value - high.astype(f32)).astype(bf16)
    return high, low


def flip_table(length):
    row = lax.broadcasted_iota(i32, (length, length), 0)
    column = lax.broadcasted_iota(i32, (length, length), 1)
    return jnp.where(row + column == length - 1, 1.0, 0.0).astype(bf16)


def columns_kernel(
    plane_s, coef_in, table_in, out_ref, coef_ref, table_ref, high_ref, low_ref, sems
):
    slots = coef_ref.shape[1]
    half = slots // 2
    copies = []
    for part in range(2):
        for piece in range(2):
            cut = pl.ds(piece * half, half)
            copies.append(
                pltpu.make_async_copy(
                    coef_in.at[part, cut], coef_ref.at[part, cut], sems.at[2 * part + piece]
                )
            )
    copies.append(pltpu.make_async_copy(table_in, table_ref, sems.at[4]))
    for copy in copies:
        copy.start()
    width = high_ref.shape[0]
    planes = out_ref.shape[0]
    high_ref[slots:, :] = jnp.zeros((width - slots, 2 * N), bf16)
    low_ref[slots:, :] = jnp.zeros((width - slots, 2 * N), bf16)
    for part in range(2):
        for piece in range(2):
            copies[2 * part + piece].wait()
            rows = slice(piece * half, (piece + 1) * half)
            high, low = halves(coef_ref[part, rows])
            high_ref[rows, part * N : (part + 1) * N] = high
            low_ref[rows, part * N : (part + 1) * N] = low
    copies[4].wait()
    rows = 2 * planes
    both = mm(table_ref[...], high_ref[...], NT)
    result = both[:rows] + both[rows:] + mm(table_ref[:rows], low_ref[...], NT)

    def put(values):
        for part in range(2):
            for piece in range(4):
                out_ref[:, 4 * part + piece, :] = values[
                    part * planes : (part + 1) * planes, piece * LANE : (piece + 1) * LANE
                ]

    reverse = plane_s[0] < planes // 2

    @pl.when(jnp.logical_not(reverse))
    def _():
        put(result)

    @pl.when(reverse)
    def _():
        high, low = halves(result)
        flip = flip_table(width)
        put(mm(high, flip) + mm(low, flip))


def wrap(offset):
    shifted = offset + HALF
    shifted = jnp.where(shifted < 0, shifted + N, shifted)
    shifted = jnp.where(shifted >= N, shifted - N, shifted)
    return SPACING * (shifted - HALF)


ERF_NUM = (
    -2.72614225801306e-10,
    2.77068142495902e-08,
    -2.10102402082508e-06,
    -5.69250639462346e-05,
    -7.34990630326855e-04,
    -2.95459980854025e-03,
    -1.60960333262415e-02,
)
ERF_DEN = (
    -1.45660718464996e-05,
    -2.13374055278905e-04,
    -1.68282697438203e-03,
    -7.37332916720468e-03,
    -1.42647390514189e-02,
)


def erf(s):
    s = jnp.minimum(s, 4.0)
    sq = s * s
    num = jnp.full_like(s, ERF_NUM[0])
    for c in ERF_NUM[1:]:
        num = num * sq + c
    den = jnp.full_like(s, ERF_DEN[0])
    for c in ERF_DEN[1:]:
        den = den * sq + c
    return s * num / den


def sort_cells(grid_ref, gb_ref, gc_ref, owner_ref, plan_s):
    cells = grid_ref[...]
    pairs = cells.shape[0] // 2
    row = jnp.floor((cells.astype(f32) + 0.5) * (1.0 / N))
    gb = jnp.where(cells < EMPTY, row, -1000.0)
    gc = jnp.where(cells < EMPTY, cells.astype(f32) - N * row, -1000.0)
    high, low = halves(jnp.concatenate([gb[:pairs], gc[:pairs]], axis=0))
    flip = flip_table(cells.shape[1])
    turned = mm(high, flip) + mm(low, flip)
    owned = jnp.where(turned[:pairs] >= 0.0, 1.0, 0.0)
    for piece in range(4):
        cut = slice(piece * LANE, (piece + 1) * LANE)
        owner_ref[:, piece, :] = owned[:, cut]
        owner_ref[:, 4 + piece, :] = owned[:, cut]
    merged_b = jnp.maximum(gb[pairs:], turned[:pairs])
    merged_c = jnp.maximum(gc[pairs:], turned[pairs:])
    found = jnp.int32(0)
    for band in range(3):
        inside = (merged_c >= band * LANE) & (merged_c < (band + 1) * LANE)
        plan_s[8 + found] = jnp.int32(band)
        found = found + jnp.max(jnp.where(inside, 1.0, 0.0)).astype(i32)
    for slot in range(4):
        plan_s[8 + slot] = jnp.where(slot < found, plan_s[8 + slot], 3)
    plan_s[2] = (found + 1) // 2
    alive = merged_b >= 0.0
    block = jnp.where(alive, merged_b * (1.0 / 16.0), 0.0).astype(i32)
    used = jnp.left_shift(jnp.where(alive, 1, 0), block)
    while used.shape[0] > 8:
        used = used[: used.shape[0] // 2] | used[used.shape[0] // 2 :]
    while used.shape[1] > LANE:
        used = used[:, : used.shape[1] // 2] | used[:, used.shape[1] // 2 :]
    for axis, width in ((0, 8), (1, LANE)):
        shift = width // 2
        while shift:
            used = used | pltpu.roll(used, shift, axis)
            shift //= 2
    occupied = jnp.max(used.astype(f32)).astype(i32)
    start = jnp.int32(-1)
    for k in range(BLOCKS):
        outside = sum(1 << ((k + j) % BLOCKS) for j in range(WINDOW // 16, BLOCKS))
        start = jnp.where((occupied & outside) == 0, k, start)
    plan_s[1] = jnp.where(start < 0, 2, 1)
    start = jnp.maximum(start, 0)
    plan_s[3] = start
    shifted = merged_b - (16 * start).astype(f32)
    shifted = jnp.where(shifted < 0.0, shifted + N, shifted)
    shifted = jnp.where(alive, shifted, -1000.0)
    for values, out in ((shifted, gb_ref), (merged_c, gc_ref)):
        for piece in range(4):
            out[piece] = values[:, piece * LANE : (piece + 1) * LANE]


def charges_kernel(
    list_s,
    cell_s,
    frac_s,
    charge_s,
    place_s,
    list_ref,
    cell_ref,
    frac_ref,
    charge_ref,
    *refs,
):
    refs = list(refs)
    grid_ref = refs.pop(0) if len(refs) > 11 else None
    pot_ref, slope_out, offb_ref, offc_ref, col_ref = refs[:5]
    uab_ref, eab_ref, uc_ref, ec_ref, slope_ref, sems = refs[-6:]
    plane = place_s[0].astype(f32)
    tile = place_s[1]
    start_row = (tile * HALF).astype(f32)
    listed = list_ref[...]
    mask = lax.broadcasted_iota(i32, (16, cell_ref.shape[1]), 1) == listed
    center = cell_ref[...].astype(f32) + frac_ref[...]

    def pick(row):
        return jnp.sum(jnp.where(mask, row, 0.0), axis=1, keepdims=True)

    ca, cb, cc = (pick(center[i : i + 1]) for i in range(3))
    strength = pick(charge_ref[...])
    off_a = wrap(plane - ca)
    col_ref[...] = jnp.concatenate(
        [off_a, strength, listed.astype(f32)] + [jnp.zeros((16, 5), f32)], axis=1
    )
    off_c = wrap(lax.broadcasted_iota(i32, (16, N), 1).astype(f32) - cc)
    offc_ref[...] = off_c
    sq_c = off_c * off_c
    uc_ref[...] = sq_c
    ec_ref[...] = jnp.exp(-sq_c)

    def across(column):
        tall = jnp.concatenate([column, jnp.zeros((LANE - 16, 1), f32)], axis=0)
        return jnp.transpose(jnp.broadcast_to(tall, (LANE, LANE)))[:1]

    row = lax.broadcasted_iota(i32, (HALF, LANE), 0).astype(f32) + start_row
    off_b = wrap(row - across(cb))
    offb_ref[...] = off_b
    row_a = across(off_a)
    uab = off_b * off_b + (row_a * row_a + SOFTEN)
    uab_ref[...] = uab
    eab_ref[...] = PEAK * jnp.exp(-uab)

    def wide(ref, q):
        return jnp.broadcast_to(ref[q : q + 1, :], (8, N))

    def power(q):
        return jnp.broadcast_to(strength[q : q + 1, :], (8, N))

    close = (row_a * row_a < 16.0).astype(f32)
    lane = lax.broadcasted_iota(i32, (1, LANE), 1)
    weight = jnp.left_shift(jnp.where(lane < 16, 1, 0), lane & 15).astype(f32)
    bits = jnp.sum(close * weight).astype(i32)

    def wide(ref, q):
        return jnp.broadcast_to(ref[q : q + 1, :], (8, N))

    def power(q):
        return jnp.broadcast_to(strength[q : q + 1, :], (8, N))

    def fix_charge(q):
        own = list_s[q]
        center = [cell_s[axis, own].astype(f32) + frac_s[axis, own] for axis in range(3)]
        strong = charge_s[0, own]
        da = wrap(plane - center[0])
        rest = da * da + SOFTEN
        dc = wrap(lax.broadcasted_iota(i32, (8, N), 1).astype(f32) - center[2])
        rest = rest + dc * dc
        row = lax.broadcasted_iota(i32, (8, N), 0).astype(f32)
        first = jnp.floor((center[1] - 16.0) * 0.125).astype(i32)

        def fix(step, _):
            group = first + step
            group = jnp.where(group < 0, group + N // 8, group)
            group = jnp.where(group >= N // 8, group - N // 8, group)
            i = group - tile * (HALF // 8)

            @pl.when((i >= 0) & (i < HALF // 8))
            def _():
                r = pl.ds(pl.multiple_of(8 * i, 8), 8)
                db = wrap(row + ((8 * group).astype(f32) - center[1]))
                u = db * db + rest
                k = lax.rsqrt(u)
                full = erf(u * k) * k
                slope = k * k * (PEAK * jnp.exp(-u) - full)
                slope_ref[q, r, :] = slope
                pot_ref[r, :] += strong * (full - k)

            return 0

        lax.fori_loop(0, 6, fix, 0)

    copies = []
    for a in range(0, 16, 4):
        lanes = [(q, wide(uc_ref, q), wide(ec_ref, q), power(q)) for q in range(a, a + 4)]
        for i in range(HALF // 8):
            r = slice(8 * i, 8 * i + 8)
            total = None if a == 0 else pot_ref[r, :]
            for q, ucq, ecq, strong in lanes:
                k = lax.rsqrt(uab_ref[r, q : q + 1] + ucq)
                e = eab_ref[r, q : q + 1] * ecq
                slope_ref[q, r, :] = k * k * (e - k)
                total = strong * k if total is None else total + strong * k
            pot_ref[r, :] = total
        found = jnp.right_shift(bits, a) & 15

        @pl.when(found > 0)
        def _(a=a, found=found):
            def visit(j, _):
                @pl.when((jnp.right_shift(found, j) & 1) > 0)
                def _():
                    fix_charge(a + j)

                return 0

            lax.fori_loop(0, 4, visit, 0)

        for q in range(a, a + 4):
            copy = pltpu.make_async_copy(slope_ref.at[q], slope_out.at[q], sems.at[q])
            copy.start()
            copies.append(copy)
    if grid_ref is not None:
        sort_cells(grid_ref, *refs[5:9])
    for copy in copies:
        copy.wait()


def grid_kernel(
    plan_s,
    place_s,
    recv_ref,
    owner_ref,
    gb_ref,
    gc_ref,
    table_ref,
    own_pot_ref,
    own_slope_in,
    own_offb_ref,
    own_offc_ref,
    own_col_ref,
    other_pot_ref,
    other_slope_in,
    other_offb_ref,
    other_offc_ref,
    other_col_ref,
    field_out,
    push_ref,
    acc_ref,
    tab_ref,
    flow_ref,
    edge_ref,
    pass_ref,
    mid_ref,
    dens_ref,
    sum_ref,
    field_ref,
    slope_ref,
    merged_ref,
    sems,
):
    slope_copies = [
        pltpu.make_async_copy(source, slope_ref.at[side], sems.at[1 + side])
        for side, source in enumerate((own_slope_in, other_slope_in))
    ]
    for copy in slope_copies:
        copy.start()
    tile = place_s[1]
    bases = [tile * HALF, (1 - tile) * HALF]
    pairs = merged_ref.shape[0]
    merged_ref[...] = jnp.where(owner_ref[...] > 0.0, recv_ref[:pairs], recv_ref[pairs:])
    def counter(rows):
        return lax.broadcasted_iota(i32, (rows, LANE), 0).astype(f32).astype(bf16)

    iota_b, iota_c = counter(WINDOW), counter(LANE)
    zero = jnp.zeros((WINDOW, LANE), bf16)
    one_c, zero_c = jnp.ones((LANE, LANE), bf16), jnp.zeros((LANE, LANE), bf16)

    def product(tile, group_b, group_c):
        columns, weights = [], []
        for j in range(TILE_CHUNKS):
            pair = tile * (TILE_CHUNKS // 4) + j // 4
            piece = j % 4
            gb = gb_ref[piece, pl.ds(pair, 1), :]
            gc = gc_ref[piece, pl.ds(pair, 1), :]
            parts = [None] * 4
            for part in range(2):
                value = merged_ref[pair, 4 * part + piece : 4 * part + piece + 1, :]
                parts[part], parts[2 + part] = halves(value)
            hots = []
            for h in range(2):
                band = (LANE * plan_s[8 + 2 * group_c + h]).astype(f32)
                hots.append(jnp.where(iota_c == (gc - band).astype(bf16), one_c, zero_c))
            weights.append(jnp.concatenate(hots, axis=0))
            hit = iota_b == (gb - WINDOW * jnp.asarray(group_b).astype(f32)).astype(bf16)
            columns.append(jnp.concatenate([jnp.where(hit, v, zero) for v in parts], axis=0))
        return mm(jnp.concatenate(columns, axis=1), jnp.concatenate(weights, axis=1), NT)

    acc_ref[0] = jnp.zeros(acc_ref.shape[1:], f32)
    def step(t, _):
        acc_ref[0] += product(t, 0, 0)
        return 0

    steps = 4 * pairs // TILE_CHUNKS
    lax.fori_loop(0, steps, step, 0)

    def rest(combo, _):
        group_b, group_c = combo >> 1, combo & 1

        @pl.when((group_b < plan_s[1]) & (group_c < plan_s[2]))
        def _():
            acc_ref[combo] = jnp.zeros(acc_ref.shape[1:], f32)

            def extra(t, _):
                acc_ref[combo] += product(t, group_b, group_c)
                return 0

            lax.fori_loop(0, steps, extra, 0)

        return 0

    lax.fori_loop(1, 4, rest, 0)

    def transform(group_b):
        def along(group_c, first):
            for level in range(2):
                for h in range(2):
                    band = jnp.minimum(plan_s[8 + 2 * group_c + h], 2) * LANE
                    base = 2 * level * N
                    cos = table_ref[pl.ds(pl.multiple_of(base + band, LANE), LANE), :]
                    sin = table_ref[pl.ds(pl.multiple_of(base + N + band, LANE), LANE), :]
                    top = slice(h * LANE, (h + 1) * LANE)
                    bottom = slice((2 + h) * LANE, (3 + h) * LANE)
                    tab_ref[level, top, :N] = cos
                    tab_ref[level, top, N:] = sin
                    tab_ref[level, bottom, :N] = -sin
                    tab_ref[level, bottom, N:] = cos
            combo = 2 * group_b + group_c
            for k in range(4):
                top = (k // 2) * WINDOW
                flow_ref[top : top + WINDOW, (k % 2) * 2 * LANE : (k % 2 + 1) * 2 * LANE] = acc_ref[
                    combo, k * WINDOW : (k + 1) * WINDOW, :
                ].astype(bf16)
            half = WINDOW
            both = mm(flow_ref[...], tab_ref[0])
            result = both[:half] + both[half:] + mm(flow_ref[:half], tab_ref[1])
            pass_ref[...] = result if first else pass_ref[...] + result

        along(0, True)

        @pl.when(plan_s[2] > 1)
        def _():
            along(1, False)

        for j in range(WINDOW // 16):
            block = plan_s[3] + (group_b * WINDOW) // 16 + j
            block = jnp.where(block >= BLOCKS, block - BLOCKS, block)
            for k in range(4):
                row = pl.multiple_of(k * N + 16 * block, 16)
                edge_ref[16 * j : 16 * j + 16, k * N : (k + 1) * N] = table_ref[pl.ds(row, 16), :]
        high, low = halves(pass_ref[...])
        result = mm(edge_ref[:, : 2 * N], high, TN) + (
            mm(edge_ref[:, 2 * N :], high, TN) + mm(edge_ref[:, : 2 * N], low, TN)
        )
        mid_ref[...] = result if group_b == 0 else mid_ref[...] + result

    transform(0)

    @pl.when(plan_s[1] > 1)
    def _():
        transform(1)

    for base, pot_ref in zip(bases, (own_pot_ref, other_pot_ref)):

        def finish(i, _, base=base, pot_ref=pot_ref):
            r = pl.ds(pl.multiple_of(base + 8 * i, 8), 8)
            s = pl.ds(pl.multiple_of(N + base + 8 * i, 8), 8)
            real = mid_ref[r, :N] - mid_ref[s, N:]
            imag = mid_ref[s, :N] + mid_ref[r, N:]
            dens_ref[r, :] = real * real + imag * imag
            pot = pot_ref[pl.ds(pl.multiple_of(8 * i, 8), 8), :]
            field_ref[0, r, :] = pot * real
            field_ref[1, r, :] = pot * imag
            return 0

        lax.fori_loop(0, HALF // 8, finish, 0, unroll=8)
    field_copy = pltpu.make_async_copy(field_ref, field_out, sems.at[0])
    field_copy.start()
    columns = []
    for side in range(2):
        slope_copies[side].wait()
        offb_ref = (own_offb_ref, other_offb_ref)[side]
        offc_ref = (own_offc_ref, other_offc_ref)[side]
        col_ref = (own_col_ref, other_col_ref)[side]
        for q in range(16):
            plain = [jnp.zeros((8, LANE), f32)] * 3
            scaled = jnp.zeros((8, LANE), f32)
            for i in range(HALF // 8):
                r = slice(8 * i, 8 * i + 8)
                rows = pl.ds(pl.multiple_of(bases[side] + 8 * i, 8), 8)
                w = dens_ref[rows, :] * slope_ref[side, q, r, :]
                w = [w[:, k * LANE : (k + 1) * LANE] for k in range(3)]
                plain = [p + v for p, v in zip(plain, w)]
                scaled = scaled + (w[0] + w[1] + w[2]) * offb_ref[r, q : q + 1]
            for k in range(3):
                cut = slice(k * LANE, (k + 1) * LANE)
                sum_ref[q : q + 1, cut] = jnp.sum(plain[k], axis=0, keepdims=True)
            sum_ref[16 + q : 17 + q, :LANE] = jnp.sum(scaled, axis=0, keepdims=True)
        plain = sum_ref[:16, :]
        scale = col_ref[:16, 1:2] * VOLUME
        push_a = col_ref[:16, 0:1] * jnp.sum(plain, axis=1, keepdims=True) * scale
        push_b = jnp.sum(sum_ref[16:, :LANE], axis=1, keepdims=True) * scale
        push_c = jnp.sum(plain * offc_ref[...], axis=1, keepdims=True) * scale
        columns.append((push_a, push_b, push_c, 0.5 * col_ref[:16, 2:3]))
    ordered = []
    for own, other in zip(*columns):
        ordered.append(jnp.where(tile == 0, own, other))
        ordered.append(jnp.where(tile == 0, other, own))
    packed = jnp.concatenate(ordered, axis=0)
    push_ref[...] = jnp.transpose(jnp.broadcast_to(packed, (LANE, LANE)))[:1]
    field_copy.wait()


def spread_kernel(terms_ref, out_ref):
    charges = out_ref.shape[1]
    rows = 32
    lane = lax.broadcasted_iota(i32, (rows, charges), 1).astype(f32)
    totals = [jnp.zeros((rows, charges), f32)] * 3
    for group in range(terms_ref.shape[0] // rows):
        terms = terms_ref[rows * group : rows * (group + 1), :]
        for q in range(32):
            hot = terms[:, 96 + q : 97 + q] == lane
            for axis in range(3):
                value = terms[:, 32 * axis + q : 32 * axis + q + 1]
                totals[axis] = totals[axis] + jnp.where(hot, value, 0.0)
    for axis in range(3):
        out_ref[axis : axis + 1, :] = jnp.sum(totals[axis], axis=0, keepdims=True)


def vmem(count):
    return [pl.BlockSpec(memory_space=pltpu.VMEM)] * count


def smem(count):
    return [pl.BlockSpec(memory_space=pltpu.SMEM)] * count


def anywhere(count):
    return [pl.BlockSpec(memory_space=pltpu.HBM)] * count


def params(mebibytes):
    return pltpu.CompilerParams(vmem_limit_bytes=mebibytes * 1024 * 1024)


def local(coefficients, col_map, charge_cell, charge_frac, charge, tile_list):
    slots = coefficients.shape[2]
    sources = lax.axis_size("pw")
    planes = sources
    plane = lax.axis_index("pw").astype(i32)
    first_table, second_table = tables(planes)

    sent = pl.pallas_call(
        columns_kernel,
        out_shape=jax.ShapeDtypeStruct((planes, 8, LANE), f32),
        in_specs=smem(1) + anywhere(2),
        out_specs=vmem(1)[0],
        scratch_shapes=[
            pltpu.VMEM((2, slots, N), f32),
            pltpu.VMEM(first_table.shape, bf16),
            pltpu.VMEM((4 * LANE, 2 * N), bf16),
            pltpu.VMEM((4 * LANE, 2 * N), bf16),
            pltpu.SemaphoreType.DMA((5,)),
        ],
        compiler_params=params(54),
        name="columns",
    )(plane[None], coefficients.reshape(2, slots, N), jnp.asarray(first_table))
    own = tile_list[0]
    other = lax.ppermute(own, "mm", [(0, 1), (1, 0)])
    tile = lax.axis_index("mm").astype(i32)
    recv = lax.all_to_all(sent, "pw", 0, 0, tiled=True)

    blocks = col_map.reshape(sources, slots)
    grid = jnp.pad(blocks, ((0, 0), (0, 4 * LANE - slots)), constant_values=EMPTY)

    def charges(listed, side, extra):
        shapes = [
            jax.ShapeDtypeStruct((HALF, N), f32),
            pltpu.HBM((16, HALF, N), f32),
            jax.ShapeDtypeStruct((HALF, LANE), f32),
            jax.ShapeDtypeStruct((16, N), f32),
            jax.ShapeDtypeStruct((16, 8), f32),
        ]
        places = vmem(1) + anywhere(1) + vmem(3)
        if extra:
            shapes += [
                jax.ShapeDtypeStruct((4, sources // 2, LANE), f32),
                jax.ShapeDtypeStruct((4, sources // 2, LANE), f32),
                jax.ShapeDtypeStruct((sources // 2, 8, LANE), f32),
                jax.ShapeDtypeStruct((16,), i32),
            ]
            places += vmem(3) + smem(1)
        place = jnp.stack([plane, side])
        column = listed[:, None]
        return pl.pallas_call(
            charges_kernel,
            out_shape=tuple(shapes),
            in_specs=smem(5) + vmem(4 + len(extra)),
            out_specs=tuple(places),
            scratch_shapes=[
                pltpu.VMEM((HALF, LANE), f32),
                pltpu.VMEM((HALF, LANE), f32),
                pltpu.VMEM((16, N), f32),
                pltpu.VMEM((16, N), f32),
                pltpu.VMEM((16, HALF, N), f32),
                pltpu.SemaphoreType.DMA((16,)),
            ],
            compiler_params=params(50),
            name="charges_own" if extra else "charges_other",
        )(
            listed,
            charge_cell,
            charge_frac,
            charge[None],
            place,
            column,
            charge_cell,
            charge_frac,
            charge[None],
            *extra,
        )

    mine = charges(own, tile, [grid])
    gb, gc, owner, plan = mine[5:]
    theirs = charges(other, 1 - tile, [])

    field, push = pl.pallas_call(
        grid_kernel,
        out_shape=(
            jax.ShapeDtypeStruct((2, N, N), f32),
            jax.ShapeDtypeStruct((1, LANE), f32),
        ),
        in_specs=smem(2) + vmem(5) + 2 * (vmem(1) + anywhere(1) + vmem(3)),
        out_specs=tuple(anywhere(1) + vmem(1)),
        scratch_shapes=[
            pltpu.VMEM((4, 4 * WINDOW, 2 * LANE), f32),
            pltpu.VMEM((2, 4 * LANE, 2 * N), bf16),
            pltpu.VMEM((2 * WINDOW, 4 * LANE), bf16),
            pltpu.VMEM((WINDOW, 4 * N), bf16),
            pltpu.VMEM((WINDOW, 2 * N), f32),
            pltpu.VMEM((2 * N, 2 * N), f32),
            pltpu.VMEM((N, N), f32),
            pltpu.VMEM((32, N), f32),
            pltpu.VMEM((2, N, N), f32),
            pltpu.VMEM((2, 16, HALF, N), f32),
            pltpu.VMEM((sources // 2, 8, LANE), f32),
            pltpu.SemaphoreType.DMA((3,)),
        ],
        compiler_params=params(50),
        name="grid",
    )(
        plan,
        jnp.stack([plane, tile]),
        recv,
        owner,
        gb,
        gc,
        jnp.asarray(second_table),
        *mine[:5],
        *theirs,
    )

    push = push + lax.ppermute(push, "mm", [(0, 1), (1, 0)])
    terms = lax.all_to_all(
        jnp.broadcast_to(push[None], (sources, 1, LANE)), "pw", 0, 0, tiled=True
    ).reshape(sources, LANE)
    forces = pl.pallas_call(
        spread_kernel,
        out_shape=jax.ShapeDtypeStruct((3, charge.shape[0]), f32),
        in_specs=vmem(1),
        out_specs=vmem(1)[0],
        compiler_params=params(12),
        name="spread",
    )(terms)
    return (field[:, None, None], forces)


def solution(mesh):
    placed = (P(None, "mm", "pw", None), P(), P(), P(), P(), P(("pw", "mm"), None))
    return jax.shard_map(
        local,
        mesh=mesh,
        in_specs=placed,
        out_specs=(P(None, "mm", "pw", None, None), P()),
        check_vma=False,
    )
```

```python
import functools
import math

import jax
import jax.numpy as jnp
import ml_dtypes
import numpy as np
from jax import lax
from jax.experimental import pallas as pl
from jax.experimental.pallas import tpu as pltpu
from jax.sharding import PartitionSpec as P

f32, bf16, i32 = jnp.float32, jnp.bfloat16, jnp.int32
N = 384
HALF = 192
LANE = 128
SPACING = 0.25
SOFTEN = 0.09
VOLUME = SPACING**3
PEAK = 2.0 / math.sqrt(math.pi)
EMPTY = N * N
TILE_CHUNKS = 32
WINDOW = 208
BLOCKS = N // 16
NT = (((1,), (1,)), ((), ()))
TN = (((0,), (0,)), ((), ()))


def split_table(table):
    high = table.astype(np.float32).astype(ml_dtypes.bfloat16)
    low = (table - high.astype(np.float64)).astype(np.float32).astype(ml_dtypes.bfloat16)
    return high, low


def tables(planes):
    index = np.arange(N, dtype=np.int64)
    angle = 2.0 * np.pi / N * ((index[:, None] * index[None, :]) % N).astype(np.float64)
    cos, sin = np.cos(angle), np.sin(angle)
    cz, sz = cos[:planes], sin[:planes]
    first = np.block([[cz, -sz], [sz, cz]])
    first_high, first_low = split_table(first)
    cos_high, cos_low = split_table(cos)
    sin_high, sin_low = split_table(sin)
    return (
        np.concatenate([first_high, first_low], axis=0),
        np.concatenate([cos_high, sin_high, cos_low, sin_low], axis=0),
    )


def mm(a, b, dims=(((1,), (0,)), ((), ()))):
    return lax.dot_general(a, b, dims, preferred_element_type=f32)


def halves(value):
    high = value.astype(bf16)
    low = (value - high.astype(f32)).astype(bf16)
    return high, low


def flip_table(length):
    row = lax.broadcasted_iota(i32, (length, length), 0)
    column = lax.broadcasted_iota(i32, (length, length), 1)
    return jnp.where(row + column == length - 1, 1.0, 0.0).astype(bf16)


def columns_kernel(
    coef_in, table_in, out_ref, coef_ref, table_ref, high_ref, low_ref, sems
):
    slots = coef_ref.shape[1]
    half = slots // 2
    copies = []
    for part in range(2):
        for piece in range(2):
            cut = pl.ds(piece * half, half)
            copies.append(
                pltpu.make_async_copy(
                    coef_in.at[part, cut], coef_ref.at[part, cut], sems.at[2 * part + piece]
                )
            )
    copies.append(pltpu.make_async_copy(table_in, table_ref, sems.at[4]))
    for copy in copies:
        copy.start()
    width = high_ref.shape[0]
    planes = out_ref.shape[0]
    high_ref[slots:, :] = jnp.zeros((width - slots, 2 * N), bf16)
    low_ref[slots:, :] = jnp.zeros((width - slots, 2 * N), bf16)
    for part in range(2):
        for piece in range(2):
            copies[2 * part + piece].wait()
            rows = slice(piece * half, (piece + 1) * half)
            high, low = halves(coef_ref[part, rows])
            high_ref[rows, part * N : (part + 1) * N] = high
            low_ref[rows, part * N : (part + 1) * N] = low
    copies[4].wait()
    rows = 2 * planes
    both = mm(table_ref[...], high_ref[...], NT)
    result = both[:rows] + both[rows:] + mm(table_ref[:rows], low_ref[...], NT)

    def put(values):
        for part in range(2):
            for piece in range(4):
                out_ref[:, 4 * part + piece, :] = values[
                    part * planes : (part + 1) * planes, piece * LANE : (piece + 1) * LANE
                ]

    reverse = lax.axis_index("pw") < planes // 2

    @pl.when(jnp.logical_not(reverse))
    def _():
        put(result)

    @pl.when(reverse)
    def _():
        high, low = halves(result)
        flip = flip_table(width)
        put(mm(high, flip) + mm(low, flip))


def wrap(offset):
    shifted = offset + HALF
    shifted = jnp.where(shifted < 0, shifted + N, shifted)
    shifted = jnp.where(shifted >= N, shifted - N, shifted)
    return SPACING * (shifted - HALF)


ERF_NUM = (
    -2.72614225801306e-10,
    2.77068142495902e-08,
    -2.10102402082508e-06,
    -5.69250639462346e-05,
    -7.34990630326855e-04,
    -2.95459980854025e-03,
    -1.60960333262415e-02,
)
ERF_DEN = (
    -1.45660718464996e-05,
    -2.13374055278905e-04,
    -1.68282697438203e-03,
    -7.37332916720468e-03,
    -1.42647390514189e-02,
)


def erf(s):
    s = jnp.minimum(s, 4.0)
    sq = s * s
    num = jnp.full_like(s, ERF_NUM[0])
    for c in ERF_NUM[1:]:
        num = num * sq + c
    den = jnp.full_like(s, ERF_DEN[0])
    for c in ERF_DEN[1:]:
        den = den * sq + c
    return s * num / den


def charges_kernel(
    list_ref,
    cell_ref,
    frac_ref,
    charge_ref,
    grid_ref,
    pot_ref,
    slope_out,
    offb_ref,
    offc_ref,
    col_ref,
    gb_ref,
    gc_ref,
    owner_ref,
    plan_s,
    uab_ref,
    eab_ref,
    uc_ref,
    ec_ref,
    slope_ref,
    sems,
):
    cells = grid_ref[...]
    pairs = cells.shape[0] // 2
    row = jnp.floor((cells.astype(f32) + 0.5) * (1.0 / N))
    gb = jnp.where(cells < EMPTY, row, -1000.0)
    gc = jnp.where(cells < EMPTY, cells.astype(f32) - N * row, -1000.0)
    high, low = halves(jnp.concatenate([gb[:pairs], gc[:pairs]], axis=0))
    flip = flip_table(cells.shape[1])
    turned = mm(high, flip) + mm(low, flip)
    owned = jnp.where(turned[:pairs] >= 0.0, 1.0, 0.0)
    for piece in range(4):
        cut = slice(piece * LANE, (piece + 1) * LANE)
        owner_ref[:, piece, :] = owned[:, cut]
        owner_ref[:, 4 + piece, :] = owned[:, cut]
    merged_b = jnp.maximum(gb[pairs:], turned[:pairs])
    merged_c = jnp.maximum(gc[pairs:], turned[pairs:])
    found = jnp.int32(0)
    for band in range(3):
        inside = (merged_c >= band * LANE) & (merged_c < (band + 1) * LANE)
        plan_s[8 + found] = jnp.int32(band)
        found = found + jnp.max(jnp.where(inside, 1.0, 0.0)).astype(i32)
    for slot in range(4):
        plan_s[8 + slot] = jnp.where(slot < found, plan_s[8 + slot], 3)
    plan_s[2] = (found + 1) // 2
    alive = merged_b >= 0.0
    block = jnp.where(alive, merged_b * (1.0 / 16.0), 0.0).astype(i32)
    used = jnp.left_shift(jnp.where(alive, 1, 0), block)
    while used.shape[0] > 8:
        used = used[: used.shape[0] // 2] | used[used.shape[0] // 2 :]
    while used.shape[1] > LANE:
        used = used[:, : used.shape[1] // 2] | used[:, used.shape[1] // 2 :]
    for axis, width in ((0, 8), (1, LANE)):
        shift = width // 2
        while shift:
            used = used | pltpu.roll(used, shift, axis)
            shift //= 2
    occupied = jnp.max(used.astype(f32)).astype(i32)
    start = jnp.int32(-1)
    for k in range(BLOCKS):
        outside = sum(1 << ((k + j) % BLOCKS) for j in range(WINDOW // 16, BLOCKS))
        start = jnp.where((occupied & outside) == 0, k, start)
    plan_s[1] = jnp.where(start < 0, 2, 1)
    start = jnp.maximum(start, 0)
    plan_s[3] = start
    shifted = merged_b - (16 * start).astype(f32)
    shifted = jnp.where(shifted < 0.0, shifted + N, shifted)
    shifted = jnp.where(alive, shifted, -1000.0)
    for values, out in ((shifted, gb_ref), (merged_c, gc_ref)):
        for piece in range(4):
            out[piece] = values[:, piece * LANE : (piece + 1) * LANE]

    listed = list_ref[...]
    mask = lax.broadcasted_iota(i32, (32, cell_ref.shape[1]), 1) == listed
    center = cell_ref[...].astype(f32) + frac_ref[...]

    def pick(row):
        return jnp.sum(jnp.where(mask, row, 0.0), axis=1, keepdims=True)

    ca, cb, cc = (pick(center[i : i + 1]) for i in range(3))
    strength = pick(charge_ref[...])
    plane = lax.axis_index("pw").astype(f32)
    off_a = wrap(plane - ca)
    col_ref[...] = jnp.concatenate(
        [off_a, strength, listed.astype(f32)] + [jnp.zeros((32, 5), f32)], axis=1
    )
    off_c = wrap(lax.broadcasted_iota(i32, (32, N), 1).astype(f32) - cc)
    offc_ref[...] = off_c
    sq_c = off_c * off_c
    uc_ref[...] = sq_c
    ec_ref[...] = jnp.exp(-sq_c)

    def across(column):
        tall = jnp.concatenate([column, jnp.zeros((LANE - 32, 1), f32)], axis=0)
        return jnp.transpose(jnp.broadcast_to(tall, (LANE, LANE)))[:1]

    row_b, row_c, row_s = across(cb), across(cc), across(strength)
    off_b = wrap(lax.broadcasted_iota(i32, (N, LANE), 0).astype(f32) - row_b)
    offb_ref[...] = off_b
    row_a = across(off_a)
    uab = off_b * off_b + (row_a * row_a + SOFTEN)
    uab_ref[...] = uab
    eab_ref[...] = PEAK * jnp.exp(-uab)

    def wide(ref, q):
        return jnp.broadcast_to(ref[q : q + 1, :], (8, N))

    def power(q):
        return jnp.broadcast_to(strength[q : q + 1, :], (8, N))

    close = (row_a * row_a < 16.0).astype(f32)
    lane = lax.broadcasted_iota(i32, (1, LANE), 1)
    bits = []
    for half in range(2):
        weight = jnp.where((lane >= 16 * half) & (lane < 16 * half + 16), 1, 0)
        weight = jnp.left_shift(weight, lane & 15).astype(f32)
        bits.append(jnp.sum(close * weight).astype(i32))

    def fix_charge(q):
        base = (q >> 4) * (HALF // 8)

        def one(row):
            return jnp.sum(jnp.where(lane == q, row, 0.0), axis=1, keepdims=True)

        da, cb_one, cc_one, strong = one(row_a), one(row_b), one(row_c), one(row_s)
        dc = wrap(lax.broadcasted_iota(i32, (8, N), 1).astype(f32) - cc_one)
        rest = dc * dc + (da * da + SOFTEN)
        row = lax.broadcasted_iota(i32, (8, N), 0).astype(f32)
        first = jnp.floor((jnp.sum(cb_one) - 16.0) * 0.125).astype(i32)

        def fix(step, _):
            group = first + step
            group = jnp.where(group < 0, group + N // 8, group)
            group = jnp.where(group >= N // 8, group - N // 8, group)
            i = group - base

            @pl.when((i >= 0) & (i < HALF // 8))
            def _():
                r = pl.ds(pl.multiple_of(8 * group, 8), 8)
                db = wrap(row + ((8 * group).astype(f32) - cb_one))
                u = db * db + rest
                k = lax.rsqrt(u)
                full = erf(u * k) * k
                slope = k * k * (PEAK * jnp.exp(-u) - full)
                slope_ref[q, pl.ds(pl.multiple_of(8 * i, 8), 8), :] = slope
                pot_ref[r, :] += strong * (full - k)

            return 0

        lax.fori_loop(0, 6, fix, 0)

    copies = []
    for a in range(0, 16, 2):
        for half in range(2):
            pair = (16 * half + a, 16 * half + a + 1)
            lanes = [(q, wide(uc_ref, q), wide(ec_ref, q), power(q)) for q in pair]
            for i in range(HALF // 8):
                r = slice(half * HALF + 8 * i, half * HALF + 8 * i + 8)
                total = None
                for q, ucq, ecq, strong in lanes:
                    k = lax.rsqrt(uab_ref[r, q : q + 1] + ucq)
                    e = eab_ref[r, q : q + 1] * ecq
                    slope_ref[q, 8 * i : 8 * i + 8, :] = k * k * (e - k)
                    total = strong * k if total is None else total + strong * k
                pot_ref[r, :] = total if a == 0 else pot_ref[r, :] + total
        found = [jnp.right_shift(value, a) & 3 for value in bits]
        found = found[0] + 4 * found[1]

        @pl.when(found > 0)
        def _(a=a, found=found):
            def visit(j, _):
                @pl.when((jnp.right_shift(found, j) & 1) > 0)
                def _():
                    fix_charge(16 * (j >> 1) + a + (j & 1))

                return 0

            lax.fori_loop(0, 4, visit, 0)

        for q in (a, a + 1, 16 + a, 17 + a):
            copy = pltpu.make_async_copy(slope_ref.at[q], slope_out.at[q], sems.at[q])
            copy.start()
            copies.append(copy)
    for copy in copies:
        copy.wait()


def grid_kernel(
    plan_s,
    recv_ref,
    owner_ref,
    gb_ref,
    gc_ref,
    table_ref,
    pot_ref,
    slope_in,
    offb_ref,
    offc_ref,
    col_ref,
    field_out,
    push_ref,
    acc_ref,
    tab_ref,
    flow_ref,
    edge_ref,
    pass_ref,
    mid_ref,
    dens_ref,
    sum_ref,
    field_ref,
    slope_ref,
    merged_ref,
    sems,
):
    slope_copy = pltpu.make_async_copy(slope_in, slope_ref, sems.at[1])
    slope_copy.start()
    pairs = merged_ref.shape[0]
    merged_ref[...] = jnp.where(owner_ref[...] > 0.0, recv_ref[:pairs], recv_ref[pairs:])
    def counter(rows):
        return lax.broadcasted_iota(i32, (rows, LANE), 0).astype(f32).astype(bf16)

    iota_b, iota_c = counter(WINDOW), counter(LANE)
    zero = jnp.zeros((WINDOW, LANE), bf16)
    one_c, zero_c = jnp.ones((LANE, LANE), bf16), jnp.zeros((LANE, LANE), bf16)

    def product(tile, group_b, group_c):
        columns, weights = [], []
        for j in range(TILE_CHUNKS):
            pair = tile * (TILE_CHUNKS // 4) + j // 4
            piece = j % 4
            gb = gb_ref[piece, pl.ds(pair, 1), :]
            gc = gc_ref[piece, pl.ds(pair, 1), :]
            parts = [None] * 4
            for part in range(2):
                value = merged_ref[pair, 4 * part + piece : 4 * part + piece + 1, :]
                parts[part], parts[2 + part] = halves(value)
            hots = []
            for h in range(2):
                band = (LANE * plan_s[8 + 2 * group_c + h]).astype(f32)
                hots.append(jnp.where(iota_c == (gc - band).astype(bf16), one_c, zero_c))
            weights.append(jnp.concatenate(hots, axis=0))
            hit = iota_b == (gb - WINDOW * jnp.asarray(group_b).astype(f32)).astype(bf16)
            columns.append(jnp.concatenate([jnp.where(hit, v, zero) for v in parts], axis=0))
        return mm(jnp.concatenate(columns, axis=1), jnp.concatenate(weights, axis=1), NT)

    acc_ref[0] = jnp.zeros(acc_ref.shape[1:], f32)
    def step(t, _):
        acc_ref[0] += product(t, 0, 0)
        return 0

    steps = 4 * pairs // TILE_CHUNKS
    lax.fori_loop(0, steps, step, 0)

    def rest(combo, _):
        group_b, group_c = combo >> 1, combo & 1

        @pl.when((group_b < plan_s[1]) & (group_c < plan_s[2]))
        def _():
            acc_ref[combo] = jnp.zeros(acc_ref.shape[1:], f32)

            def extra(t, _):
                acc_ref[combo] += product(t, group_b, group_c)
                return 0

            lax.fori_loop(0, steps, extra, 0)

        return 0

    lax.fori_loop(1, 4, rest, 0)

    def transform(group_b):
        def along(group_c, first):
            for level in range(2):
                for h in range(2):
                    band = jnp.minimum(plan_s[8 + 2 * group_c + h], 2) * LANE
                    base = 2 * level * N
                    cos = table_ref[pl.ds(pl.multiple_of(base + band, LANE), LANE), :]
                    sin = table_ref[pl.ds(pl.multiple_of(base + N + band, LANE), LANE), :]
                    top = slice(h * LANE, (h + 1) * LANE)
                    bottom = slice((2 + h) * LANE, (3 + h) * LANE)
                    tab_ref[level, top, :N] = cos
                    tab_ref[level, top, N:] = sin
                    tab_ref[level, bottom, :N] = -sin
                    tab_ref[level, bottom, N:] = cos
            combo = 2 * group_b + group_c
            for k in range(4):
                top = (k // 2) * WINDOW
                flow_ref[top : top + WINDOW, (k % 2) * 2 * LANE : (k % 2 + 1) * 2 * LANE] = acc_ref[
                    combo, k * WINDOW : (k + 1) * WINDOW, :
                ].astype(bf16)
            half = WINDOW
            both = mm(flow_ref[...], tab_ref[0])
            result = both[:half] + both[half:] + mm(flow_ref[:half], tab_ref[1])
            pass_ref[...] = result if first else pass_ref[...] + result

        along(0, True)

        @pl.when(plan_s[2] > 1)
        def _():
            along(1, False)

        for j in range(WINDOW // 16):
            block = plan_s[3] + (group_b * WINDOW) // 16 + j
            block = jnp.where(block >= BLOCKS, block - BLOCKS, block)
            for k in range(4):
                row = pl.multiple_of(k * N + 16 * block, 16)
                edge_ref[16 * j : 16 * j + 16, k * N : (k + 1) * N] = table_ref[pl.ds(row, 16), :]
        high, low = halves(pass_ref[...])
        result = mm(edge_ref[:, : 2 * N], high, TN) + (
            mm(edge_ref[:, 2 * N :], high, TN) + mm(edge_ref[:, : 2 * N], low, TN)
        )
        mid_ref[...] = result if group_b == 0 else mid_ref[...] + result

    transform(0)

    @pl.when(plan_s[1] > 1)
    def _():
        transform(1)

    def finish(i, _):
        r = pl.ds(pl.multiple_of(8 * i, 8), 8)
        s = pl.ds(pl.multiple_of(N + 8 * i, 8), 8)
        real = mid_ref[r, :N] - mid_ref[s, N:]
        imag = mid_ref[s, :N] + mid_ref[r, N:]
        dens_ref[r, :] = real * real + imag * imag
        pot = pot_ref[r, :]
        field_ref[0, r, :] = pot * real
        field_ref[1, r, :] = pot * imag
        return 0

    lax.fori_loop(0, N // 8, finish, 0, unroll=8)
    field_copy = pltpu.make_async_copy(field_ref, field_out, sems.at[0])
    field_copy.start()
    slope_copy.wait()
    for q in range(32):
        base = (q // 16) * HALF
        plain = [jnp.zeros((8, LANE), f32)] * 3
        scaled = jnp.zeros((8, LANE), f32)
        for i in range(HALF // 8):
            r = slice(base + 8 * i, base + 8 * i + 8)
            w = dens_ref[r, :] * slope_ref[q, 8 * i : 8 * i + 8, :]
            w = [w[:, k * LANE : (k + 1) * LANE] for k in range(3)]
            plain = [p + v for p, v in zip(plain, w)]
            scaled = scaled + (w[0] + w[1] + w[2]) * offb_ref[r, q : q + 1]
        for k in range(3):
            sum_ref[q : q + 1, k * LANE : (k + 1) * LANE] = jnp.sum(plain[k], axis=0, keepdims=True)
        sum_ref[32 + q : 33 + q, :LANE] = jnp.sum(scaled, axis=0, keepdims=True)
    plain = sum_ref[:32, :]
    off_a = col_ref[:32, 0:1]
    scale = col_ref[:32, 1:2] * VOLUME
    push_a = off_a * jnp.sum(plain, axis=1, keepdims=True) * scale
    push_b = jnp.sum(sum_ref[32:, :LANE], axis=1, keepdims=True) * scale
    push_c = jnp.sum(plain * offc_ref[...], axis=1, keepdims=True) * scale
    packed = jnp.concatenate([push_a, push_b, push_c, 0.5 * col_ref[:32, 2:3]], axis=0)
    push_ref[...] = jnp.transpose(jnp.broadcast_to(packed, (LANE, LANE)))[:1]
    field_copy.wait()


def spread_kernel(terms_ref, out_ref):
    terms = terms_ref[...]
    charges = out_ref.shape[1]
    lane = lax.broadcasted_iota(i32, (terms.shape[0], charges), 1).astype(f32)
    totals = [jnp.zeros((terms.shape[0], charges), f32)] * 3
    for q in range(32):
        hot = terms[:, 96 + q : 97 + q] == lane
        for axis in range(3):
            value = terms[:, 32 * axis + q : 32 * axis + q + 1]
            totals[axis] = totals[axis] + jnp.where(hot, value, 0.0)
    for axis in range(3):
        out_ref[axis : axis + 1, :] = jnp.sum(totals[axis], axis=0, keepdims=True)


def vmem(count):
    return [pl.BlockSpec(memory_space=pltpu.VMEM)] * count


def smem(count):
    return [pl.BlockSpec(memory_space=pltpu.SMEM)] * count


def anywhere(count):
    return [pl.BlockSpec(memory_space=pltpu.HBM)] * count


def params(mebibytes):
    return pltpu.CompilerParams(vmem_limit_bytes=mebibytes * 1024 * 1024)


def local(coefficients, col_map, charge_cell, charge_frac, charge, tile_list):
    slots = coefficients.shape[2]
    sources = lax.axis_size("pw")
    planes = sources
    first_table, second_table = tables(planes)

    sent = pl.pallas_call(
        columns_kernel,
        out_shape=jax.ShapeDtypeStruct((planes, 8, LANE), f32),
        in_specs=anywhere(2),
        out_specs=vmem(1)[0],
        scratch_shapes=[
            pltpu.VMEM((2, slots, N), f32),
            pltpu.VMEM(first_table.shape, bf16),
            pltpu.VMEM((4 * LANE, 2 * N), bf16),
            pltpu.VMEM((4 * LANE, 2 * N), bf16),
            pltpu.SemaphoreType.DMA((5,)),
        ],
        compiler_params=params(54),
        name="columns",
    )(coefficients.reshape(2, slots, N), jnp.asarray(first_table))
    own = tile_list[0]
    other = lax.ppermute(own, "mm", [(0, 1), (1, 0)])
    first = lax.axis_index("mm") == 0
    listed = jnp.concatenate([jnp.where(first, own, other), jnp.where(first, other, own)])

    recv = lax.all_to_all(sent, "pw", 0, 0, tiled=True)

    blocks = col_map.reshape(sources, slots)
    grid = jnp.pad(blocks, ((0, 0), (0, 4 * LANE - slots)), constant_values=EMPTY)

    pot, slope, offb, offc, col, gb, gc, owner, plan = pl.pallas_call(
        charges_kernel,
        out_shape=(
            jax.ShapeDtypeStruct((N, N), f32),
            pltpu.HBM((32, HALF, N), f32),
            jax.ShapeDtypeStruct((N, LANE), f32),
            jax.ShapeDtypeStruct((32, N), f32),
            jax.ShapeDtypeStruct((32, 8), f32),
            jax.ShapeDtypeStruct((4, sources // 2, LANE), f32),
            jax.ShapeDtypeStruct((4, sources // 2, LANE), f32),
            jax.ShapeDtypeStruct((sources // 2, 8, LANE), f32),
            jax.ShapeDtypeStruct((16,), i32),
        ),
        in_specs=vmem(5),
        out_specs=tuple(vmem(1) + anywhere(1) + vmem(6) + smem(1)),
        scratch_shapes=[
            pltpu.VMEM((N, LANE), f32),
            pltpu.VMEM((N, LANE), f32),
            pltpu.VMEM((32, N), f32),
            pltpu.VMEM((32, N), f32),
            pltpu.VMEM((32, HALF, N), f32),
            pltpu.SemaphoreType.DMA((32,)),
        ],
        compiler_params=params(50),
        name="charges",
    )(
        listed[:, None],
        charge_cell,
        charge_frac,
        charge[None],
        grid,
    )

    field, push = pl.pallas_call(
        grid_kernel,
        out_shape=(
            jax.ShapeDtypeStruct((2, N, N), f32),
            jax.ShapeDtypeStruct((1, LANE), f32),
        ),
        in_specs=smem(1) + vmem(6) + anywhere(1) + vmem(3),
        out_specs=tuple(anywhere(1) + vmem(1)),
        scratch_shapes=[
            pltpu.VMEM((4, 4 * WINDOW, 2 * LANE), f32),
            pltpu.VMEM((2, 4 * LANE, 2 * N), bf16),
            pltpu.VMEM((2 * WINDOW, 4 * LANE), bf16),
            pltpu.VMEM((WINDOW, 4 * N), bf16),
            pltpu.VMEM((WINDOW, 2 * N), f32),
            pltpu.VMEM((2 * N, 2 * N), f32),
            pltpu.VMEM((N, N), f32),
            pltpu.VMEM((64, N), f32),
            pltpu.VMEM((2, N, N), f32),
            pltpu.VMEM((32, HALF, N), f32),
            pltpu.VMEM((sources // 2, 8, LANE), f32),
            pltpu.SemaphoreType.DMA((2,)),
        ],
        compiler_params=params(50),
        name="grid",
    )(plan, recv, owner, gb, gc, jnp.asarray(second_table), pot, slope, offb, offc, col)

    push = push + lax.ppermute(push, "mm", [(0, 1), (1, 0)])
    terms = lax.all_to_all(
        jnp.broadcast_to(push[None], (sources, 1, LANE)), "pw", 0, 0, tiled=True
    ).reshape(sources, LANE)
    forces = pl.pallas_call(
        spread_kernel,
        out_shape=jax.ShapeDtypeStruct((3, charge.shape[0]), f32),
        in_specs=vmem(1),
        out_specs=vmem(1)[0],
        compiler_params=params(12),
        name="spread",
    )(terms)
    return (field[:, None, None], forces)


def solution(mesh):
    placed = (P(None, "mm", "pw", None), P(), P(), P(), P(), P(("pw", "mm"), None))
    return jax.shard_map(
        local,
        mesh=mesh,
        in_specs=placed,
        out_specs=(P(None, "mm", "pw", None, None), P()),
        check_vma=False,
    )
```

```python
import functools
import math

import jax
import jax.numpy as jnp
import ml_dtypes
import numpy as np
from jax import lax
from jax.experimental import pallas as pl
from jax.experimental.pallas import tpu as pltpu
from jax.sharding import PartitionSpec as P

f32, bf16, i32 = jnp.float32, jnp.bfloat16, jnp.int32
N = 384
HALF = 192
LANE = 128
SPACING = 0.25
SOFTEN = 0.09
VOLUME = SPACING**3
PEAK = 2.0 / math.sqrt(math.pi)
EMPTY = N * N
TILE_CHUNKS = 32
WINDOW = 208
BLOCKS = N // 16
NT = (((1,), (1,)), ((), ()))
TN = (((0,), (0,)), ((), ()))


def split_table(table):
    high = table.astype(np.float32).astype(ml_dtypes.bfloat16)
    low = (table - high.astype(np.float64)).astype(np.float32).astype(ml_dtypes.bfloat16)
    return high, low


def tables(planes):
    index = np.arange(N, dtype=np.int64)
    angle = 2.0 * np.pi / N * ((index[:, None] * index[None, :]) % N).astype(np.float64)
    cos, sin = np.cos(angle), np.sin(angle)
    cz, sz = cos[:planes], sin[:planes]
    first = np.block([[cz, -sz], [sz, cz]])
    first_high, first_low = split_table(first)
    cos_high, cos_low = split_table(cos)
    sin_high, sin_low = split_table(sin)
    return (
        np.concatenate([first_high, first_low], axis=0),
        np.concatenate([cos_high, sin_high, cos_low, sin_low], axis=0),
    )


def mm(a, b, dims=(((1,), (0,)), ((), ()))):
    return lax.dot_general(a, b, dims, preferred_element_type=f32)


def halves(value):
    high = value.astype(bf16)
    low = (value - high.astype(f32)).astype(bf16)
    return high, low


def flip_table(length):
    row = lax.broadcasted_iota(i32, (length, length), 0)
    column = lax.broadcasted_iota(i32, (length, length), 1)
    return jnp.where(row + column == length - 1, 1.0, 0.0).astype(bf16)


def columns_kernel(
    coef_in, table_in, out_ref, coef_ref, table_ref, high_ref, low_ref, sems
):
    slots = coef_ref.shape[1]
    half = slots // 2
    copies = []
    for part in range(2):
        for piece in range(2):
            cut = pl.ds(piece * half, half)
            copies.append(
                pltpu.make_async_copy(
                    coef_in.at[part, cut], coef_ref.at[part, cut], sems.at[2 * part + piece]
                )
            )
    copies.append(pltpu.make_async_copy(table_in, table_ref, sems.at[4]))
    for copy in copies:
        copy.start()
    width = high_ref.shape[0]
    planes = out_ref.shape[0]
    high_ref[slots:, :] = jnp.zeros((width - slots, 2 * N), bf16)
    low_ref[slots:, :] = jnp.zeros((width - slots, 2 * N), bf16)
    for part in range(2):
        for piece in range(2):
            copies[2 * part + piece].wait()
            rows = slice(piece * half, (piece + 1) * half)
            high, low = halves(coef_ref[part, rows])
            high_ref[rows, part * N : (part + 1) * N] = high
            low_ref[rows, part * N : (part + 1) * N] = low
    copies[4].wait()
    rows = 2 * planes
    both = mm(table_ref[...], high_ref[...], NT)
    result = both[:rows] + both[rows:] + mm(table_ref[:rows], low_ref[...], NT)

    def put(values):
        for part in range(2):
            for piece in range(4):
                out_ref[:, 4 * part + piece, :] = values[
                    part * planes : (part + 1) * planes, piece * LANE : (piece + 1) * LANE
                ]

    reverse = lax.axis_index("pw") < planes // 2

    @pl.when(jnp.logical_not(reverse))
    def _():
        put(result)

    @pl.when(reverse)
    def _():
        high, low = halves(result)
        flip = flip_table(width)
        put(mm(high, flip) + mm(low, flip))


def wrap(offset):
    shifted = offset + HALF
    shifted = jnp.where(shifted < 0, shifted + N, shifted)
    shifted = jnp.where(shifted >= N, shifted - N, shifted)
    return SPACING * (shifted - HALF)


ERF_NUM = (
    -2.72614225801306e-10,
    2.77068142495902e-08,
    -2.10102402082508e-06,
    -5.69250639462346e-05,
    -7.34990630326855e-04,
    -2.95459980854025e-03,
    -1.60960333262415e-02,
)
ERF_DEN = (
    -1.45660718464996e-05,
    -2.13374055278905e-04,
    -1.68282697438203e-03,
    -7.37332916720468e-03,
    -1.42647390514189e-02,
)


def erf(s):
    s = jnp.minimum(s, 4.0)
    sq = s * s
    num = jnp.full_like(s, ERF_NUM[0])
    for c in ERF_NUM[1:]:
        num = num * sq + c
    den = jnp.full_like(s, ERF_DEN[0])
    for c in ERF_DEN[1:]:
        den = den * sq + c
    return s * num / den


def charges_kernel(
    list_ref,
    cell_ref,
    frac_ref,
    charge_ref,
    grid_ref,
    pot_ref,
    slope_out,
    offb_ref,
    offc_ref,
    col_ref,
    gb_ref,
    gc_ref,
    owner_ref,
    plan_s,
    uab_ref,
    eab_ref,
    uc_ref,
    ec_ref,
    slope_ref,
    sems,
):
    cells = grid_ref[...]
    pairs = cells.shape[0] // 2
    row = jnp.floor((cells.astype(f32) + 0.5) * (1.0 / N))
    gb = jnp.where(cells < EMPTY, row, -1000.0)
    gc = jnp.where(cells < EMPTY, cells.astype(f32) - N * row, -1000.0)
    high, low = halves(jnp.concatenate([gb[:pairs], gc[:pairs]], axis=0))
    flip = flip_table(cells.shape[1])
    turned = mm(high, flip) + mm(low, flip)
    owned = jnp.where(turned[:pairs] >= 0.0, 1.0, 0.0)
    for piece in range(4):
        cut = slice(piece * LANE, (piece + 1) * LANE)
        owner_ref[:, piece, :] = owned[:, cut]
        owner_ref[:, 4 + piece, :] = owned[:, cut]
    merged_b = jnp.maximum(gb[pairs:], turned[:pairs])
    merged_c = jnp.maximum(gc[pairs:], turned[pairs:])
    found = jnp.int32(0)
    for band in range(3):
        inside = (merged_c >= band * LANE) & (merged_c < (band + 1) * LANE)
        plan_s[8 + found] = jnp.int32(band)
        found = found + jnp.max(jnp.where(inside, 1.0, 0.0)).astype(i32)
    for slot in range(4):
        plan_s[8 + slot] = jnp.where(slot < found, plan_s[8 + slot], 3)
    plan_s[2] = (found + 1) // 2
    alive = merged_b >= 0.0
    block = jnp.where(alive, merged_b * (1.0 / 16.0), 0.0).astype(i32)
    used = jnp.left_shift(jnp.where(alive, 1, 0), block)
    while used.shape[0] > 8:
        used = used[: used.shape[0] // 2] | used[used.shape[0] // 2 :]
    while used.shape[1] > LANE:
        used = used[:, : used.shape[1] // 2] | used[:, used.shape[1] // 2 :]
    for axis, width in ((0, 8), (1, LANE)):
        shift = width // 2
        while shift:
            used = used | pltpu.roll(used, shift, axis)
            shift //= 2
    occupied = jnp.max(used.astype(f32)).astype(i32)
    start = jnp.int32(-1)
    for k in range(BLOCKS):
        outside = sum(1 << ((k + j) % BLOCKS) for j in range(WINDOW // 16, BLOCKS))
        start = jnp.where((occupied & outside) == 0, k, start)
    plan_s[1] = jnp.where(start < 0, 2, 1)
    start = jnp.maximum(start, 0)
    plan_s[3] = start
    shifted = merged_b - (16 * start).astype(f32)
    shifted = jnp.where(shifted < 0.0, shifted + N, shifted)
    shifted = jnp.where(alive, shifted, -1000.0)
    for values, out in ((shifted, gb_ref), (merged_c, gc_ref)):
        for piece in range(4):
            out[piece] = values[:, piece * LANE : (piece + 1) * LANE]

    listed = list_ref[...]
    mask = lax.broadcasted_iota(i32, (32, cell_ref.shape[1]), 1) == listed
    center = cell_ref[...].astype(f32) + frac_ref[...]

    def pick(row):
        return jnp.sum(jnp.where(mask, row, 0.0), axis=1, keepdims=True)

    ca, cb, cc = (pick(center[i : i + 1]) for i in range(3))
    strength = pick(charge_ref[...])
    plane = lax.axis_index("pw").astype(f32)
    off_a = wrap(plane - ca)
    col_ref[...] = jnp.concatenate(
        [off_a, strength, listed.astype(f32)] + [jnp.zeros((32, 5), f32)], axis=1
    )
    off_c = wrap(lax.broadcasted_iota(i32, (32, N), 1).astype(f32) - cc)
    offc_ref[...] = off_c
    sq_c = off_c * off_c
    uc_ref[...] = sq_c
    ec_ref[...] = jnp.exp(-sq_c)

    def across(column):
        tall = jnp.concatenate([column, jnp.zeros((LANE - 32, 1), f32)], axis=0)
        return jnp.transpose(jnp.broadcast_to(tall, (LANE, LANE)))[:1]

    row_b, row_c, row_s = across(cb), across(cc), across(strength)
    off_b = wrap(lax.broadcasted_iota(i32, (N, LANE), 0).astype(f32) - row_b)
    offb_ref[...] = off_b
    row_a = across(off_a)
    uab = off_b * off_b + (row_a * row_a + SOFTEN)
    uab_ref[...] = uab
    eab_ref[...] = PEAK * jnp.exp(-uab)

    def wide(ref, q):
        return jnp.broadcast_to(ref[q : q + 1, :], (8, N))

    def power(q):
        return jnp.broadcast_to(strength[q : q + 1, :], (8, N))

    close = (row_a * row_a < 16.0).astype(f32)
    lane = lax.broadcasted_iota(i32, (1, LANE), 1)
    bits = []
    for half in range(2):
        weight = jnp.where((lane >= 16 * half) & (lane < 16 * half + 16), 1, 0)
        weight = jnp.left_shift(weight, lane & 15).astype(f32)
        bits.append(jnp.sum(close * weight).astype(i32))

    def fix_charge(q):
        base = (q >> 4) * (HALF // 8)

        def one(row):
            return jnp.sum(jnp.where(lane == q, row, 0.0), axis=1, keepdims=True)

        da, cb_one, cc_one, strong = one(row_a), one(row_b), one(row_c), one(row_s)
        dc = wrap(lax.broadcasted_iota(i32, (8, N), 1).astype(f32) - cc_one)
        rest = dc * dc + (da * da + SOFTEN)
        row = lax.broadcasted_iota(i32, (8, N), 0).astype(f32)
        first = jnp.floor((jnp.sum(cb_one) - 16.0) * 0.125).astype(i32)

        def fix(step, _):
            group = first + step
            group = jnp.where(group < 0, group + N // 8, group)
            group = jnp.where(group >= N // 8, group - N // 8, group)
            i = group - base

            @pl.when((i >= 0) & (i < HALF // 8))
            def _():
                r = pl.ds(pl.multiple_of(8 * group, 8), 8)
                db = wrap(row + ((8 * group).astype(f32) - cb_one))
                u = db * db + rest
                k = lax.rsqrt(u)
                full = erf(u * k) * k
                slope = k * k * (PEAK * jnp.exp(-u) - full)
                slope_ref[q, pl.ds(pl.multiple_of(8 * i, 8), 8), :] = slope
                pot_ref[r, :] += strong * (full - k)

            return 0

        lax.fori_loop(0, 6, fix, 0)

    copies = []
    for a in range(0, 16, 2):
        for half in range(2):
            pair = (16 * half + a, 16 * half + a + 1)
            lanes = [(q, wide(uc_ref, q), wide(ec_ref, q), power(q)) for q in pair]
            for i in range(HALF // 8):
                r = slice(half * HALF + 8 * i, half * HALF + 8 * i + 8)
                total = None
                for q, ucq, ecq, strong in lanes:
                    k = lax.rsqrt(uab_ref[r, q : q + 1] + ucq)
                    e = eab_ref[r, q : q + 1] * ecq
                    slope_ref[q, 8 * i : 8 * i + 8, :] = k * k * (e - k)
                    total = strong * k if total is None else total + strong * k
                pot_ref[r, :] = total if a == 0 else pot_ref[r, :] + total
        found = [jnp.right_shift(value, a) & 3 for value in bits]
        found = found[0] + 4 * found[1]

        @pl.when(found > 0)
        def _(a=a, found=found):
            def visit(j, _):
                @pl.when((jnp.right_shift(found, j) & 1) > 0)
                def _():
                    fix_charge(16 * (j >> 1) + a + (j & 1))

                return 0

            lax.fori_loop(0, 4, visit, 0)

        for q in (a, a + 1, 16 + a, 17 + a):
            copy = pltpu.make_async_copy(slope_ref.at[q], slope_out.at[q], sems.at[q])
            copy.start()
            copies.append(copy)
    for copy in copies:
        copy.wait()


def grid_kernel(
    plan_s,
    recv_ref,
    owner_ref,
    gb_ref,
    gc_ref,
    table_ref,
    pot_ref,
    slope_in,
    offb_ref,
    offc_ref,
    col_ref,
    field_out,
    push_ref,
    acc_ref,
    tab_ref,
    flow_ref,
    edge_ref,
    pass_ref,
    mid_ref,
    dens_ref,
    sum_ref,
    field_ref,
    slope_ref,
    merged_ref,
    sems,
):
    slope_copy = pltpu.make_async_copy(slope_in, slope_ref, sems.at[1])
    slope_copy.start()
    pairs = merged_ref.shape[0]
    merged_ref[...] = jnp.where(owner_ref[...] > 0.0, recv_ref[:pairs], recv_ref[pairs:])
    def counter(rows):
        return lax.broadcasted_iota(i32, (rows, LANE), 0).astype(f32).astype(bf16)

    iota_b, iota_c = counter(WINDOW), counter(LANE)
    zero = jnp.zeros((WINDOW, LANE), bf16)
    one_c, zero_c = jnp.ones((LANE, LANE), bf16), jnp.zeros((LANE, LANE), bf16)

    def product(tile, group_b, group_c):
        columns, weights = [], []
        for j in range(TILE_CHUNKS):
            pair = tile * (TILE_CHUNKS // 4) + j // 4
            piece = j % 4
            gb = gb_ref[piece, pl.ds(pair, 1), :]
            gc = gc_ref[piece, pl.ds(pair, 1), :]
            parts = [None] * 4
            for part in range(2):
                value = merged_ref[pair, 4 * part + piece : 4 * part + piece + 1, :]
                parts[part], parts[2 + part] = halves(value)
            hots = []
            for h in range(2):
                band = (LANE * plan_s[8 + 2 * group_c + h]).astype(f32)
                hots.append(jnp.where(iota_c == (gc - band).astype(bf16), one_c, zero_c))
            weights.append(jnp.concatenate(hots, axis=0))
            hit = iota_b == (gb - WINDOW * jnp.asarray(group_b).astype(f32)).astype(bf16)
            columns.append(jnp.concatenate([jnp.where(hit, v, zero) for v in parts], axis=0))
        return mm(jnp.concatenate(columns, axis=1), jnp.concatenate(weights, axis=1), NT)

    acc_ref[0] = jnp.zeros(acc_ref.shape[1:], f32)
    def step(t, _):
        acc_ref[0] += product(t, 0, 0)
        return 0

    steps = 4 * pairs // TILE_CHUNKS
    lax.fori_loop(0, steps, step, 0)

    def rest(combo, _):
        group_b, group_c = combo >> 1, combo & 1

        @pl.when((group_b < plan_s[1]) & (group_c < plan_s[2]))
        def _():
            acc_ref[combo] = jnp.zeros(acc_ref.shape[1:], f32)

            def extra(t, _):
                acc_ref[combo] += product(t, group_b, group_c)
                return 0

            lax.fori_loop(0, steps, extra, 0)

        return 0

    lax.fori_loop(1, 4, rest, 0)

    def transform(group_b):
        def along(group_c, first):
            for level in range(2):
                for h in range(2):
                    band = jnp.minimum(plan_s[8 + 2 * group_c + h], 2) * LANE
                    base = 2 * level * N
                    cos = table_ref[pl.ds(pl.multiple_of(base + band, LANE), LANE), :]
                    sin = table_ref[pl.ds(pl.multiple_of(base + N + band, LANE), LANE), :]
                    top = slice(h * LANE, (h + 1) * LANE)
                    bottom = slice((2 + h) * LANE, (3 + h) * LANE)
                    tab_ref[level, top, :N] = cos
                    tab_ref[level, top, N:] = sin
                    tab_ref[level, bottom, :N] = -sin
                    tab_ref[level, bottom, N:] = cos
            combo = 2 * group_b + group_c
            for k in range(4):
                top = (k // 2) * WINDOW
                flow_ref[top : top + WINDOW, (k % 2) * 2 * LANE : (k % 2 + 1) * 2 * LANE] = acc_ref[
                    combo, k * WINDOW : (k + 1) * WINDOW, :
                ].astype(bf16)
            half = WINDOW
            both = mm(flow_ref[...], tab_ref[0])
            result = both[:half] + both[half:] + mm(flow_ref[:half], tab_ref[1])
            pass_ref[...] = result if first else pass_ref[...] + result

        along(0, True)

        @pl.when(plan_s[2] > 1)
        def _():
            along(1, False)

        for j in range(WINDOW // 16):
            block = plan_s[3] + (group_b * WINDOW) // 16 + j
            block = jnp.where(block >= BLOCKS, block - BLOCKS, block)
            for k in range(4):
                row = pl.multiple_of(k * N + 16 * block, 16)
                edge_ref[16 * j : 16 * j + 16, k * N : (k + 1) * N] = table_ref[pl.ds(row, 16), :]
        high, low = halves(pass_ref[...])
        result = mm(edge_ref[:, : 2 * N], high, TN) + (
            mm(edge_ref[:, 2 * N :], high, TN) + mm(edge_ref[:, : 2 * N], low, TN)
        )
        mid_ref[...] = result if group_b == 0 else mid_ref[...] + result

    transform(0)

    @pl.when(plan_s[1] > 1)
    def _():
        transform(1)

    def finish(i, _):
        r = pl.ds(pl.multiple_of(8 * i, 8), 8)
        s = pl.ds(pl.multiple_of(N + 8 * i, 8), 8)
        real = mid_ref[r, :N] - mid_ref[s, N:]
        imag = mid_ref[s, :N] + mid_ref[r, N:]
        dens_ref[r, :] = real * real + imag * imag
        pot = pot_ref[r, :]
        field_ref[0, r, :] = pot * real
        field_ref[1, r, :] = pot * imag
        return 0

    lax.fori_loop(0, N // 8, finish, 0, unroll=8)
    field_copy = pltpu.make_async_copy(field_ref, field_out, sems.at[0])
    field_copy.start()
    slope_copy.wait()
    for q in range(32):
        base = (q // 16) * HALF
        plain = [jnp.zeros((8, LANE), f32)] * 3
        scaled = jnp.zeros((8, LANE), f32)
        for i in range(HALF // 8):
            r = slice(base + 8 * i, base + 8 * i + 8)
            w = dens_ref[r, :] * slope_ref[q, 8 * i : 8 * i + 8, :]
            w = [w[:, k * LANE : (k + 1) * LANE] for k in range(3)]
            plain = [p + v for p, v in zip(plain, w)]
            scaled = scaled + (w[0] + w[1] + w[2]) * offb_ref[r, q : q + 1]
        for k in range(3):
            sum_ref[q : q + 1, k * LANE : (k + 1) * LANE] = jnp.sum(plain[k], axis=0, keepdims=True)
        sum_ref[32 + q : 33 + q, :LANE] = jnp.sum(scaled, axis=0, keepdims=True)
    plain = sum_ref[:32, :]
    off_a = col_ref[:32, 0:1]
    scale = col_ref[:32, 1:2] * VOLUME
    push_a = off_a * jnp.sum(plain, axis=1, keepdims=True) * scale
    push_b = jnp.sum(sum_ref[32:, :LANE], axis=1, keepdims=True) * scale
    push_c = jnp.sum(plain * offc_ref[...], axis=1, keepdims=True) * scale
    packed = jnp.concatenate([push_a, push_b, push_c, 0.5 * col_ref[:32, 2:3]], axis=0)
    push_ref[...] = jnp.transpose(jnp.broadcast_to(packed, (LANE, LANE)))[:1]
    field_copy.wait()


def spread_kernel(terms_ref, out_ref):
    terms = terms_ref[...]
    sources = terms.shape[0]
    width = out_ref.shape[1] // 2
    turned = jnp.transpose(jnp.concatenate([terms, pltpu.roll(terms, LANE - 1, 1)], axis=0))
    rows = []
    for axis in range(3):
        picked = [32 * axis + 2 * k for k in range(16)]
        rows.append(jnp.concatenate([turned[r : r + 1, :] for r in picked], axis=1))
    value = jnp.concatenate(rows, axis=0)
    first = value.astype(bf16).astype(f32)
    second = (value - first).astype(bf16).astype(f32)
    third = value - first - second
    zeros = jnp.zeros((7, value.shape[1]), f32)
    parts = jnp.concatenate([first, second, third, zeros], axis=0).astype(bf16)
    iota = lax.broadcasted_iota(i32, (sources, width), 1).astype(f32).astype(bf16)
    one, zero = jnp.ones((sources, width), bf16), jnp.zeros((sources, width), bf16)
    hots = []
    for q in range(32):
        number = terms[:, 96 + q : 97 + q]
        hot = []
        for half in range(2):
            wide = jnp.broadcast_to(number - half * width, (sources, width)).astype(bf16)
            hot.append(jnp.where(iota == wide, one, zero))
        hots.append(jnp.concatenate(hot, axis=1))
    result = mm(parts, jnp.concatenate(hots, axis=0))
    out_ref[...] = result[0:3] + result[3:6] + result[6:9]


def vmem(count):
    return [pl.BlockSpec(memory_space=pltpu.VMEM)] * count


def smem(count):
    return [pl.BlockSpec(memory_space=pltpu.SMEM)] * count


def anywhere(count):
    return [pl.BlockSpec(memory_space=pltpu.HBM)] * count


def params(mebibytes):
    return pltpu.CompilerParams(vmem_limit_bytes=mebibytes * 1024 * 1024)


def local(coefficients, col_map, charge_cell, charge_frac, charge, tile_list):
    slots = coefficients.shape[2]
    sources = lax.axis_size("pw")
    planes = sources
    first_table, second_table = tables(planes)

    sent = pl.pallas_call(
        columns_kernel,
        out_shape=jax.ShapeDtypeStruct((planes, 8, LANE), f32),
        in_specs=anywhere(2),
        out_specs=vmem(1)[0],
        scratch_shapes=[
            pltpu.VMEM((2, slots, N), f32),
            pltpu.VMEM(first_table.shape, bf16),
            pltpu.VMEM((4 * LANE, 2 * N), bf16),
            pltpu.VMEM((4 * LANE, 2 * N), bf16),
            pltpu.SemaphoreType.DMA((5,)),
        ],
        compiler_params=params(54),
        name="columns",
    )(coefficients.reshape(2, slots, N), jnp.asarray(first_table))
    own = tile_list[0]
    other = lax.ppermute(own, "mm", [(0, 1), (1, 0)])
    first = lax.axis_index("mm") == 0
    listed = jnp.concatenate([jnp.where(first, own, other), jnp.where(first, other, own)])

    recv = lax.all_to_all(sent, "pw", 0, 0, tiled=True)

    blocks = col_map.reshape(sources, slots)
    grid = jnp.pad(blocks, ((0, 0), (0, 4 * LANE - slots)), constant_values=EMPTY)

    pot, slope, offb, offc, col, gb, gc, owner, plan = pl.pallas_call(
        charges_kernel,
        out_shape=(
            jax.ShapeDtypeStruct((N, N), f32),
            pltpu.HBM((32, HALF, N), f32),
            jax.ShapeDtypeStruct((N, LANE), f32),
            jax.ShapeDtypeStruct((32, N), f32),
            jax.ShapeDtypeStruct((32, 8), f32),
            jax.ShapeDtypeStruct((4, sources // 2, LANE), f32),
            jax.ShapeDtypeStruct((4, sources // 2, LANE), f32),
            jax.ShapeDtypeStruct((sources // 2, 8, LANE), f32),
            jax.ShapeDtypeStruct((16,), i32),
        ),
        in_specs=vmem(5),
        out_specs=tuple(vmem(1) + anywhere(1) + vmem(6) + smem(1)),
        scratch_shapes=[
            pltpu.VMEM((N, LANE), f32),
            pltpu.VMEM((N, LANE), f32),
            pltpu.VMEM((32, N), f32),
            pltpu.VMEM((32, N), f32),
            pltpu.VMEM((32, HALF, N), f32),
            pltpu.SemaphoreType.DMA((32,)),
        ],
        compiler_params=params(50),
        name="charges",
    )(
        listed[:, None],
        charge_cell,
        charge_frac,
        charge[None],
        grid,
    )

    field, push = pl.pallas_call(
        grid_kernel,
        out_shape=(
            jax.ShapeDtypeStruct((2, N, N), f32),
            jax.ShapeDtypeStruct((1, LANE), f32),
        ),
        in_specs=smem(1) + vmem(6) + anywhere(1) + vmem(3),
        out_specs=tuple(anywhere(1) + vmem(1)),
        scratch_shapes=[
            pltpu.VMEM((4, 4 * WINDOW, 2 * LANE), f32),
            pltpu.VMEM((2, 4 * LANE, 2 * N), bf16),
            pltpu.VMEM((2 * WINDOW, 4 * LANE), bf16),
            pltpu.VMEM((WINDOW, 4 * N), bf16),
            pltpu.VMEM((WINDOW, 2 * N), f32),
            pltpu.VMEM((2 * N, 2 * N), f32),
            pltpu.VMEM((N, N), f32),
            pltpu.VMEM((64, N), f32),
            pltpu.VMEM((2, N, N), f32),
            pltpu.VMEM((32, HALF, N), f32),
            pltpu.VMEM((sources // 2, 8, LANE), f32),
            pltpu.SemaphoreType.DMA((2,)),
        ],
        compiler_params=params(50),
        name="grid",
    )(plan, recv, owner, gb, gc, jnp.asarray(second_table), pot, slope, offb, offc, col)

    push = push + lax.ppermute(push, "mm", [(0, 1), (1, 0)])
    terms = lax.all_to_all(
        jnp.broadcast_to(push[None], (sources, 1, LANE)), "pw", 0, 0, tiled=True
    ).reshape(sources, LANE)
    forces = pl.pallas_call(
        spread_kernel,
        out_shape=jax.ShapeDtypeStruct((3, charge.shape[0]), f32),
        in_specs=vmem(1),
        out_specs=vmem(1)[0],
        compiler_params=params(12),
        name="spread",
    )(terms)
    return (field[:, None, None], forces)


def solution(mesh):
    placed = (P(None, "mm", "pw", None), P(), P(), P(), P(), P(("pw", "mm"), None))
    return jax.shard_map(
        local,
        mesh=mesh,
        in_specs=placed,
        out_specs=(P(None, "mm", "pw", None, None), P()),
        check_vma=False,
    )
```

```python
import functools
import math

import jax
import jax.numpy as jnp
import ml_dtypes
import numpy as np
from jax import lax
from jax.experimental import pallas as pl
from jax.experimental.pallas import tpu as pltpu
from jax.sharding import PartitionSpec as P

f32, bf16, i32 = jnp.float32, jnp.bfloat16, jnp.int32
N = 384
HALF = 192
LANE = 128
SPACING = 0.25
SOFTEN = 0.09
VOLUME = SPACING**3
PEAK = 2.0 / math.sqrt(math.pi)
EMPTY = N * N
TILE_CHUNKS = 64
WINDOW = 208
BLOCKS = N // 16
NT = (((1,), (1,)), ((), ()))
TN = (((0,), (0,)), ((), ()))


def split_table(table):
    high = table.astype(np.float32).astype(ml_dtypes.bfloat16)
    low = (table - high.astype(np.float64)).astype(np.float32).astype(ml_dtypes.bfloat16)
    return high, low


def tables(planes):
    index = np.arange(N, dtype=np.int64)
    angle = 2.0 * np.pi / N * ((index[:, None] * index[None, :]) % N).astype(np.float64)
    cos, sin = np.cos(angle), np.sin(angle)
    cz, sz = cos[:planes], sin[:planes]
    first = np.block([[cz, -sz], [sz, cz]])
    first_high, first_low = split_table(first)
    cos_high, cos_low = split_table(cos)
    sin_high, sin_low = split_table(sin)
    return (
        np.concatenate([first_high, first_low], axis=0),
        np.concatenate([cos_high, sin_high, cos_low, sin_low], axis=0),
    )


def mm(a, b, dims=(((1,), (0,)), ((), ()))):
    return lax.dot_general(a, b, dims, preferred_element_type=f32)


def halves(value):
    high = value.astype(bf16)
    low = (value - high.astype(f32)).astype(bf16)
    return high, low


def flip_table(length):
    row = lax.broadcasted_iota(i32, (length, length), 0)
    column = lax.broadcasted_iota(i32, (length, length), 1)
    return jnp.where(row + column == length - 1, 1.0, 0.0).astype(bf16)


def columns_kernel(
    coef_in, table_in, out_ref, coef_ref, table_ref, high_ref, low_ref, sems
):
    slots = coef_ref.shape[1]
    half = slots // 2
    copies = []
    for part in range(2):
        for piece in range(2):
            cut = pl.ds(piece * half, half)
            copies.append(
                pltpu.make_async_copy(
                    coef_in.at[part, cut], coef_ref.at[part, cut], sems.at[2 * part + piece]
                )
            )
    copies.append(pltpu.make_async_copy(table_in, table_ref, sems.at[4]))
    for copy in copies:
        copy.start()
    width = high_ref.shape[0]
    planes = out_ref.shape[0]
    high_ref[slots:, :] = jnp.zeros((width - slots, 2 * N), bf16)
    low_ref[slots:, :] = jnp.zeros((width - slots, 2 * N), bf16)
    for part in range(2):
        for piece in range(2):
            copies[2 * part + piece].wait()
            rows = slice(piece * half, (piece + 1) * half)
            high, low = halves(coef_ref[part, rows])
            high_ref[rows, part * N : (part + 1) * N] = high
            low_ref[rows, part * N : (part + 1) * N] = low
    copies[4].wait()
    rows = 2 * planes
    both = mm(table_ref[...], high_ref[...], NT)
    result = both[:rows] + both[rows:] + mm(table_ref[:rows], low_ref[...], NT)

    def put(values):
        for part in range(2):
            for piece in range(4):
                out_ref[:, 4 * part + piece, :] = values[
                    part * planes : (part + 1) * planes, piece * LANE : (piece + 1) * LANE
                ]

    reverse = lax.axis_index("pw") < planes // 2

    @pl.when(jnp.logical_not(reverse))
    def _():
        put(result)

    @pl.when(reverse)
    def _():
        high, low = halves(result)
        flip = flip_table(width)
        put(mm(high, flip) + mm(low, flip))


def wrap(offset):
    shifted = offset + HALF
    shifted = jnp.where(shifted < 0, shifted + N, shifted)
    shifted = jnp.where(shifted >= N, shifted - N, shifted)
    return SPACING * (shifted - HALF)


ERF_NUM = (
    -2.72614225801306e-10,
    2.77068142495902e-08,
    -2.10102402082508e-06,
    -5.69250639462346e-05,
    -7.34990630326855e-04,
    -2.95459980854025e-03,
    -1.60960333262415e-02,
)
ERF_DEN = (
    -1.45660718464996e-05,
    -2.13374055278905e-04,
    -1.68282697438203e-03,
    -7.37332916720468e-03,
    -1.42647390514189e-02,
)


def erf(s):
    s = jnp.minimum(s, 4.0)
    sq = s * s
    num = jnp.full_like(s, ERF_NUM[0])
    for c in ERF_NUM[1:]:
        num = num * sq + c
    den = jnp.full_like(s, ERF_DEN[0])
    for c in ERF_DEN[1:]:
        den = den * sq + c
    return s * num / den


def charges_kernel(
    list_ref,
    cell_ref,
    frac_ref,
    charge_ref,
    grid_ref,
    pot_ref,
    slope_out,
    offb_ref,
    offc_ref,
    col_ref,
    gb_ref,
    gc_ref,
    owner_ref,
    plan_s,
    uab_ref,
    eab_ref,
    uc_ref,
    ec_ref,
    slope_ref,
    sems,
):
    cells = grid_ref[...]
    pairs = cells.shape[0] // 2
    row = jnp.floor((cells.astype(f32) + 0.5) * (1.0 / N))
    gb = jnp.where(cells < EMPTY, row, -1000.0)
    gc = jnp.where(cells < EMPTY, cells.astype(f32) - N * row, -1000.0)
    high, low = halves(jnp.concatenate([gb[:pairs], gc[:pairs]], axis=0))
    flip = flip_table(cells.shape[1])
    turned = mm(high, flip) + mm(low, flip)
    owned = jnp.where(turned[:pairs] >= 0.0, 1.0, 0.0)
    for piece in range(4):
        cut = slice(piece * LANE, (piece + 1) * LANE)
        owner_ref[:, piece, :] = owned[:, cut]
        owner_ref[:, 4 + piece, :] = owned[:, cut]
    merged_b = jnp.maximum(gb[pairs:], turned[:pairs])
    merged_c = jnp.maximum(gc[pairs:], turned[pairs:])
    found = jnp.int32(0)
    for band in range(3):
        inside = (merged_c >= band * LANE) & (merged_c < (band + 1) * LANE)
        plan_s[8 + found] = jnp.int32(band)
        found = found + jnp.max(jnp.where(inside, 1.0, 0.0)).astype(i32)
    for slot in range(4):
        plan_s[8 + slot] = jnp.where(slot < found, plan_s[8 + slot], 3)
    plan_s[2] = (found + 1) // 2
    alive = merged_b >= 0.0
    block = jnp.where(alive, merged_b * (1.0 / 16.0), 0.0).astype(i32)
    used = jnp.left_shift(jnp.where(alive, 1, 0), block)
    while used.shape[0] > 8:
        used = used[: used.shape[0] // 2] | used[used.shape[0] // 2 :]
    while used.shape[1] > LANE:
        used = used[:, : used.shape[1] // 2] | used[:, used.shape[1] // 2 :]
    for axis, width in ((0, 8), (1, LANE)):
        shift = width // 2
        while shift:
            used = used | pltpu.roll(used, shift, axis)
            shift //= 2
    occupied = jnp.max(used.astype(f32)).astype(i32)
    start = jnp.int32(-1)
    for k in range(BLOCKS):
        outside = sum(1 << ((k + j) % BLOCKS) for j in range(WINDOW // 16, BLOCKS))
        start = jnp.where((occupied & outside) == 0, k, start)
    plan_s[1] = jnp.where(start < 0, 2, 1)
    start = jnp.maximum(start, 0)
    plan_s[3] = start
    shifted = merged_b - (16 * start).astype(f32)
    shifted = jnp.where(shifted < 0.0, shifted + N, shifted)
    shifted = jnp.where(alive, shifted, -1000.0)
    for values, out in ((shifted, gb_ref), (merged_c, gc_ref)):
        for piece in range(4):
            out[piece] = values[:, piece * LANE : (piece + 1) * LANE]

    listed = list_ref[...]
    mask = lax.broadcasted_iota(i32, (32, cell_ref.shape[1]), 1) == listed
    center = cell_ref[...].astype(f32) + frac_ref[...]

    def pick(row):
        return jnp.sum(jnp.where(mask, row, 0.0), axis=1, keepdims=True)

    ca, cb, cc = (pick(center[i : i + 1]) for i in range(3))
    strength = pick(charge_ref[...])
    plane = lax.axis_index("pw").astype(f32)
    off_a = wrap(plane - ca)
    col_ref[...] = jnp.concatenate(
        [off_a, strength, listed.astype(f32)] + [jnp.zeros((32, 5), f32)], axis=1
    )
    off_c = wrap(lax.broadcasted_iota(i32, (32, N), 1).astype(f32) - cc)
    offc_ref[...] = off_c
    sq_c = off_c * off_c
    uc_ref[...] = sq_c
    ec_ref[...] = jnp.exp(-sq_c)

    def across(column):
        tall = jnp.concatenate([column, jnp.zeros((LANE - 32, 1), f32)], axis=0)
        return jnp.transpose(jnp.broadcast_to(tall, (LANE, LANE)))[:1]

    row_b, row_c, row_s = across(cb), across(cc), across(strength)
    off_b = wrap(lax.broadcasted_iota(i32, (N, LANE), 0).astype(f32) - row_b)
    offb_ref[...] = off_b
    row_a = across(off_a)
    uab = off_b * off_b + (row_a * row_a + SOFTEN)
    uab_ref[...] = uab
    eab_ref[...] = PEAK * jnp.exp(-uab)

    def wide(ref, q):
        return jnp.broadcast_to(ref[q : q + 1, :], (8, N))

    def power(q):
        return jnp.broadcast_to(strength[q : q + 1, :], (8, N))

    close = (row_a * row_a < 16.0).astype(f32)
    lane = lax.broadcasted_iota(i32, (1, LANE), 1)
    bits = []
    for half in range(2):
        weight = jnp.where((lane >= 16 * half) & (lane < 16 * half + 16), 1, 0)
        weight = jnp.left_shift(weight, lane & 15).astype(f32)
        bits.append(jnp.sum(close * weight).astype(i32))

    def fix_charge(q):
        base = (q >> 4) * (HALF // 8)

        def one(row):
            return jnp.sum(jnp.where(lane == q, row, 0.0), axis=1, keepdims=True)

        da, cb_one, cc_one, strong = one(row_a), one(row_b), one(row_c), one(row_s)
        dc = wrap(lax.broadcasted_iota(i32, (8, N), 1).astype(f32) - cc_one)
        rest = dc * dc + (da * da + SOFTEN)
        local = jnp.floor((jnp.sum(cb_one) - 16.0) * 0.125).astype(i32) - base
        local = jnp.where(local < -5, local + N // 8, local)
        local = jnp.where(local >= N // 8 - 5, local - N // 8, local)

        @pl.when(local < HALF // 8)
        def _():
            i = jnp.clip(local, 0, HALF // 8 - 6)
            row = lax.broadcasted_iota(i32, (48, N), 0).astype(f32)
            db = wrap(row + ((8 * (base + i)).astype(f32) - cb_one))
            u = db * db + rest[:1]
            k = lax.rsqrt(u)
            full = erf(u * k) * k
            rows = pl.ds(pl.multiple_of(8 * i, 8), 48)
            slope_ref[q, rows, :] = k * k * (PEAK * jnp.exp(-u) - full)
            pot_ref[pl.ds(pl.multiple_of(8 * (base + i), 8), 48), :] += strong * (full - k)

    copies = []
    for a in range(0, 16, 2):
        for half in range(2):
            pair = (16 * half + a, 16 * half + a + 1)
            lanes = [(q, wide(uc_ref, q), wide(ec_ref, q), power(q)) for q in pair]
            for i in range(HALF // 8):
                r = slice(half * HALF + 8 * i, half * HALF + 8 * i + 8)
                total = None
                for q, ucq, ecq, strong in lanes:
                    k = lax.rsqrt(uab_ref[r, q : q + 1] + ucq)
                    e = eab_ref[r, q : q + 1] * ecq
                    slope_ref[q, 8 * i : 8 * i + 8, :] = k * k * (e - k)
                    total = strong * k if total is None else total + strong * k
                pot_ref[r, :] = total if a == 0 else pot_ref[r, :] + total
        found = [jnp.right_shift(value, a) & 3 for value in bits]
        found = found[0] + 4 * found[1]

        @pl.when(found > 0)
        def _(a=a, found=found):
            def visit(j, _):
                @pl.when((jnp.right_shift(found, j) & 1) > 0)
                def _():
                    fix_charge(16 * (j >> 1) + a + (j & 1))

                return 0

            lax.fori_loop(0, 4, visit, 0)

        for q in (a, a + 1, 16 + a, 17 + a):
            copy = pltpu.make_async_copy(slope_ref.at[q], slope_out.at[q], sems.at[q])
            copy.start()
            copies.append(copy)
    for copy in copies:
        copy.wait()


def grid_kernel(
    plan_s,
    recv_ref,
    owner_ref,
    gb_ref,
    gc_ref,
    table_ref,
    pot_ref,
    slope_in,
    offb_ref,
    offc_ref,
    col_ref,
    field_out,
    push_ref,
    acc_ref,
    tab_ref,
    flow_ref,
    edge_ref,
    pass_ref,
    mid_ref,
    dens_ref,
    sum_ref,
    field_ref,
    slope_ref,
    merged_ref,
    sems,
):
    slope_copy = pltpu.make_async_copy(slope_in, slope_ref, sems.at[1])
    slope_copy.start()
    pairs = merged_ref.shape[0]
    merged_ref[...] = jnp.where(owner_ref[...] > 0.0, recv_ref[:pairs], recv_ref[pairs:])
    def counter(rows):
        return lax.broadcasted_iota(i32, (rows, LANE), 0).astype(f32).astype(bf16)

    iota_b, iota_c = counter(WINDOW), counter(LANE)
    zero = jnp.zeros((WINDOW, LANE), bf16)
    one_c, zero_c = jnp.ones((LANE, LANE), bf16), jnp.zeros((LANE, LANE), bf16)

    def product(tile, group_b, group_c):
        columns, weights = [], []
        for j in range(TILE_CHUNKS):
            pair = tile * (TILE_CHUNKS // 4) + j // 4
            piece = j % 4
            gb = gb_ref[piece, pl.ds(pair, 1), :]
            gc = gc_ref[piece, pl.ds(pair, 1), :]
            parts = [None] * 4
            for part in range(2):
                value = merged_ref[pair, 4 * part + piece : 4 * part + piece + 1, :]
                parts[part], parts[2 + part] = halves(value)
            hots = []
            for h in range(2):
                band = (LANE * plan_s[8 + 2 * group_c + h]).astype(f32)
                hots.append(jnp.where(iota_c == (gc - band).astype(bf16), one_c, zero_c))
            weights.append(jnp.concatenate(hots, axis=0))
            hit = iota_b == (gb - WINDOW * jnp.asarray(group_b).astype(f32)).astype(bf16)
            columns.append(jnp.concatenate([jnp.where(hit, v, zero) for v in parts], axis=0))
        return mm(jnp.concatenate(columns, axis=1), jnp.concatenate(weights, axis=1), NT)

    acc_ref[0] = jnp.zeros(acc_ref.shape[1:], f32)
    def step(t, _):
        acc_ref[0] += product(t, 0, 0)
        return 0

    steps = 4 * pairs // TILE_CHUNKS
    lax.fori_loop(0, steps, step, 0)

    def rest(combo, _):
        group_b, group_c = combo >> 1, combo & 1

        @pl.when((group_b < plan_s[1]) & (group_c < plan_s[2]))
        def _():
            acc_ref[combo] = jnp.zeros(acc_ref.shape[1:], f32)

            def extra(t, _):
                acc_ref[combo] += product(t, group_b, group_c)
                return 0

            lax.fori_loop(0, steps, extra, 0)

        return 0

    lax.fori_loop(1, 4, rest, 0)

    def transform(group_b):
        def along(group_c, first):
            for level in range(2):
                for h in range(2):
                    band = jnp.minimum(plan_s[8 + 2 * group_c + h], 2) * LANE
                    base = 2 * level * N
                    cos = table_ref[pl.ds(pl.multiple_of(base + band, LANE), LANE), :]
                    sin = table_ref[pl.ds(pl.multiple_of(base + N + band, LANE), LANE), :]
                    top = slice(h * LANE, (h + 1) * LANE)
                    bottom = slice((2 + h) * LANE, (3 + h) * LANE)
                    tab_ref[level, top, :N] = cos
                    tab_ref[level, top, N:] = sin
                    tab_ref[level, bottom, :N] = -sin
                    tab_ref[level, bottom, N:] = cos
            combo = 2 * group_b + group_c
            for k in range(4):
                top = (k // 2) * WINDOW
                flow_ref[top : top + WINDOW, (k % 2) * 2 * LANE : (k % 2 + 1) * 2 * LANE] = acc_ref[
                    combo, k * WINDOW : (k + 1) * WINDOW, :
                ].astype(bf16)
            half = WINDOW
            both = mm(flow_ref[...], tab_ref[0])
            result = both[:half] + both[half:] + mm(flow_ref[:half], tab_ref[1])
            pass_ref[...] = result if first else pass_ref[...] + result

        along(0, True)

        @pl.when(plan_s[2] > 1)
        def _():
            along(1, False)

        for j in range(WINDOW // 16):
            block = plan_s[3] + (group_b * WINDOW) // 16 + j
            block = jnp.where(block >= BLOCKS, block - BLOCKS, block)
            for k in range(4):
                row = pl.multiple_of(k * N + 16 * block, 16)
                edge_ref[16 * j : 16 * j + 16, k * N : (k + 1) * N] = table_ref[pl.ds(row, 16), :]
        high, low = halves(pass_ref[...])
        result = mm(edge_ref[:, : 2 * N], high, TN) + (
            mm(edge_ref[:, 2 * N :], high, TN) + mm(edge_ref[:, : 2 * N], low, TN)
        )
        mid_ref[...] = result if group_b == 0 else mid_ref[...] + result

    transform(0)

    @pl.when(plan_s[1] > 1)
    def _():
        transform(1)

    def finish(i, _):
        r = pl.ds(pl.multiple_of(8 * i, 8), 8)
        s = pl.ds(pl.multiple_of(N + 8 * i, 8), 8)
        real = mid_ref[r, :N] - mid_ref[s, N:]
        imag = mid_ref[s, :N] + mid_ref[r, N:]
        dens_ref[r, :] = real * real + imag * imag
        pot = pot_ref[r, :]
        field_ref[0, r, :] = pot * real
        field_ref[1, r, :] = pot * imag
        return 0

    lax.fori_loop(0, N // 8, finish, 0, unroll=8)
    field_copy = pltpu.make_async_copy(field_ref, field_out, sems.at[0])
    field_copy.start()
    slope_copy.wait()
    for q in range(32):
        base = (q // 16) * HALF
        plain = [jnp.zeros((8, LANE), f32)] * 3
        scaled = jnp.zeros((8, LANE), f32)
        for i in range(HALF // 8):
            r = slice(base + 8 * i, base + 8 * i + 8)
            w = dens_ref[r, :] * slope_ref[q, 8 * i : 8 * i + 8, :]
            w = [w[:, k * LANE : (k + 1) * LANE] for k in range(3)]
            plain = [p + v for p, v in zip(plain, w)]
            scaled = scaled + (w[0] + w[1] + w[2]) * offb_ref[r, q : q + 1]
        for k in range(3):
            sum_ref[q : q + 1, k * LANE : (k + 1) * LANE] = jnp.sum(plain[k], axis=0, keepdims=True)
        sum_ref[32 + q : 33 + q, :LANE] = jnp.sum(scaled, axis=0, keepdims=True)
    plain = sum_ref[:32, :]
    off_a = col_ref[:32, 0:1]
    scale = col_ref[:32, 1:2] * VOLUME
    push_a = off_a * jnp.sum(plain, axis=1, keepdims=True) * scale
    push_b = jnp.sum(sum_ref[32:, :LANE], axis=1, keepdims=True) * scale
    push_c = jnp.sum(plain * offc_ref[...], axis=1, keepdims=True) * scale
    packed = jnp.concatenate([push_a, push_b, push_c, 0.5 * col_ref[:32, 2:3]], axis=0)
    push_ref[...] = jnp.transpose(jnp.broadcast_to(packed, (LANE, LANE)))[:1]
    field_copy.wait()


def spread_kernel(terms_ref, out_ref):
    terms = terms_ref[...]
    sources = terms.shape[0]
    width = out_ref.shape[1] // 2
    turned = jnp.transpose(jnp.concatenate([terms, pltpu.roll(terms, LANE - 1, 1)], axis=0))
    rows = []
    for axis in range(3):
        picked = [32 * axis + 2 * k for k in range(16)]
        rows.append(jnp.concatenate([turned[r : r + 1, :] for r in picked], axis=1))
    value = jnp.concatenate(rows, axis=0)
    first = value.astype(bf16).astype(f32)
    second = (value - first).astype(bf16).astype(f32)
    third = value - first - second
    zeros = jnp.zeros((7, value.shape[1]), f32)
    parts = jnp.concatenate([first, second, third, zeros], axis=0).astype(bf16)
    iota = lax.broadcasted_iota(i32, (sources, width), 1).astype(f32).astype(bf16)
    one, zero = jnp.ones((sources, width), bf16), jnp.zeros((sources, width), bf16)
    hots = []
    for q in range(32):
        number = terms[:, 96 + q : 97 + q]
        hot = []
        for half in range(2):
            wide = jnp.broadcast_to(number - half * width, (sources, width)).astype(bf16)
            hot.append(jnp.where(iota == wide, one, zero))
        hots.append(jnp.concatenate(hot, axis=1))
    result = mm(parts, jnp.concatenate(hots, axis=0))
    out_ref[...] = result[0:3] + result[3:6] + result[6:9]


def vmem(count):
    return [pl.BlockSpec(memory_space=pltpu.VMEM)] * count


def smem(count):
    return [pl.BlockSpec(memory_space=pltpu.SMEM)] * count


def anywhere(count):
    return [pl.BlockSpec(memory_space=pltpu.HBM)] * count


def params(mebibytes):
    return pltpu.CompilerParams(vmem_limit_bytes=mebibytes * 1024 * 1024)


def local(coefficients, col_map, charge_cell, charge_frac, charge, tile_list):
    slots = coefficients.shape[2]
    sources = lax.axis_size("pw")
    planes = sources
    first_table, second_table = tables(planes)

    sent = pl.pallas_call(
        columns_kernel,
        out_shape=jax.ShapeDtypeStruct((planes, 8, LANE), f32),
        in_specs=anywhere(2),
        out_specs=vmem(1)[0],
        scratch_shapes=[
            pltpu.VMEM((2, slots, N), f32),
            pltpu.VMEM(first_table.shape, bf16),
            pltpu.VMEM((4 * LANE, 2 * N), bf16),
            pltpu.VMEM((4 * LANE, 2 * N), bf16),
            pltpu.SemaphoreType.DMA((5,)),
        ],
        compiler_params=params(54),
        name="columns",
    )(coefficients.reshape(2, slots, N), jnp.asarray(first_table))
    own = tile_list[0]
    other = lax.ppermute(own, "mm", [(0, 1), (1, 0)])
    first = lax.axis_index("mm") == 0
    listed = jnp.concatenate([jnp.where(first, own, other), jnp.where(first, other, own)])

    recv = lax.all_to_all(sent, "pw", 0, 0, tiled=True)

    blocks = col_map.reshape(sources, slots)
    grid = jnp.pad(blocks, ((0, 0), (0, 4 * LANE - slots)), constant_values=EMPTY)

    pot, slope, offb, offc, col, gb, gc, owner, plan = pl.pallas_call(
        charges_kernel,
        out_shape=(
            jax.ShapeDtypeStruct((N, N), f32),
            pltpu.HBM((32, HALF, N), f32),
            jax.ShapeDtypeStruct((N, LANE), f32),
            jax.ShapeDtypeStruct((32, N), f32),
            jax.ShapeDtypeStruct((32, 8), f32),
            jax.ShapeDtypeStruct((4, sources // 2, LANE), f32),
            jax.ShapeDtypeStruct((4, sources // 2, LANE), f32),
            jax.ShapeDtypeStruct((sources // 2, 8, LANE), f32),
            jax.ShapeDtypeStruct((16,), i32),
        ),
        in_specs=vmem(5),
        out_specs=tuple(vmem(1) + anywhere(1) + vmem(6) + smem(1)),
        scratch_shapes=[
            pltpu.VMEM((N, LANE), f32),
            pltpu.VMEM((N, LANE), f32),
            pltpu.VMEM((32, N), f32),
            pltpu.VMEM((32, N), f32),
            pltpu.VMEM((32, HALF, N), f32),
            pltpu.SemaphoreType.DMA((32,)),
        ],
        compiler_params=params(50),
        name="charges",
    )(
        listed[:, None],
        charge_cell,
        charge_frac,
        charge[None],
        grid,
    )

    field, push = pl.pallas_call(
        grid_kernel,
        out_shape=(
            jax.ShapeDtypeStruct((2, N, N), f32),
            jax.ShapeDtypeStruct((1, LANE), f32),
        ),
        in_specs=smem(1) + vmem(6) + anywhere(1) + vmem(3),
        out_specs=tuple(anywhere(1) + vmem(1)),
        scratch_shapes=[
            pltpu.VMEM((4, 4 * WINDOW, 2 * LANE), f32),
            pltpu.VMEM((2, 4 * LANE, 2 * N), bf16),
            pltpu.VMEM((2 * WINDOW, 4 * LANE), bf16),
            pltpu.VMEM((WINDOW, 4 * N), bf16),
            pltpu.VMEM((WINDOW, 2 * N), f32),
            pltpu.VMEM((2 * N, 2 * N), f32),
            pltpu.VMEM((N, N), f32),
            pltpu.VMEM((64, N), f32),
            pltpu.VMEM((2, N, N), f32),
            pltpu.VMEM((32, HALF, N), f32),
            pltpu.VMEM((sources // 2, 8, LANE), f32),
            pltpu.SemaphoreType.DMA((2,)),
        ],
        compiler_params=params(50),
        name="grid",
    )(plan, recv, owner, gb, gc, jnp.asarray(second_table), pot, slope, offb, offc, col)

    push = push + lax.ppermute(push, "mm", [(0, 1), (1, 0)])
    terms = lax.all_to_all(
        jnp.broadcast_to(push[None], (sources, 1, LANE)), "pw", 0, 0, tiled=True
    ).reshape(sources, LANE)
    forces = pl.pallas_call(
        spread_kernel,
        out_shape=jax.ShapeDtypeStruct((3, charge.shape[0]), f32),
        in_specs=vmem(1),
        out_specs=vmem(1)[0],
        compiler_params=params(12),
        name="spread",
    )(terms)
    return (field[:, None, None], forces)


def solution(mesh):
    placed = (P(None, "mm", "pw", None), P(), P(), P(), P(), P(("pw", "mm"), None))
    return jax.shard_map(
        local,
        mesh=mesh,
        in_specs=placed,
        out_specs=(P(None, "mm", "pw", None, None), P()),
        check_vma=False,
    )
```

```python
import functools
import math

import jax
import jax.numpy as jnp
import ml_dtypes
import numpy as np
from jax import lax
from jax.experimental import pallas as pl
from jax.experimental.pallas import tpu as pltpu
from jax.sharding import PartitionSpec as P

f32, bf16, i32 = jnp.float32, jnp.bfloat16, jnp.int32
N = 384
HALF = 192
LANE = 128
SPACING = 0.25
SOFTEN = 0.09
VOLUME = SPACING**3
PEAK = 2.0 / math.sqrt(math.pi)
EMPTY = N * N
TILE_CHUNKS = 64
WINDOW = 208
BLOCKS = N // 16
LAST = (14, 15)
STORED = 30
NT = (((1,), (1,)), ((), ()))
TN = (((0,), (0,)), ((), ()))


def split_table(table):
    high = table.astype(np.float32).astype(ml_dtypes.bfloat16)
    low = (table - high.astype(np.float64)).astype(np.float32).astype(ml_dtypes.bfloat16)
    return high, low


def tables(planes):
    index = np.arange(N, dtype=np.int64)
    angle = 2.0 * np.pi / N * ((index[:, None] * index[None, :]) % N).astype(np.float64)
    cos, sin = np.cos(angle), np.sin(angle)
    cz, sz = cos[:planes], sin[:planes]
    first = np.block([[cz, -sz], [sz, cz]])
    first_high, first_low = split_table(first)
    cos_high, cos_low = split_table(cos)
    sin_high, sin_low = split_table(sin)
    return (
        np.concatenate([first_high, first_low], axis=0),
        np.concatenate([cos_high, sin_high, cos_low, sin_low], axis=0),
    )


def mm(a, b, dims=(((1,), (0,)), ((), ()))):
    return lax.dot_general(a, b, dims, preferred_element_type=f32)


def halves(value):
    high = value.astype(bf16)
    low = (value - high.astype(f32)).astype(bf16)
    return high, low


def flip_table(length):
    row = lax.broadcasted_iota(i32, (length, length), 0)
    column = lax.broadcasted_iota(i32, (length, length), 1)
    return jnp.where(row + column == length - 1, 1.0, 0.0).astype(bf16)


def columns_kernel(
    coef_in, table_in, out_ref, coef_ref, table_ref, high_ref, low_ref, sems
):
    slots = coef_ref.shape[1]
    half = slots // 2
    copies = []
    for part in range(2):
        for piece in range(2):
            cut = pl.ds(piece * half, half)
            copies.append(
                pltpu.make_async_copy(
                    coef_in.at[part, cut], coef_ref.at[part, cut], sems.at[2 * part + piece]
                )
            )
    copies.append(pltpu.make_async_copy(table_in, table_ref, sems.at[4]))
    for copy in copies:
        copy.start()
    width = high_ref.shape[0]
    planes = out_ref.shape[0]
    high_ref[slots:, :] = jnp.zeros((width - slots, 2 * N), bf16)
    low_ref[slots:, :] = jnp.zeros((width - slots, 2 * N), bf16)
    for part in range(2):
        for piece in range(2):
            copies[2 * part + piece].wait()
            rows = slice(piece * half, (piece + 1) * half)
            high, low = halves(coef_ref[part, rows])
            high_ref[rows, part * N : (part + 1) * N] = high
            low_ref[rows, part * N : (part + 1) * N] = low
    copies[4].wait()
    rows = 2 * planes
    both = mm(table_ref[...], high_ref[...], NT)
    result = both[:rows] + both[rows:] + mm(table_ref[:rows], low_ref[...], NT)

    def put(values):
        for part in range(2):
            for piece in range(4):
                out_ref[:, 4 * part + piece, :] = values[
                    part * planes : (part + 1) * planes, piece * LANE : (piece + 1) * LANE
                ]

    reverse = lax.axis_index("pw") < planes // 2

    @pl.when(jnp.logical_not(reverse))
    def _():
        put(result)

    @pl.when(reverse)
    def _():
        high, low = halves(result)
        flip = flip_table(width)
        put(mm(high, flip) + mm(low, flip))


def wrap(offset):
    shifted = offset + HALF
    shifted = jnp.where(shifted < 0, shifted + N, shifted)
    shifted = jnp.where(shifted >= N, shifted - N, shifted)
    return SPACING * (shifted - HALF)


ERF_NUM = (
    -2.72614225801306e-10,
    2.77068142495902e-08,
    -2.10102402082508e-06,
    -5.69250639462346e-05,
    -7.34990630326855e-04,
    -2.95459980854025e-03,
    -1.60960333262415e-02,
)
ERF_DEN = (
    -1.45660718464996e-05,
    -2.13374055278905e-04,
    -1.68282697438203e-03,
    -7.37332916720468e-03,
    -1.42647390514189e-02,
)


def erf(s):
    s = jnp.minimum(s, 4.0)
    sq = s * s
    num = jnp.full_like(s, ERF_NUM[0])
    for c in ERF_NUM[1:]:
        num = num * sq + c
    den = jnp.full_like(s, ERF_DEN[0])
    for c in ERF_DEN[1:]:
        den = den * sq + c
    return s * num / den


def place(last_ref, slope_ref, q):
    return (last_ref, q - LAST[0]) if q in LAST else (slope_ref, q - 2 * (q // 16))


def charges_kernel(
    list_ref,
    cell_ref,
    frac_ref,
    charge_ref,
    grid_ref,
    pot_ref,
    last_ref,
    slope_out,
    offb_ref,
    offc_ref,
    col_ref,
    gb_ref,
    gc_ref,
    owner_ref,
    plan_s,
    uab_ref,
    eab_ref,
    uc_ref,
    ec_ref,
    slope_ref,
    sems,
):
    cells = grid_ref[...]
    pairs = cells.shape[0] // 2
    row = jnp.floor((cells.astype(f32) + 0.5) * (1.0 / N))
    gb = jnp.where(cells < EMPTY, row, -1000.0)
    gc = jnp.where(cells < EMPTY, cells.astype(f32) - N * row, -1000.0)
    high, low = halves(jnp.concatenate([gb[:pairs], gc[:pairs]], axis=0))
    flip = flip_table(cells.shape[1])
    turned = mm(high, flip) + mm(low, flip)
    owned = jnp.where(turned[:pairs] >= 0.0, 1.0, 0.0)
    for piece in range(4):
        cut = slice(piece * LANE, (piece + 1) * LANE)
        owner_ref[:, piece, :] = owned[:, cut]
        owner_ref[:, 4 + piece, :] = owned[:, cut]
    merged_b = jnp.maximum(gb[pairs:], turned[:pairs])
    merged_c = jnp.maximum(gc[pairs:], turned[pairs:])
    found = jnp.int32(0)
    for band in range(3):
        inside = (merged_c >= band * LANE) & (merged_c < (band + 1) * LANE)
        plan_s[8 + found] = jnp.int32(band)
        found = found + jnp.max(jnp.where(inside, 1.0, 0.0)).astype(i32)
    for slot in range(4):
        plan_s[8 + slot] = jnp.where(slot < found, plan_s[8 + slot], 3)
    plan_s[2] = (found + 1) // 2
    alive = merged_b >= 0.0
    block = jnp.where(alive, merged_b * (1.0 / 16.0), 0.0).astype(i32)
    used = jnp.left_shift(jnp.where(alive, 1, 0), block)
    while used.shape[0] > 8:
        used = used[: used.shape[0] // 2] | used[used.shape[0] // 2 :]
    while used.shape[1] > LANE:
        used = used[:, : used.shape[1] // 2] | used[:, used.shape[1] // 2 :]
    for axis, width in ((0, 8), (1, LANE)):
        shift = width // 2
        while shift:
            used = used | pltpu.roll(used, shift, axis)
            shift //= 2
    occupied = jnp.max(used.astype(f32)).astype(i32)
    start = jnp.int32(-1)
    for k in range(BLOCKS):
        outside = sum(1 << ((k + j) % BLOCKS) for j in range(WINDOW // 16, BLOCKS))
        start = jnp.where((occupied & outside) == 0, k, start)
    plan_s[1] = jnp.where(start < 0, 2, 1)
    start = jnp.maximum(start, 0)
    plan_s[3] = start
    shifted = merged_b - (16 * start).astype(f32)
    shifted = jnp.where(shifted < 0.0, shifted + N, shifted)
    shifted = jnp.where(alive, shifted, -1000.0)
    for values, out in ((shifted, gb_ref), (merged_c, gc_ref)):
        for piece in range(4):
            out[piece] = values[:, piece * LANE : (piece + 1) * LANE]

    listed = list_ref[...]
    mask = lax.broadcasted_iota(i32, (32, cell_ref.shape[1]), 1) == listed
    center = cell_ref[...].astype(f32) + frac_ref[...]

    def pick(row):
        return jnp.sum(jnp.where(mask, row, 0.0), axis=1, keepdims=True)

    ca, cb, cc = (pick(center[i : i + 1]) for i in range(3))
    strength = pick(charge_ref[...])
    plane = lax.axis_index("pw").astype(f32)
    off_a = wrap(plane - ca)
    col_ref[...] = jnp.concatenate(
        [off_a, strength, listed.astype(f32)] + [jnp.zeros((32, 5), f32)], axis=1
    )
    off_c = wrap(lax.broadcasted_iota(i32, (32, N), 1).astype(f32) - cc)
    offc_ref[...] = off_c
    sq_c = off_c * off_c
    uc_ref[...] = sq_c
    ec_ref[...] = jnp.exp(-sq_c)

    def across(column):
        tall = jnp.concatenate([column, jnp.zeros((LANE - 32, 1), f32)], axis=0)
        return jnp.transpose(jnp.broadcast_to(tall, (LANE, LANE)))[:1]

    row_b, row_c, row_s = across(cb), across(cc), across(strength)
    off_b = wrap(lax.broadcasted_iota(i32, (N, LANE), 0).astype(f32) - row_b)
    offb_ref[...] = off_b
    row_a = across(off_a)
    uab = off_b * off_b + (row_a * row_a + SOFTEN)
    uab_ref[...] = uab
    eab_ref[...] = PEAK * jnp.exp(-uab)

    def wide(ref, q):
        return jnp.broadcast_to(ref[q : q + 1, :], (8, N))

    def power(q):
        return jnp.broadcast_to(strength[q : q + 1, :], (8, N))

    close = (row_a * row_a < 16.0).astype(f32)
    lane = lax.broadcasted_iota(i32, (1, LANE), 1)
    bits = []
    for half in range(2):
        weight = jnp.where((lane >= 16 * half) & (lane < 16 * half + 16), 1, 0)
        weight = jnp.left_shift(weight, lane & 15).astype(f32)
        bits.append(jnp.sum(close * weight).astype(i32))

    def fix_charge(q, target_ref, slot):
        base = (q >> 4) * (HALF // 8)

        def one(row):
            return jnp.sum(jnp.where(lane == q, row, 0.0), axis=1, keepdims=True)

        da, cb_one, cc_one, strong = one(row_a), one(row_b), one(row_c), one(row_s)
        dc = wrap(lax.broadcasted_iota(i32, (8, N), 1).astype(f32) - cc_one)
        rest = dc * dc + (da * da + SOFTEN)
        local = jnp.floor((jnp.sum(cb_one) - 16.0) * 0.125).astype(i32) - base
        local = jnp.where(local < -5, local + N // 8, local)
        local = jnp.where(local >= N // 8 - 5, local - N // 8, local)

        @pl.when(local < HALF // 8)
        def _():
            i = jnp.clip(local, 0, HALF // 8 - 6)
            row = lax.broadcasted_iota(i32, (48, N), 0).astype(f32)
            db = wrap(row + ((8 * (base + i)).astype(f32) - cb_one))
            u = db * db + rest[:1]
            k = lax.rsqrt(u)
            full = erf(u * k) * k
            rows = pl.ds(pl.multiple_of(8 * i, 8), 48)
            target_ref[slot, rows, :] = k * k * (PEAK * jnp.exp(-u) - full)
            pot_ref[pl.ds(pl.multiple_of(8 * (base + i), 8), 48), :] += strong * (full - k)

    copies = []
    rounds = [(a, (0, 1)) for a in range(0, LAST[0], 2)] + [(LAST[0], (1,)), (LAST[0], (0,))]
    for a, sides in rounds:
        for half in sides:
            pair = (16 * half + a, 16 * half + a + 1)
            lanes = [(q, wide(uc_ref, q), wide(ec_ref, q), power(q)) for q in pair]
            for i in range(HALF // 8):
                r = slice(half * HALF + 8 * i, half * HALF + 8 * i + 8)
                total = None
                for q, ucq, ecq, strong in lanes:
                    k = lax.rsqrt(uab_ref[r, q : q + 1] + ucq)
                    e = eab_ref[r, q : q + 1] * ecq
                    target_ref, slot = place(last_ref, slope_ref, q)
                    target_ref[slot, 8 * i : 8 * i + 8, :] = k * k * (e - k)
                    total = strong * k if total is None else total + strong * k
                pot_ref[r, :] = total if a == 0 else pot_ref[r, :] + total
        found = [jnp.right_shift(value, a) & 3 for value in bits]
        found = found[0] + 4 * found[1] if len(sides) == 2 else found[sides[0]]

        @pl.when(found > 0)
        def _(a=a, sides=sides, found=found):
            def visit(j, _):
                @pl.when((jnp.right_shift(found, j) & 1) > 0)
                def _():
                    half = (j >> 1) + sides[0]
                    q = 16 * half + a + (j & 1)
                    if sides == (0,) and a == LAST[0]:
                        fix_charge(q, last_ref, q - LAST[0])
                    else:
                        fix_charge(q, slope_ref, q - 2 * half)

                return 0

            lax.fori_loop(0, 2 * len(sides), visit, 0)

        for half in sides:
            for q in (16 * half + a, 16 * half + a + 1):
                if q not in LAST:
                    slot = q - 2 * half
                    copy = pltpu.make_async_copy(
                        slope_ref.at[slot], slope_out.at[slot], sems.at[slot]
                    )
                    copy.start()
                    copies.append(copy)
    for copy in copies:
        copy.wait()


def grid_kernel(
    plan_s,
    recv_ref,
    owner_ref,
    gb_ref,
    gc_ref,
    table_ref,
    pot_ref,
    last_ref,
    slope_in,
    offb_ref,
    offc_ref,
    col_ref,
    field_out,
    push_ref,
    acc_ref,
    tab_ref,
    flow_ref,
    edge_ref,
    pass_ref,
    mid_ref,
    dens_ref,
    sum_ref,
    field_ref,
    slope_ref,
    merged_ref,
    sems,
):
    slope_copy = pltpu.make_async_copy(slope_in, slope_ref, sems.at[1])
    slope_copy.start()
    pairs = merged_ref.shape[0]
    merged_ref[...] = jnp.where(owner_ref[...] > 0.0, recv_ref[:pairs], recv_ref[pairs:])
    def counter(rows):
        return lax.broadcasted_iota(i32, (rows, LANE), 0).astype(f32).astype(bf16)

    iota_b, iota_c = counter(WINDOW), counter(LANE)
    zero = jnp.zeros((WINDOW, LANE), bf16)
    one_c, zero_c = jnp.ones((LANE, LANE), bf16), jnp.zeros((LANE, LANE), bf16)

    def product(tile, group_b, group_c):
        columns, weights = [], []
        for j in range(TILE_CHUNKS):
            pair = tile * (TILE_CHUNKS // 4) + j // 4
            piece = j % 4
            gb = gb_ref[piece, pl.ds(pair, 1), :]
            gc = gc_ref[piece, pl.ds(pair, 1), :]
            parts = [None] * 4
            for part in range(2):
                value = merged_ref[pair, 4 * part + piece : 4 * part + piece + 1, :]
                parts[part], parts[2 + part] = halves(value)
            hots = []
            for h in range(2):
                band = (LANE * plan_s[8 + 2 * group_c + h]).astype(f32)
                hots.append(jnp.where(iota_c == (gc - band).astype(bf16), one_c, zero_c))
            weights.append(jnp.concatenate(hots, axis=0))
            hit = iota_b == (gb - WINDOW * jnp.asarray(group_b).astype(f32)).astype(bf16)
            columns.append(jnp.concatenate([jnp.where(hit, v, zero) for v in parts], axis=0))
        return mm(jnp.concatenate(columns, axis=1), jnp.concatenate(weights, axis=1), NT)

    acc_ref[0] = jnp.zeros(acc_ref.shape[1:], f32)
    def step(t, _):
        acc_ref[0] += product(t, 0, 0)
        return 0

    steps = 4 * pairs // TILE_CHUNKS
    lax.fori_loop(0, steps, step, 0)

    def rest(combo, _):
        group_b, group_c = combo >> 1, combo & 1

        @pl.when((group_b < plan_s[1]) & (group_c < plan_s[2]))
        def _():
            acc_ref[combo] = jnp.zeros(acc_ref.shape[1:], f32)

            def extra(t, _):
                acc_ref[combo] += product(t, group_b, group_c)
                return 0

            lax.fori_loop(0, steps, extra, 0)

        return 0

    lax.fori_loop(1, 4, rest, 0)

    def transform(group_b):
        def along(group_c, first):
            for level in range(2):
                for h in range(2):
                    band = jnp.minimum(plan_s[8 + 2 * group_c + h], 2) * LANE
                    base = 2 * level * N
                    cos = table_ref[pl.ds(pl.multiple_of(base + band, LANE), LANE), :]
                    sin = table_ref[pl.ds(pl.multiple_of(base + N + band, LANE), LANE), :]
                    top = slice(h * LANE, (h + 1) * LANE)
                    bottom = slice((2 + h) * LANE, (3 + h) * LANE)
                    tab_ref[level, top, :N] = cos
                    tab_ref[level, top, N:] = sin
                    tab_ref[level, bottom, :N] = -sin
                    tab_ref[level, bottom, N:] = cos
            combo = 2 * group_b + group_c
            for k in range(4):
                top = (k // 2) * WINDOW
                flow_ref[top : top + WINDOW, (k % 2) * 2 * LANE : (k % 2 + 1) * 2 * LANE] = acc_ref[
                    combo, k * WINDOW : (k + 1) * WINDOW, :
                ].astype(bf16)
            half = WINDOW
            both = mm(flow_ref[...], tab_ref[0])
            result = both[:half] + both[half:] + mm(flow_ref[:half], tab_ref[1])
            pass_ref[...] = result if first else pass_ref[...] + result

        along(0, True)

        @pl.when(plan_s[2] > 1)
        def _():
            along(1, False)

        for j in range(WINDOW // 16):
            block = plan_s[3] + (group_b * WINDOW) // 16 + j
            block = jnp.where(block >= BLOCKS, block - BLOCKS, block)
            for k in range(4):
                row = pl.multiple_of(k * N + 16 * block, 16)
                edge_ref[16 * j : 16 * j + 16, k * N : (k + 1) * N] = table_ref[pl.ds(row, 16), :]
        high, low = halves(pass_ref[...])
        result = mm(edge_ref[:, : 2 * N], high, TN) + (
            mm(edge_ref[:, 2 * N :], high, TN) + mm(edge_ref[:, : 2 * N], low, TN)
        )
        mid_ref[...] = result if group_b == 0 else mid_ref[...] + result

    transform(0)

    @pl.when(plan_s[1] > 1)
    def _():
        transform(1)

    def finish(i, _):
        r = pl.ds(pl.multiple_of(8 * i, 8), 8)
        s = pl.ds(pl.multiple_of(N + 8 * i, 8), 8)
        real = mid_ref[r, :N] - mid_ref[s, N:]
        imag = mid_ref[s, :N] + mid_ref[r, N:]
        dens_ref[r, :] = real * real + imag * imag
        pot = pot_ref[r, :]
        field_ref[0, r, :] = pot * real
        field_ref[1, r, :] = pot * imag
        return 0

    lax.fori_loop(0, N // 8, finish, 0, unroll=8)
    field_copy = pltpu.make_async_copy(field_ref, field_out, sems.at[0])
    field_copy.start()
    slope_copy.wait()
    for q in range(32):
        base = (q // 16) * HALF
        plain = [jnp.zeros((8, LANE), f32)] * 3
        scaled = jnp.zeros((8, LANE), f32)
        for i in range(HALF // 8):
            r = slice(base + 8 * i, base + 8 * i + 8)
            source_ref, slot = place(last_ref, slope_ref, q)
            w = dens_ref[r, :] * source_ref[slot, 8 * i : 8 * i + 8, :]
            w = [w[:, k * LANE : (k + 1) * LANE] for k in range(3)]
            plain = [p + v for p, v in zip(plain, w)]
            scaled = scaled + (w[0] + w[1] + w[2]) * offb_ref[r, q : q + 1]
        for k in range(3):
            sum_ref[q : q + 1, k * LANE : (k + 1) * LANE] = jnp.sum(plain[k], axis=0, keepdims=True)
        sum_ref[32 + q : 33 + q, :LANE] = jnp.sum(scaled, axis=0, keepdims=True)
    plain = sum_ref[:32, :]
    off_a = col_ref[:32, 0:1]
    scale = col_ref[:32, 1:2] * VOLUME
    push_a = off_a * jnp.sum(plain, axis=1, keepdims=True) * scale
    push_b = jnp.sum(sum_ref[32:, :LANE], axis=1, keepdims=True) * scale
    push_c = jnp.sum(plain * offc_ref[...], axis=1, keepdims=True) * scale
    packed = jnp.concatenate([push_a, push_b, push_c, 0.5 * col_ref[:32, 2:3]], axis=0)
    push_ref[...] = jnp.transpose(jnp.broadcast_to(packed, (LANE, LANE)))[:1]
    field_copy.wait()


def spread_kernel(terms_ref, out_ref):
    terms = terms_ref[...]
    sources = terms.shape[0]
    width = out_ref.shape[1] // 2
    turned = jnp.transpose(jnp.concatenate([terms, pltpu.roll(terms, LANE - 1, 1)], axis=0))
    rows = []
    for axis in range(3):
        picked = [32 * axis + 2 * k for k in range(16)]
        rows.append(jnp.concatenate([turned[r : r + 1, :] for r in picked], axis=1))
    value = jnp.concatenate(rows, axis=0)
    first = value.astype(bf16).astype(f32)
    second = (value - first).astype(bf16).astype(f32)
    third = value - first - second
    zeros = jnp.zeros((7, value.shape[1]), f32)
    parts = jnp.concatenate([first, second, third, zeros], axis=0).astype(bf16)
    iota = lax.broadcasted_iota(i32, (sources, width), 1).astype(f32).astype(bf16)
    one, zero = jnp.ones((sources, width), bf16), jnp.zeros((sources, width), bf16)
    hots = []
    for q in range(32):
        number = terms[:, 96 + q : 97 + q]
        hot = []
        for half in range(2):
            wide = jnp.broadcast_to(number - half * width, (sources, width)).astype(bf16)
            hot.append(jnp.where(iota == wide, one, zero))
        hots.append(jnp.concatenate(hot, axis=1))
    result = mm(parts, jnp.concatenate(hots, axis=0))
    out_ref[...] = result[0:3] + result[3:6] + result[6:9]


def vmem(count):
    return [pl.BlockSpec(memory_space=pltpu.VMEM)] * count


def smem(count):
    return [pl.BlockSpec(memory_space=pltpu.SMEM)] * count


def anywhere(count):
    return [pl.BlockSpec(memory_space=pltpu.HBM)] * count


def params(mebibytes):
    return pltpu.CompilerParams(vmem_limit_bytes=mebibytes * 1024 * 1024)


def local(coefficients, col_map, charge_cell, charge_frac, charge, tile_list):
    slots = coefficients.shape[2]
    sources = lax.axis_size("pw")
    planes = sources
    first_table, second_table = tables(planes)

    sent = pl.pallas_call(
        columns_kernel,
        out_shape=jax.ShapeDtypeStruct((planes, 8, LANE), f32),
        in_specs=anywhere(2),
        out_specs=vmem(1)[0],
        scratch_shapes=[
            pltpu.VMEM((2, slots, N), f32),
            pltpu.VMEM(first_table.shape, bf16),
            pltpu.VMEM((4 * LANE, 2 * N), bf16),
            pltpu.VMEM((4 * LANE, 2 * N), bf16),
            pltpu.SemaphoreType.DMA((5,)),
        ],
        compiler_params=params(54),
        name="columns",
    )(coefficients.reshape(2, slots, N), jnp.asarray(first_table))
    own = tile_list[0]
    other = lax.ppermute(own, "mm", [(0, 1), (1, 0)])
    first = lax.axis_index("mm") == 0
    listed = jnp.concatenate([jnp.where(first, own, other), jnp.where(first, other, own)])

    recv = lax.all_to_all(sent, "pw", 0, 0, tiled=True)

    blocks = col_map.reshape(sources, slots)
    grid = jnp.pad(blocks, ((0, 0), (0, 4 * LANE - slots)), constant_values=EMPTY)

    pot, last, slope, offb, offc, col, gb, gc, owner, plan = pl.pallas_call(
        charges_kernel,
        out_shape=(
            jax.ShapeDtypeStruct((N, N), f32),
            jax.ShapeDtypeStruct((2, HALF, N), f32),
            pltpu.HBM((STORED, HALF, N), f32),
            jax.ShapeDtypeStruct((N, LANE), f32),
            jax.ShapeDtypeStruct((32, N), f32),
            jax.ShapeDtypeStruct((32, 8), f32),
            jax.ShapeDtypeStruct((4, sources // 2, LANE), f32),
            jax.ShapeDtypeStruct((4, sources // 2, LANE), f32),
            jax.ShapeDtypeStruct((sources // 2, 8, LANE), f32),
            jax.ShapeDtypeStruct((16,), i32),
        ),
        in_specs=vmem(5),
        out_specs=tuple(vmem(2) + anywhere(1) + vmem(6) + smem(1)),
        scratch_shapes=[
            pltpu.VMEM((N, LANE), f32),
            pltpu.VMEM((N, LANE), f32),
            pltpu.VMEM((32, N), f32),
            pltpu.VMEM((32, N), f32),
            pltpu.VMEM((STORED, HALF, N), f32),
            pltpu.SemaphoreType.DMA((STORED,)),
        ],
        compiler_params=params(50),
        name="charges",
    )(
        listed[:, None],
        charge_cell,
        charge_frac,
        charge[None],
        grid,
    )

    field, push = pl.pallas_call(
        grid_kernel,
        out_shape=(
            jax.ShapeDtypeStruct((2, N, N), f32),
            jax.ShapeDtypeStruct((1, LANE), f32),
        ),
        in_specs=smem(1) + vmem(7) + anywhere(1) + vmem(3),
        out_specs=tuple(anywhere(1) + vmem(1)),
        scratch_shapes=[
            pltpu.VMEM((4, 4 * WINDOW, 2 * LANE), f32),
            pltpu.VMEM((2, 4 * LANE, 2 * N), bf16),
            pltpu.VMEM((2 * WINDOW, 4 * LANE), bf16),
            pltpu.VMEM((WINDOW, 4 * N), bf16),
            pltpu.VMEM((WINDOW, 2 * N), f32),
            pltpu.VMEM((2 * N, 2 * N), f32),
            pltpu.VMEM((N, N), f32),
            pltpu.VMEM((64, N), f32),
            pltpu.VMEM((2, N, N), f32),
            pltpu.VMEM((STORED, HALF, N), f32),
            pltpu.VMEM((sources // 2, 8, LANE), f32),
            pltpu.SemaphoreType.DMA((2,)),
        ],
        compiler_params=params(50),
        name="grid",
    )(plan, recv, owner, gb, gc, jnp.asarray(second_table), pot, last, slope, offb, offc, col)

    push = push + lax.ppermute(push, "mm", [(0, 1), (1, 0)])
    terms = lax.all_to_all(
        jnp.broadcast_to(push[None], (sources, 1, LANE)), "pw", 0, 0, tiled=True
    ).reshape(sources, LANE)
    forces = pl.pallas_call(
        spread_kernel,
        out_shape=jax.ShapeDtypeStruct((3, charge.shape[0]), f32),
        in_specs=vmem(1),
        out_specs=vmem(1)[0],
        compiler_params=params(12),
        name="spread",
    )(terms)
    return (field[:, None, None], forces)


def solution(mesh):
    placed = (P(None, "mm", "pw", None), P(), P(), P(), P(), P(("pw", "mm"), None))
    return jax.shard_map(
        local,
        mesh=mesh,
        in_specs=placed,
        out_specs=(P(None, "mm", "pw", None, None), P()),
        check_vma=False,
    )
```

```python
import functools
import math

import jax
import jax.numpy as jnp
import ml_dtypes
import numpy as np
from jax import lax
from jax.experimental import pallas as pl
from jax.experimental.pallas import tpu as pltpu
from jax.sharding import PartitionSpec as P

f32, bf16, i32 = jnp.float32, jnp.bfloat16, jnp.int32
N = 384
HALF = 192
LANE = 128
SPACING = 0.25
SOFTEN = 0.09
VOLUME = SPACING**3
PEAK = 2.0 / math.sqrt(math.pi)
EMPTY = N * N
TILE_CHUNKS = 64
WINDOW = 208
BLOCKS = N // 16
LAST = (14, 15)
STORED = 30
NT = (((1,), (1,)), ((), ()))
TN = (((0,), (0,)), ((), ()))


def split_table(table):
    high = table.astype(np.float32).astype(ml_dtypes.bfloat16)
    low = (table - high.astype(np.float64)).astype(np.float32).astype(ml_dtypes.bfloat16)
    return high, low


def tables(planes):
    index = np.arange(N, dtype=np.int64)
    angle = 2.0 * np.pi / N * ((index[:, None] * index[None, :]) % N).astype(np.float64)
    cos, sin = np.cos(angle), np.sin(angle)
    cz, sz = cos[:planes], sin[:planes]
    first = np.block([[cz, -sz], [sz, cz]])
    first_high, first_low = split_table(first)
    cos_high, cos_low = split_table(cos)
    sin_high, sin_low = split_table(sin)
    return (
        np.concatenate([first_high, first_low], axis=0),
        np.concatenate([cos_high, sin_high, cos_low, sin_low], axis=0),
    )


def mm(a, b, dims=(((1,), (0,)), ((), ()))):
    return lax.dot_general(a, b, dims, preferred_element_type=f32)


def halves(value):
    high = value.astype(bf16)
    low = (value - high.astype(f32)).astype(bf16)
    return high, low


def flip_table(length):
    row = lax.broadcasted_iota(i32, (length, length), 0)
    column = lax.broadcasted_iota(i32, (length, length), 1)
    return jnp.where(row + column == length - 1, 1.0, 0.0).astype(bf16)


def columns_kernel(
    coef_in, table_in, out_ref, coef_ref, table_ref, high_ref, low_ref, sems
):
    slots = coef_ref.shape[1]
    half = slots // 2
    copies = []
    for part in range(2):
        for piece in range(2):
            cut = pl.ds(piece * half, half)
            copies.append(
                pltpu.make_async_copy(
                    coef_in.at[part, cut], coef_ref.at[part, cut], sems.at[2 * part + piece]
                )
            )
    copies.append(pltpu.make_async_copy(table_in, table_ref, sems.at[4]))
    for copy in copies:
        copy.start()
    width = high_ref.shape[0]
    planes = out_ref.shape[0]
    high_ref[slots:, :] = jnp.zeros((width - slots, 2 * N), bf16)
    low_ref[slots:, :] = jnp.zeros((width - slots, 2 * N), bf16)
    for part in range(2):
        for piece in range(2):
            copies[2 * part + piece].wait()
            rows = slice(piece * half, (piece + 1) * half)
            high, low = halves(coef_ref[part, rows])
            high_ref[rows, part * N : (part + 1) * N] = high
            low_ref[rows, part * N : (part + 1) * N] = low
    copies[4].wait()
    rows = 2 * planes
    both = mm(table_ref[...], high_ref[...], NT)
    result = both[:rows] + both[rows:] + mm(table_ref[:rows], low_ref[...], NT)

    def put(values):
        for part in range(2):
            for piece in range(4):
                out_ref[:, 4 * part + piece, :] = values[
                    part * planes : (part + 1) * planes, piece * LANE : (piece + 1) * LANE
                ]

    reverse = lax.axis_index("pw") < planes // 2

    @pl.when(jnp.logical_not(reverse))
    def _():
        put(result)

    @pl.when(reverse)
    def _():
        high, low = halves(result)
        flip = flip_table(width)
        put(mm(high, flip) + mm(low, flip))


def wrap(offset):
    shifted = offset + HALF
    shifted = jnp.where(shifted < 0, shifted + N, shifted)
    shifted = jnp.where(shifted >= N, shifted - N, shifted)
    return SPACING * (shifted - HALF)


ERF_NUM = (
    -2.72614225801306e-10,
    2.77068142495902e-08,
    -2.10102402082508e-06,
    -5.69250639462346e-05,
    -7.34990630326855e-04,
    -2.95459980854025e-03,
    -1.60960333262415e-02,
)
ERF_DEN = (
    -1.45660718464996e-05,
    -2.13374055278905e-04,
    -1.68282697438203e-03,
    -7.37332916720468e-03,
    -1.42647390514189e-02,
)


def erf(s):
    s = jnp.minimum(s, 4.0)
    sq = s * s
    num = jnp.full_like(s, ERF_NUM[0])
    for c in ERF_NUM[1:]:
        num = num * sq + c
    den = jnp.full_like(s, ERF_DEN[0])
    for c in ERF_DEN[1:]:
        den = den * sq + c
    return s * num / den


def sort_cells(grid_ref, gb_ref, gc_ref, owner_ref, plan_s):
    cells = grid_ref[...]
    pairs = cells.shape[0] // 2
    row = jnp.floor((cells.astype(f32) + 0.5) * (1.0 / N))
    gb = jnp.where(cells < EMPTY, row, -1000.0)
    gc = jnp.where(cells < EMPTY, cells.astype(f32) - N * row, -1000.0)
    high, low = halves(jnp.concatenate([gb[:pairs], gc[:pairs]], axis=0))
    flip = flip_table(cells.shape[1])
    turned = mm(high, flip) + mm(low, flip)
    owned = jnp.where(turned[:pairs] >= 0.0, 1.0, 0.0)
    for piece in range(4):
        cut = slice(piece * LANE, (piece + 1) * LANE)
        owner_ref[:, piece, :] = owned[:, cut]
        owner_ref[:, 4 + piece, :] = owned[:, cut]
    merged_b = jnp.maximum(gb[pairs:], turned[:pairs])
    merged_c = jnp.maximum(gc[pairs:], turned[pairs:])
    found = jnp.int32(0)
    for band in range(3):
        inside = (merged_c >= band * LANE) & (merged_c < (band + 1) * LANE)
        plan_s[8 + found] = jnp.int32(band)
        found = found + jnp.max(jnp.where(inside, 1.0, 0.0)).astype(i32)
    for slot in range(4):
        plan_s[8 + slot] = jnp.where(slot < found, plan_s[8 + slot], 3)
    plan_s[2] = (found + 1) // 2
    alive = merged_b >= 0.0
    block = jnp.where(alive, merged_b * (1.0 / 16.0), 0.0).astype(i32)
    used = jnp.left_shift(jnp.where(alive, 1, 0), block)
    while used.shape[0] > 8:
        used = used[: used.shape[0] // 2] | used[used.shape[0] // 2 :]
    while used.shape[1] > LANE:
        used = used[:, : used.shape[1] // 2] | used[:, used.shape[1] // 2 :]
    for axis, width in ((0, 8), (1, LANE)):
        shift = width // 2
        while shift:
            used = used | pltpu.roll(used, shift, axis)
            shift //= 2
    occupied = jnp.max(used.astype(f32)).astype(i32)
    start = jnp.int32(-1)
    for k in range(BLOCKS):
        outside = sum(1 << ((k + j) % BLOCKS) for j in range(WINDOW // 16, BLOCKS))
        start = jnp.where((occupied & outside) == 0, k, start)
    plan_s[1] = jnp.where(start < 0, 2, 1)
    start = jnp.maximum(start, 0)
    plan_s[3] = start
    shifted = merged_b - (16 * start).astype(f32)
    shifted = jnp.where(shifted < 0.0, shifted + N, shifted)
    shifted = jnp.where(alive, shifted, -1000.0)
    for values, out in ((shifted, gb_ref), (merged_c, gc_ref)):
        for piece in range(4):
            out[piece] = values[:, piece * LANE : (piece + 1) * LANE]


def place(last_ref, slope_ref, q):
    return (last_ref, q - LAST[0]) if q in LAST else (slope_ref, q - 2 * (q // 16))


def charges_kernel(
    list_ref,
    cell_ref,
    frac_ref,
    charge_ref,
    grid_ref,
    pot_ref,
    last_ref,
    slope_out,
    offb_ref,
    offc_ref,
    col_ref,
    gb_ref,
    gc_ref,
    owner_ref,
    plan_s,
    uab_ref,
    eab_ref,
    uc_ref,
    ec_ref,
    slope_ref,
    sems,
):
    listed = list_ref[...]
    mask = lax.broadcasted_iota(i32, (32, cell_ref.shape[1]), 1) == listed
    center = cell_ref[...].astype(f32) + frac_ref[...]

    def pick(row):
        return jnp.sum(jnp.where(mask, row, 0.0), axis=1, keepdims=True)

    ca, cb, cc = (pick(center[i : i + 1]) for i in range(3))
    strength = pick(charge_ref[...])
    plane = lax.axis_index("pw").astype(f32)
    off_a = wrap(plane - ca)
    col_ref[...] = jnp.concatenate(
        [off_a, strength, listed.astype(f32)] + [jnp.zeros((32, 5), f32)], axis=1
    )
    off_c = wrap(lax.broadcasted_iota(i32, (32, N), 1).astype(f32) - cc)
    offc_ref[...] = off_c
    sq_c = off_c * off_c
    uc_ref[...] = sq_c
    ec_ref[...] = jnp.exp(-sq_c)

    def across(column):
        tall = jnp.concatenate([column, jnp.zeros((LANE - 32, 1), f32)], axis=0)
        return jnp.transpose(jnp.broadcast_to(tall, (LANE, LANE)))[:1]

    row_b, row_c, row_s = across(cb), across(cc), across(strength)
    off_b = wrap(lax.broadcasted_iota(i32, (N, LANE), 0).astype(f32) - row_b)
    offb_ref[...] = off_b
    row_a = across(off_a)
    uab = off_b * off_b + (row_a * row_a + SOFTEN)
    uab_ref[...] = uab
    eab_ref[...] = PEAK * jnp.exp(-uab)

    def wide(ref, q):
        return jnp.broadcast_to(ref[q : q + 1, :], (8, N))

    def power(q):
        return jnp.broadcast_to(strength[q : q + 1, :], (8, N))

    close = (row_a * row_a < 16.0).astype(f32)
    lane = lax.broadcasted_iota(i32, (1, LANE), 1)
    bits = []
    for half in range(2):
        weight = jnp.where((lane >= 16 * half) & (lane < 16 * half + 16), 1, 0)
        weight = jnp.left_shift(weight, lane & 15).astype(f32)
        bits.append(jnp.sum(close * weight).astype(i32))

    def fix_charge(q, target_ref, slot):
        base = (q >> 4) * (HALF // 8)

        def one(row):
            return jnp.sum(jnp.where(lane == q, row, 0.0), axis=1, keepdims=True)

        da, cb_one, cc_one, strong = one(row_a), one(row_b), one(row_c), one(row_s)
        dc = wrap(lax.broadcasted_iota(i32, (8, N), 1).astype(f32) - cc_one)
        rest = dc * dc + (da * da + SOFTEN)
        local = jnp.floor((jnp.sum(cb_one) - 16.0) * 0.125).astype(i32) - base
        local = jnp.where(local < -5, local + N // 8, local)
        local = jnp.where(local >= N // 8 - 5, local - N // 8, local)

        @pl.when(local < HALF // 8)
        def _():
            i = jnp.clip(local, 0, HALF // 8 - 6)
            row = lax.broadcasted_iota(i32, (48, N), 0).astype(f32)
            db = wrap(row + ((8 * (base + i)).astype(f32) - cb_one))
            u = db * db + rest[:1]
            k = lax.rsqrt(u)
            full = erf(u * k) * k
            rows = pl.ds(pl.multiple_of(8 * i, 8), 48)
            target_ref[slot, rows, :] = k * k * (PEAK * jnp.exp(-u) - full)
            pot_ref[pl.ds(pl.multiple_of(8 * (base + i), 8), 48), :] += strong * (full - k)

    copies = []
    rounds = [(a, (0, 1)) for a in range(0, LAST[0], 2)] + [(LAST[0], (1,)), (LAST[0], (0,))]
    for a, sides in rounds:
        for half in sides:
            pair = (16 * half + a, 16 * half + a + 1)
            lanes = [(q, wide(uc_ref, q), wide(ec_ref, q), power(q)) for q in pair]
            for i in range(HALF // 8):
                r = slice(half * HALF + 8 * i, half * HALF + 8 * i + 8)
                total = None
                for q, ucq, ecq, strong in lanes:
                    k = lax.rsqrt(uab_ref[r, q : q + 1] + ucq)
                    e = eab_ref[r, q : q + 1] * ecq
                    target_ref, slot = place(last_ref, slope_ref, q)
                    target_ref[slot, 8 * i : 8 * i + 8, :] = k * k * (e - k)
                    total = strong * k if total is None else total + strong * k
                pot_ref[r, :] = total if a == 0 else pot_ref[r, :] + total
        found = [jnp.right_shift(value, a) & 3 for value in bits]
        found = found[0] + 4 * found[1] if len(sides) == 2 else found[sides[0]]

        @pl.when(found > 0)
        def _(a=a, sides=sides, found=found):
            def visit(j, _):
                @pl.when((jnp.right_shift(found, j) & 1) > 0)
                def _():
                    half = (j >> 1) + sides[0]
                    q = 16 * half + a + (j & 1)
                    if sides == (0,) and a == LAST[0]:
                        fix_charge(q, last_ref, q - LAST[0])
                    else:
                        fix_charge(q, slope_ref, q - 2 * half)

                return 0

            lax.fori_loop(0, 2 * len(sides), visit, 0)

        for half in sides:
            for q in (16 * half + a, 16 * half + a + 1):
                if q not in LAST:
                    slot = q - 2 * half
                    copy = pltpu.make_async_copy(
                        slope_ref.at[slot], slope_out.at[slot], sems.at[slot]
                    )
                    copy.start()
                    copies.append(copy)
        if a == 0:
            sort_cells(grid_ref, gb_ref, gc_ref, owner_ref, plan_s)
    for copy in copies:
        copy.wait()


def grid_kernel(
    plan_s,
    recv_ref,
    owner_ref,
    gb_ref,
    gc_ref,
    table_ref,
    pot_ref,
    last_ref,
    slope_in,
    offb_ref,
    offc_ref,
    col_ref,
    field_out,
    push_ref,
    acc_ref,
    tab_ref,
    flow_ref,
    edge_ref,
    pass_ref,
    mid_ref,
    dens_ref,
    sum_ref,
    field_ref,
    slope_ref,
    merged_ref,
    sems,
):
    slope_copy = pltpu.make_async_copy(slope_in, slope_ref, sems.at[1])
    slope_copy.start()
    pairs = merged_ref.shape[0]
    merged_ref[...] = jnp.where(owner_ref[...] > 0.0, recv_ref[:pairs], recv_ref[pairs:])
    def counter(rows):
        return lax.broadcasted_iota(i32, (rows, LANE), 0).astype(f32).astype(bf16)

    iota_b, iota_c = counter(WINDOW), counter(LANE)
    zero = jnp.zeros((WINDOW, LANE), bf16)
    one_c, zero_c = jnp.ones((LANE, LANE), bf16), jnp.zeros((LANE, LANE), bf16)

    def product(tile, group_b, group_c):
        columns, weights = [], []
        for j in range(TILE_CHUNKS):
            pair = tile * (TILE_CHUNKS // 4) + j // 4
            piece = j % 4
            gb = gb_ref[piece, pl.ds(pair, 1), :]
            gc = gc_ref[piece, pl.ds(pair, 1), :]
            parts = [None] * 4
            for part in range(2):
                value = merged_ref[pair, 4 * part + piece : 4 * part + piece + 1, :]
                parts[part], parts[2 + part] = halves(value)
            hots = []
            for h in range(2):
                band = (LANE * plan_s[8 + 2 * group_c + h]).astype(f32)
                hots.append(jnp.where(iota_c == (gc - band).astype(bf16), one_c, zero_c))
            weights.append(jnp.concatenate(hots, axis=0))
            hit = iota_b == (gb - WINDOW * jnp.asarray(group_b).astype(f32)).astype(bf16)
            columns.append(jnp.concatenate([jnp.where(hit, v, zero) for v in parts], axis=0))
        return mm(jnp.concatenate(columns, axis=1), jnp.concatenate(weights, axis=1), NT)

    acc_ref[0] = jnp.zeros(acc_ref.shape[1:], f32)
    def step(t, _):
        acc_ref[0] += product(t, 0, 0)
        return 0

    steps = 4 * pairs // TILE_CHUNKS
    lax.fori_loop(0, steps, step, 0)

    def rest(combo, _):
        group_b, group_c = combo >> 1, combo & 1

        @pl.when((group_b < plan_s[1]) & (group_c < plan_s[2]))
        def _():
            acc_ref[combo] = jnp.zeros(acc_ref.shape[1:], f32)

            def extra(t, _):
                acc_ref[combo] += product(t, group_b, group_c)
                return 0

            lax.fori_loop(0, steps, extra, 0)

        return 0

    lax.fori_loop(1, 4, rest, 0)

    def transform(group_b):
        def along(group_c, first):
            for level in range(2):
                for h in range(2):
                    band = jnp.minimum(plan_s[8 + 2 * group_c + h], 2) * LANE
                    base = 2 * level * N
                    cos = table_ref[pl.ds(pl.multiple_of(base + band, LANE), LANE), :]
                    sin = table_ref[pl.ds(pl.multiple_of(base + N + band, LANE), LANE), :]
                    top = slice(h * LANE, (h + 1) * LANE)
                    bottom = slice((2 + h) * LANE, (3 + h) * LANE)
                    tab_ref[level, top, :N] = cos
                    tab_ref[level, top, N:] = sin
                    tab_ref[level, bottom, :N] = -sin
                    tab_ref[level, bottom, N:] = cos
            combo = 2 * group_b + group_c
            for k in range(4):
                top = (k // 2) * WINDOW
                flow_ref[top : top + WINDOW, (k % 2) * 2 * LANE : (k % 2 + 1) * 2 * LANE] = acc_ref[
                    combo, k * WINDOW : (k + 1) * WINDOW, :
                ].astype(bf16)
            half = WINDOW
            both = mm(flow_ref[...], tab_ref[0])
            result = both[:half] + both[half:] + mm(flow_ref[:half], tab_ref[1])
            pass_ref[...] = result if first else pass_ref[...] + result

        along(0, True)

        @pl.when(plan_s[2] > 1)
        def _():
            along(1, False)

        for j in range(WINDOW // 16):
            block = plan_s[3] + (group_b * WINDOW) // 16 + j
            block = jnp.where(block >= BLOCKS, block - BLOCKS, block)
            for k in range(4):
                row = pl.multiple_of(k * N + 16 * block, 16)
                edge_ref[16 * j : 16 * j + 16, k * N : (k + 1) * N] = table_ref[pl.ds(row, 16), :]
        high, low = halves(pass_ref[...])
        result = mm(edge_ref[:, : 2 * N], high, TN) + (
            mm(edge_ref[:, 2 * N :], high, TN) + mm(edge_ref[:, : 2 * N], low, TN)
        )
        mid_ref[...] = result if group_b == 0 else mid_ref[...] + result

    transform(0)

    @pl.when(plan_s[1] > 1)
    def _():
        transform(1)

    def finish(i, _):
        r = pl.ds(pl.multiple_of(8 * i, 8), 8)
        s = pl.ds(pl.multiple_of(N + 8 * i, 8), 8)
        real = mid_ref[r, :N] - mid_ref[s, N:]
        imag = mid_ref[s, :N] + mid_ref[r, N:]
        dens_ref[r, :] = real * real + imag * imag
        pot = pot_ref[r, :]
        field_ref[0, r, :] = pot * real
        field_ref[1, r, :] = pot * imag
        return 0

    lax.fori_loop(0, N // 8, finish, 0, unroll=8)
    field_copy = pltpu.make_async_copy(field_ref, field_out, sems.at[0])
    field_copy.start()
    slope_copy.wait()
    for q in range(32):
        base = (q // 16) * HALF
        plain = [jnp.zeros((8, LANE), f32)] * 3
        scaled = jnp.zeros((8, LANE), f32)
        for i in range(HALF // 8):
            r = slice(base + 8 * i, base + 8 * i + 8)
            source_ref, slot = place(last_ref, slope_ref, q)
            w = dens_ref[r, :] * source_ref[slot, 8 * i : 8 * i + 8, :]
            w = [w[:, k * LANE : (k + 1) * LANE] for k in range(3)]
            plain = [p + v for p, v in zip(plain, w)]
            scaled = scaled + (w[0] + w[1] + w[2]) * offb_ref[r, q : q + 1]
        for k in range(3):
            sum_ref[q : q + 1, k * LANE : (k + 1) * LANE] = jnp.sum(plain[k], axis=0, keepdims=True)
        sum_ref[32 + q : 33 + q, :LANE] = jnp.sum(scaled, axis=0, keepdims=True)
    plain = sum_ref[:32, :]
    off_a = col_ref[:32, 0:1]
    scale = col_ref[:32, 1:2] * VOLUME
    push_a = off_a * jnp.sum(plain, axis=1, keepdims=True) * scale
    push_b = jnp.sum(sum_ref[32:, :LANE], axis=1, keepdims=True) * scale
    push_c = jnp.sum(plain * offc_ref[...], axis=1, keepdims=True) * scale
    packed = jnp.concatenate([push_a, push_b, push_c, 0.5 * col_ref[:32, 2:3]], axis=0)
    push_ref[...] = jnp.transpose(jnp.broadcast_to(packed, (LANE, LANE)))[:1]
    field_copy.wait()


def spread_kernel(terms_ref, out_ref):
    terms = terms_ref[...]
    sources = terms.shape[0]
    width = out_ref.shape[1] // 2
    turned = jnp.transpose(jnp.concatenate([terms, pltpu.roll(terms, LANE - 1, 1)], axis=0))
    rows = []
    for axis in range(3):
        picked = [32 * axis + 2 * k for k in range(16)]
        rows.append(jnp.concatenate([turned[r : r + 1, :] for r in picked], axis=1))
    value = jnp.concatenate(rows, axis=0)
    first = value.astype(bf16).astype(f32)
    second = (value - first).astype(bf16).astype(f32)
    third = value - first - second
    zeros = jnp.zeros((7, value.shape[1]), f32)
    parts = jnp.concatenate([first, second, third, zeros], axis=0).astype(bf16)
    iota = lax.broadcasted_iota(i32, (sources, width), 1).astype(f32).astype(bf16)
    one, zero = jnp.ones((sources, width), bf16), jnp.zeros((sources, width), bf16)
    hots = []
    for q in range(32):
        number = terms[:, 96 + q : 97 + q]
        hot = []
        for half in range(2):
            wide = jnp.broadcast_to(number - half * width, (sources, width)).astype(bf16)
            hot.append(jnp.where(iota == wide, one, zero))
        hots.append(jnp.concatenate(hot, axis=1))
    result = mm(parts, jnp.concatenate(hots, axis=0))
    out_ref[...] = result[0:3] + result[3:6] + result[6:9]


def vmem(count):
    return [pl.BlockSpec(memory_space=pltpu.VMEM)] * count


def smem(count):
    return [pl.BlockSpec(memory_space=pltpu.SMEM)] * count


def anywhere(count):
    return [pl.BlockSpec(memory_space=pltpu.HBM)] * count


def params(mebibytes):
    return pltpu.CompilerParams(vmem_limit_bytes=mebibytes * 1024 * 1024)


def local(coefficients, col_map, charge_cell, charge_frac, charge, tile_list):
    slots = coefficients.shape[2]
    sources = lax.axis_size("pw")
    planes = sources
    first_table, second_table = tables(planes)

    sent = pl.pallas_call(
        columns_kernel,
        out_shape=jax.ShapeDtypeStruct((planes, 8, LANE), f32),
        in_specs=anywhere(2),
        out_specs=vmem(1)[0],
        scratch_shapes=[
            pltpu.VMEM((2, slots, N), f32),
            pltpu.VMEM(first_table.shape, bf16),
            pltpu.VMEM((4 * LANE, 2 * N), bf16),
            pltpu.VMEM((4 * LANE, 2 * N), bf16),
            pltpu.SemaphoreType.DMA((5,)),
        ],
        compiler_params=params(54),
        name="columns",
    )(coefficients.reshape(2, slots, N), jnp.asarray(first_table))
    own = tile_list[0]
    other = lax.ppermute(own, "mm", [(0, 1), (1, 0)])
    first = lax.axis_index("mm") == 0
    listed = jnp.concatenate([jnp.where(first, own, other), jnp.where(first, other, own)])

    recv = lax.all_to_all(sent, "pw", 0, 0, tiled=True)

    blocks = col_map.reshape(sources, slots)
    grid = jnp.pad(blocks, ((0, 0), (0, 4 * LANE - slots)), constant_values=EMPTY)

    pot, last, slope, offb, offc, col, gb, gc, owner, plan = pl.pallas_call(
        charges_kernel,
        out_shape=(
            jax.ShapeDtypeStruct((N, N), f32),
            jax.ShapeDtypeStruct((2, HALF, N), f32),
            pltpu.HBM((STORED, HALF, N), f32),
            jax.ShapeDtypeStruct((N, LANE), f32),
            jax.ShapeDtypeStruct((32, N), f32),
            jax.ShapeDtypeStruct((32, 8), f32),
            jax.ShapeDtypeStruct((4, sources // 2, LANE), f32),
            jax.ShapeDtypeStruct((4, sources // 2, LANE), f32),
            jax.ShapeDtypeStruct((sources // 2, 8, LANE), f32),
            jax.ShapeDtypeStruct((16,), i32),
        ),
        in_specs=vmem(5),
        out_specs=tuple(vmem(2) + anywhere(1) + vmem(6) + smem(1)),
        scratch_shapes=[
            pltpu.VMEM((N, LANE), f32),
            pltpu.VMEM((N, LANE), f32),
            pltpu.VMEM((32, N), f32),
            pltpu.VMEM((32, N), f32),
            pltpu.VMEM((STORED, HALF, N), f32),
            pltpu.SemaphoreType.DMA((STORED,)),
        ],
        compiler_params=params(50),
        name="charges",
    )(
        listed[:, None],
        charge_cell,
        charge_frac,
        charge[None],
        grid,
    )

    field, push = pl.pallas_call(
        grid_kernel,
        out_shape=(
            jax.ShapeDtypeStruct((2, N, N), f32),
            jax.ShapeDtypeStruct((1, LANE), f32),
        ),
        in_specs=smem(1) + vmem(7) + anywhere(1) + vmem(3),
        out_specs=tuple(anywhere(1) + vmem(1)),
        scratch_shapes=[
            pltpu.VMEM((4, 4 * WINDOW, 2 * LANE), f32),
            pltpu.VMEM((2, 4 * LANE, 2 * N), bf16),
            pltpu.VMEM((2 * WINDOW, 4 * LANE), bf16),
            pltpu.VMEM((WINDOW, 4 * N), bf16),
            pltpu.VMEM((WINDOW, 2 * N), f32),
            pltpu.VMEM((2 * N, 2 * N), f32),
            pltpu.VMEM((N, N), f32),
            pltpu.VMEM((64, N), f32),
            pltpu.VMEM((2, N, N), f32),
            pltpu.VMEM((STORED, HALF, N), f32),
            pltpu.VMEM((sources // 2, 8, LANE), f32),
            pltpu.SemaphoreType.DMA((2,)),
        ],
        compiler_params=params(50),
        name="grid",
    )(plan, recv, owner, gb, gc, jnp.asarray(second_table), pot, last, slope, offb, offc, col)

    push = push + lax.ppermute(push, "mm", [(0, 1), (1, 0)])
    terms = lax.all_to_all(
        jnp.broadcast_to(push[None], (sources, 1, LANE)), "pw", 0, 0, tiled=True
    ).reshape(sources, LANE)
    forces = pl.pallas_call(
        spread_kernel,
        out_shape=jax.ShapeDtypeStruct((3, charge.shape[0]), f32),
        in_specs=vmem(1),
        out_specs=vmem(1)[0],
        compiler_params=params(12),
        name="spread",
    )(terms)
    return (field[:, None, None], forces)


def solution(mesh):
    placed = (P(None, "mm", "pw", None), P(), P(), P(), P(), P(("pw", "mm"), None))
    return jax.shard_map(
        local,
        mesh=mesh,
        in_specs=placed,
        out_specs=(P(None, "mm", "pw", None, None), P()),
        check_vma=False,
    )
```
